32 devices in a mesh: groups: 2 (over y), dom: 4 (over z), sub: 4 (over x, core).
Axes of the slice: x: 2, y: 2, z: 4, core: 2. Of those that a mesh axis runs over, the one named last changes fastest.
Arguments:
- positions: float32 [3, 16, 16, 128], P(None, ('groups', 'dom'), 'sub'), parts along dimension 1, may hold values from -50 to 80, as said below
- charge: float32 [16, 16, 128], P(('groups', 'dom'), 'sub'), parts along dimension 0, may hold values from -2.5 to 2.5
- radius: float32 [16, 16, 128], P(('groups', 'dom'), 'sub'), parts along dimension 0, may hold values from 1.3 to 2.2
- segment: int32 [16, 16, 128], P(('groups', 'dom'), 'sub'), parts along dimension 0, may hold values from 0 to 15, never falling along the last dimension, each value on 1 to 16 neighbouring positions
- near_tiles: int32 [16, 16, 8], P(('groups', 'dom'), 'sub'), parts along dimension 0, may hold values from 0 to 1, as said below
Outputs:
- born_radii: float32 [16, 16, 128], P(('groups', 'dom'), 'sub'), parts along dimension 0
- radius_grad: float32 [16, 16, 128], P(('groups', 'dom'), 'sub'), parts along dimension 0
- forces: float32 [3, 16, 16, 128], P(None, ('groups', 'dom'), 'sub'), parts along dimension 1
The draws below stay inside these ranges and needn't reach their ends.
There are 2 independent parts, one for each index of `groups`. The reference program is written for one: setup_inputs(seed, part) draws one part's arguments, and reference() takes and returns one part's arrays. A program takes and returns all parts, laid end to end along the dimension named above; each array names one. Nothing has to cross between parts.
Inputs may be any that keep to these rules, and one draw needn't show every extreme that they name: `positions`: coordinates in angstroms; the third runs along the fiber. near_tiles[a, b, k] is 1 when the partner tile of step k is near tile (a, b), else 0. The relation is symmetric: a tile is near its partner exactly when the partner is near it by the opposite step. No tile is near a tile beyond either end of the first tile dimension; the second dimension closes around the fiber. `segment`: within each tile the component numbers never fall along the atoms, and each of the 16 components has 1 to 16 atoms.
All inputs are finite; a program needn't handle non-finite values.
Results may differ from the reference program's by a relative error of at most 0.0003.
Values sent between devices are 32-bit elements; how exact they have to be, the bound alone decides.
No kernel may reach another device: no remote copies, remote signals or barrier semaphores. Data moves between devices by JAX's collectives and lax.ppermute only.
A program may use at most 64 MiB of HBM per device.

```python
import math
import jax
import jax.numpy as jnp
import numpy as np
from jax import lax

TILE = 128
CT = 16
SEG_MOST = 16
GZ = 8
GS = 16
COMPS = 2048


def draw_positions(key, part):
    uniform_draw = jax.random.uniform(key, (3, GZ, GS, TILE), jnp.float32)
    tile_z = jnp.arange(GZ, dtype=jnp.float32)[:, None, None]
    tile_s = jnp.arange(GS, dtype=jnp.float32)[None, :, None]
    along_axis = (tile_z + uniform_draw[0]) * 10.0
    angle_around = 2.0 * math.pi * (tile_s + uniform_draw[1]) / GS
    distance_out = 45.0 + 5.0 * uniform_draw[2]
    return jnp.stack([distance_out * jnp.cos(angle_around), distance_out * jnp.sin(angle_around), along_axis])


def draw_near_tiles(key, part):
    first_key, second_key = jax.random.split(key)
    density = jax.random.randint(first_key, (GZ, 1), 4, 11)
    coin_draw = jax.random.randint(second_key, (4, GZ, GS), 0, 10)
    forward_bits = (coin_draw < density[None]).astype(jnp.int32)
    forward_bits = forward_bits.at[1:4, GZ - 1].set(0)
    forward_steps = ((0, 1), (1, -1), (1, 0), (1, 1))
    backward = []
    for which_step in range(4):
        step_z, step_s = forward_steps[which_step]
        backward.append(jnp.roll(forward_bits[which_step], (step_z, step_s), axis=(0, 1)))
    slot_list = [backward[3], backward[2], backward[1], backward[0], forward_bits[0], forward_bits[1], forward_bits[2], forward_bits[3]]
    return jnp.stack(slot_list, axis=-1).astype(jnp.int32)


def steps_of(rng, shape, cuts, low, high):
    def one(axis_at, shards_of):
        draws = jax.random.uniform(jax.random.fold_in(jax.random.fold_in(rng, 6), axis_at), (shards_of,), jnp.float32, low / len(cuts), high / len(cuts))
        return jnp.repeat(jnp.exp(draws), shape[axis_at] // shards_of).reshape((-1,) + (1,) * (len(shape) - axis_at - 1))

    level = one(*cuts[0])
    for cut in cuts[1:]:
        level = level * one(*cut)
    return level


def length_profile(number_of, total, bound, skew):
    weights = [(1 << 20) // math.isqrt(rank ** skew) + 1 for rank in range(2, number_of + 1)]
    spare, holding = total - bound - (number_of - 1), [1] * (number_of - 1)
    while spare > 0:
        movable = [i for i in range(number_of - 1) if holding[i] < bound]
        mass, remaining = sum([weights[i] for i in movable]), spare
        for i in movable:
            more = min(bound - holding[i], max(1, remaining * weights[i] // mass), spare)
            holding[i] = holding[i] + more
            spare = spare - more
    return np.array([bound] + holding)


def uneven_parts(key, amount, total, most, lean):
    if amount == 2:
        one = jax.random.randint(key, (), max(1, total - most), min(most, total - 1) + 1)
        return jnp.stack([one, total - one])
    lengths = jnp.asarray(length_profile(amount, total, most, lean), jnp.int32)
    pairs = (amount - 1) // 2
    donor, receiver = lengths[1:1 + 2 * pairs:2], lengths[2:2 + 2 * pairs:2]
    slack = jnp.minimum(donor - 1, most - receiver)
    shifted = jax.random.randint(jax.random.fold_in(key, 1), (pairs,), 0, 1 << 20) % (slack + 1)
    lengths = lengths.at[1:1 + 2 * pairs:2].set(donor - shifted).at[2:2 + 2 * pairs:2].set(receiver + shifted)
    return lengths[jax.random.permutation(jax.random.fold_in(key, 2), amount)]


def gaussian(stream_key, shape, deviation, bound, cuts=(), kind=jnp.bfloat16):
    level = steps_of(stream_key, shape, cuts, -0.22, 0.18) if cuts else 1.0
    values = jax.random.normal(stream_key, shape, jnp.float32) * deviation * level
    return jnp.minimum(jnp.maximum(values, -bound), bound).astype(kind)


def setup_inputs(seed: int = 0, part: int = 0) -> dict:
    seeds = jax.random.split(jax.random.key(seed), 6)
    part_keys = jax.random.split(jax.random.fold_in(seeds[5], part), 6)
    return {
        "positions": draw_positions(jax.random.fold_in(jax.random.fold_in(seeds[5], part), 71), part),
        "charge": gaussian(part_keys[1], (GZ, GS, TILE), 0.5, 2.5, ((0, 4), (1, 4)), jnp.float32),
        "radius": jnp.clip(1.3 + 0.9000001 * jax.random.uniform(part_keys[2], (GZ, GS, TILE), jnp.float32) ** steps_of(part_keys[2], (GZ, GS, TILE), ((0, 4), (1, 4)), -0.2, 0.2), 1.3, 2.2),
        "segment": jax.vmap(lambda own: jnp.searchsorted(jnp.cumsum(uneven_parts(own, CT, TILE, SEG_MOST, 1)), jnp.arange(TILE), side="right"))(jax.random.split(part_keys[3], GZ * GS)).reshape((GZ, GS, TILE)).astype(jnp.int32),
        "near_tiles": draw_near_tiles(jax.random.fold_in(jax.random.fold_in(seeds[5], part), 71), part),
    }


neighbour_steps = ((-1, -1), (-1, 0), (-1, 1), (0, -1), (0, 1), (1, -1), (1, 0), (1, 1))
switch_span = 64.0
radius_factor = 1.5
highest = lax.Precision.HIGHEST

def far_keep(tile_along, tile_round, tile_near, comp_along, comp_round, around_count):
    struck = (tile_along[:, None] == comp_along[None, :]) & (tile_round[:, None] == comp_round[None, :])
    for slot_index, (step_z, step_s) in enumerate(neighbour_steps):
        flagged = (tile_near[:, slot_index] == 1)[:, None]
        same_along = (tile_along + step_z)[:, None] == comp_along[None, :]
        same_round = jnp.mod(tile_round + step_s, around_count)[:, None] == comp_round[None, :]
        struck = struck | flagged & same_along & same_round
    return jnp.logical_not(struck)

def pair_distance(own_pos, part_pos):
    dist_sq = jnp.zeros(own_pos.shape[1:] + (part_pos.shape[-1],), own_pos.dtype)
    for axis_slot in range(3):
        apart_axis = own_pos[axis_slot][..., :, None] - part_pos[axis_slot][..., None, :]
        dist_sq = dist_sq + apart_axis * apart_axis
    return dist_sq

def born_distance(dist_sq, product):
    return jnp.sqrt(dist_sq + product * jnp.exp(-dist_sq / (4.0 * product)))

def tile_screen(own_pos, part_pos, part_rho, keep_mask):
    dist_sq = pair_distance(own_pos, part_pos)
    radius_sq = part_rho[..., None, :] * part_rho[..., None, :]
    denom_sq = dist_sq + radius_sq
    pair_term = radius_sq * part_rho[..., None, :] / (denom_sq * denom_sq)
    return lax.optimization_barrier(jnp.sum(jnp.where(keep_mask, pair_term, 0.0), axis=-1))

def tile_energy(own_pos, own_born, part_pos, part_q, part_born, keep_mask):
    dist_sq = pair_distance(own_pos, part_pos)
    product = own_born[..., :, None] * part_born[..., None, :]
    pair_term = part_q[..., None, :] / born_distance(dist_sq, product)
    return lax.optimization_barrier(jnp.sum(jnp.where(keep_mask, pair_term, 0.0), axis=-1))

def centre_distance(flat_pos, centre):
    dist_sq = jnp.zeros((flat_pos.shape[1], centre.shape[1]), flat_pos.dtype)
    for axis_slot in range(3):
        apart_axis = flat_pos[axis_slot][:, None] - centre[axis_slot][None, :]
        dist_sq = dist_sq + apart_axis * apart_axis
    return dist_sq

def screen_block(flat_pos, centre, volume, comp_radius, keep):
    dist_sq = centre_distance(flat_pos, centre)
    weight = dist_sq / (dist_sq + switch_span)
    denom_sq = dist_sq + comp_radius * comp_radius
    return lax.optimization_barrier(jnp.sum(jnp.where(keep, volume * weight / (denom_sq * denom_sq), 0.0), axis=1))

def potential_block(flat_pos, flat_born, centre, total_q, comp_radius, keep):
    dist_sq = centre_distance(flat_pos, centre)
    weight = dist_sq / (dist_sq + switch_span)
    product = flat_born[:, None] * comp_radius[None, :]
    return lax.optimization_barrier(jnp.sum(jnp.where(keep, total_q * weight / born_distance(dist_sq, product), 0.0), axis=1))

def components(positions, charge, radius, segment):
    onehot = (segment[..., None] == jnp.arange(CT, dtype=jnp.int32)).astype(jnp.float32)
    members = lax.optimization_barrier(jnp.sum(onehot, axis=2))
    total_q = jnp.einsum('abl,ablc->abc', charge, onehot, precision=highest)
    volume = jnp.einsum('abl,ablc->abc', radius * radius * radius, onehot, precision=highest)
    comp_radius = radius_factor * jnp.einsum('abl,ablc->abc', radius, onehot, precision=highest) / members
    return (onehot, members, total_q, volume, comp_radius)

def roll_tiles(values, step_z, step_s):
    return jnp.roll(values, (-step_z, -step_s), axis=(values.ndim - 3, values.ndim - 2))

def tile_keys(near_tiles):
    tile_index = jnp.arange(GZ * GS, dtype=jnp.int32)
    comp_tile = jnp.arange(COMPS, dtype=jnp.int32) // CT
    return (tile_index // GS, tile_index % GS, near_tiles.reshape(-1, 8), comp_tile // GS, comp_tile % GS)

def block_keep(width, along_one, round_one, near_row, comp_along, comp_round):
    zeros_int = jnp.zeros((width,), jnp.int32)
    near_rows = jnp.broadcast_to(near_row[None, :], (width, 8))
    return far_keep(zeros_int + along_one, zeros_int + round_one, near_rows, comp_along, comp_round, GS)

def born_field(coords, radius, near_tiles, centre, volume, comp_radius):
    tile_width = coords.shape[-1]
    self_keep = jnp.arange(tile_width)[:, None] != jnp.arange(tile_width)[None, :]
    screen_fn = jax.checkpoint(tile_screen)
    screening = screen_fn(coords, coords, radius, self_keep)
    for slot_index, (step_z, step_s) in enumerate(neighbour_steps):
        keep_mask = (near_tiles[..., slot_index] == 1)[..., None, None]
        screening = screening + screen_fn(coords, roll_tiles(coords, step_z, step_s), roll_tiles(radius, step_z, step_s), keep_mask)
    blocks = jnp.moveaxis(coords.reshape(3, -1, tile_width), 1, 0)
    tile_alongs, tile_rounds, near_rows, comp_along, comp_round = tile_keys(near_tiles)

    def far_fn(pieces):
        keep = block_keep(tile_width, pieces[1], pieces[2], pieces[3], comp_along, comp_round)
        return screen_block(pieces[0], centre, volume, comp_radius, keep)
    far_part = lax.map(jax.checkpoint(far_fn), (blocks, tile_alongs, tile_rounds, near_rows))
    screening = screening + far_part.reshape(radius.shape)
    return radius * (1.0 + radius * screening)

def energy_field(coords, radii_now, charge, near_tiles, centre, total_q, comp_radius):
    tile_width = coords.shape[-1]
    self_keep = jnp.arange(tile_width)[:, None] != jnp.arange(tile_width)[None, :]
    energy_fn = jax.checkpoint(tile_energy)
    potential = energy_fn(coords, radii_now, coords, charge, radii_now, self_keep)
    for slot_index, (step_z, step_s) in enumerate(neighbour_steps):
        keep_mask = (near_tiles[..., slot_index] == 1)[..., None, None]
        potential = potential + energy_fn(coords, radii_now, roll_tiles(coords, step_z, step_s), roll_tiles(charge, step_z, step_s), roll_tiles(radii_now, step_z, step_s), keep_mask)
    pos_blocks = jnp.moveaxis(coords.reshape(3, -1, tile_width), 1, 0)
    born_blocks = radii_now.reshape(-1, tile_width)
    tile_alongs, tile_rounds, near_rows, comp_along, comp_round = tile_keys(near_tiles)

    def far_fn(pieces):
        keep = block_keep(tile_width, pieces[2], pieces[3], pieces[4], comp_along, comp_round)
        return potential_block(pieces[0], pieces[1], centre, total_q, comp_radius, keep)
    far_part = lax.map(jax.checkpoint(far_fn), (pos_blocks, born_blocks, tile_alongs, tile_rounds, near_rows))
    potential = potential + far_part.reshape(charge.shape)
    return -0.5 * jnp.sum(charge * (charge / radii_now + potential))

def reference(positions, charge, radius, segment, near_tiles):
    onehot, members, total_q, volume, comp_radius = components(positions, charge, radius, segment)
    flat_q = total_q.reshape(-1)
    flat_volume = volume.reshape(-1)
    flat_radius = comp_radius.reshape(-1)

    def centres_of(coords):
        return (jnp.einsum('kabl,ablc->kabc', coords, onehot, precision=highest) / members).reshape(3, -1)

    def born_of(coords):
        return born_field(coords, radius, near_tiles, centres_of(coords), flat_volume, flat_radius)

    def energy_of(coords, radii_now):
        return energy_field(coords, radii_now, charge, near_tiles, centres_of(coords), flat_q, flat_radius)
    born_radii, born_back = jax.vjp(born_of, positions)
    energy_back = jax.vjp(energy_of, positions, born_radii)[1]
    grad_pos, radius_grad = energy_back(jnp.ones((), jnp.float32))
    chain_pos = born_back(radius_grad)[0]
    return (born_radii, radius_grad, -(grad_pos + chain_pos))
```

```python
import jax
import jax.numpy as jnp
from jax import lax
from jax.experimental import pallas as pl
from jax.experimental.pallas import tpu as pltpu
from jax.sharding import PartitionSpec as P

CT = 16
LANES = 128
SUBLANES = 8
WIDE = 2
SPAN = 64.0
RADIUS_FACTOR = 1.5
LOG2E = 1.4426950408889634
LN2 = 0.6931471805599453
HIGHEST = lax.Precision.HIGHEST
AXES = ("dom", "sub")
STEPS = ((-1, -1), (-1, 0), (-1, 1), (0, -1), (0, 1), (1, -1), (1, 0), (1, 1))
SELF = len(STEPS)
NEAR = len(STEPS) + 1


def side_tiles(rz, rs, rows, cols):
    along = {0: range(rows), 1: [rows - 1], -1: [0]}[rz]
    around = {0: range(cols), 1: [cols - 1], -1: [0]}[rs]
    return [(a, b) for a in along for b in around]


def partner(a, b, k, rows, cols):
    dz, ds = STEPS[k] if k < SELF else (0, 0)
    az, bs = a + dz, b + ds
    rz = -1 if az < 0 else 1 if az >= rows else 0
    rs = -1 if bs < 0 else 1 if bs >= cols else 0
    tile = (az % rows, bs % cols)
    if rz == 0 and rs == 0:
        return (0, 0), None, tile
    return (rz, rs), side_tiles(-rz, -rs, rows, cols).index(tile), tile


def device_at(rz, rs, dom_count, sub_count):
    along = jnp.clip(lax.axis_index("dom") + rz, 0, dom_count - 1)
    around = lax.rem(lax.axis_index("sub") + rs + sub_count, sub_count)
    return along * sub_count + around


def in_range(rz, dom_count):
    at = lax.axis_index("dom") + rz
    return (at >= 0) & (at < dom_count)


def far_unroll(devices):
    return 16 if devices % 16 == 0 else 1


def member_table(seg_ref, a, b, cols):
    comp = lax.broadcasted_iota(jnp.int32, (LANES, LANES), 0)
    owner = seg_ref[a, b : b + 1, :] + (a * cols + b) * CT
    return (comp == owner).astype(jnp.float32)


def turned(row):
    block = jnp.broadcast_to(row, (LANES, LANES)).T
    return block.reshape(LANES // SUBLANES, SUBLANES, LANES)


def lane_sums(block):
    return jnp.sum(block.reshape(LANES, LANES).T, axis=0, keepdims=True)


def pack_body(dims, pos_ref, q_ref, r_ref, seg_ref, send_ref, members_ref):
    rows, cols, dom_count, sub_count = dims
    slots = max(rows, cols)
    total = jnp.zeros((SUBLANES, LANES), jnp.float32)
    one = jnp.ones((1, LANES), jnp.float32)
    for a in range(rows):
        for b in range(cols):
            at = slice(b, b + 1)
            rho = r_ref[a, at, :]
            values = jnp.concatenate(
                [pos_ref[0, a, at, :], pos_ref[1, a, at, :], pos_ref[2, a, at, :],
                 q_ref[a, at, :], rho * rho * rho, rho, one, one], axis=0)
            total = total + lax.dot_general(
                values, member_table(seg_ref, a, b, cols), (((1,), (1,)), ((), ())),
                precision=HIGHEST, preferred_element_type=jnp.float32)
    members = total[6:7]
    comp_radius = RADIUS_FACTOR * total[5:6] / members
    table = jnp.concatenate(
        [total[0:3] / members, total[3:5], comp_radius, (-0.25 * LOG2E) / comp_radius,
         comp_radius * comp_radius], axis=0)
    members_ref[...] = jnp.broadcast_to(members, (SUBLANES, LANES))

    def put(d, carry):
        send_ref[d, 0:8, :] = table
        return carry

    lax.fori_loop(0, dom_count * sub_count, put, 0)
    for rz in (-1, 0, 1):
        for rs in (-1, 0, 1):
            where = device_at(rz, rs, dom_count, sub_count)

            @pl.when(in_range(rz, dom_count))
            def _(rz=rz, rs=rs, where=where):
                for slot, (a, b) in enumerate(side_tiles(rz, rs, rows, cols)[:slots]):
                    at = slice(b, b + 1)
                    for c in range(3):
                        line = 8 + c * slots + slot
                        send_ref[where, line : line + 1, :] = pos_ref[c, a, at, :]
                    line = 8 + 3 * slots + slot
                    send_ref[where, line : line + 1, :] = r_ref[a, at, :]


def near_row(dims, k, a, b, recv_ref, own, base, c):
    rows, cols, dom_count, sub_count = dims
    slots = max(rows, cols)
    (rz, rs), slot, (pa, pb) = partner(a, b, k, rows, cols)
    if slot is None:
        return own(c, pa, pb)
    line = base + c * slots + slot
    return recv_ref[device_at(rz, rs, dom_count, sub_count), line : line + 1, :]


def mask_rows(dims, near_ref, table_ref):
    rows, cols, dom_count, sub_count = dims
    tile_of = lax.broadcasted_iota(jnp.int32, (1, LANES), 1) // CT
    for a in range(rows):
        for b in range(cols):
            t = a * cols + b
            for k in range(NEAR):
                (rz, rs), _, (pa, pb) = partner(a, b, k, rows, cols)
                where = device_at(rz, rs, dom_count, sub_count)
                struck = tile_of == pa * cols + pb
                if k < SELF:
                    struck = struck & (near_ref[a, b, k] == 1)
                kept = table_ref[where, t : t + 1, :]
                table_ref[where, t : t + 1, :] = jnp.where(struck, 0.0, kept)


def spread(ref, lead, line):
    return ref[lead, pl.ds(line, SUBLANES, stride=0), :]


def own_pair_mask(g, t, v):
    atom = (g * WIDE + v - t * (LANES // SUBLANES)) * SUBLANES
    atom = atom + lax.broadcasted_iota(jnp.int32, (SUBLANES, LANES), 0)
    return atom == lax.broadcasted_iota(jnp.int32, (SUBLANES, LANES), 1)


def screen_body(dims, near_ref, recv_ref, pos_ref, q_ref, r_ref, born_ref, send_ref,
                turned_ref, near_tab, far_vol, sums_ref):
    rows, cols, dom_count, sub_count = dims
    devices = dom_count * sub_count
    slots = max(rows, cols)
    per_tile = LANES // SUBLANES

    def own(c, a, b):
        if c < 3:
            return pos_ref[c, a, b : b + 1, :]
        return r_ref[a, b : b + 1, :]

    def put(d, carry):
        far_vol[d] = jnp.broadcast_to(recv_ref[d, 4:5, :], (rows * cols, LANES))
        return carry

    lax.fori_loop(0, devices, put, 0)
    mask_rows(dims, near_ref, far_vol)
    for a in range(rows):
        for b in range(cols):
            t = a * cols + b
            for c in range(3):
                turned_ref[c, t * per_tile : (t + 1) * per_tile] = turned(own(c, a, b))
            for k in range(NEAR):
                x, y, z, rho = [near_row(dims, k, a, b, recv_ref, own, 8, c) for c in range(4)]
                volume = rho * rho * rho
                if k < SELF:
                    volume = jnp.where(near_ref[a, b, k] == 1, volume, 0.0)
                near_tab[t * NEAR + k, 0:1, :] = x
                near_tab[t * NEAR + k, 1:2, :] = y
                near_tab[t * NEAR + k, 2:3, :] = z
                near_tab[t * NEAR + k, 3:4, :] = rho * rho
                near_tab[t * NEAR + k, 4:5, :] = volume

    unroll = far_unroll(devices)

    def group(g, carry):
        t = g // (per_tile // WIDE)
        own_at = [[turned_ref[c, g * WIDE + v] for c in range(3)] for v in range(WIDE)]

        def dist(v, x, y, z):
            dx, dy, dz = own_at[v][0] - x, own_at[v][1] - y, own_at[v][2] - z
            return dx * dx + dy * dy + dz * dz

        sums = [jnp.zeros((SUBLANES, LANES), jnp.float32) for _ in range(WIDE)]
        for k in range(NEAR):
            x, y, z, rho_sq, volume = [spread(near_tab, t * NEAR + k, c) for c in range(5)]
            for v in range(WIDE):
                vol = jnp.where(own_pair_mask(g, t, v), 0.0, volume) if k == SELF else volume
                d = dist(v, x, y, z) + rho_sq
                sums[v] = sums[v] + vol / (d * d)

        def chunk(n, sums):
            sums = list(sums)
            for j in range(unroll):
                d = n * unroll + j
                x, y, z = [spread(recv_ref, d, c) for c in range(3)]
                rho_sq = spread(recv_ref, d, 7)
                volume = spread(far_vol, d, t)
                for v in range(WIDE):
                    s = dist(v, x, y, z)
                    near = s + rho_sq
                    sums[v] = sums[v] + volume * s / ((s + SPAN) * (near * near))
            return tuple(sums)

        sums = lax.fori_loop(0, devices // unroll, chunk, tuple(sums))
        for v in range(WIDE):
            sums_ref[g * WIDE + v] = sums[v]
        return carry

    lax.fori_loop(0, rows * cols * per_tile // WIDE, group, 0)
    for a in range(rows):
        for b in range(cols):
            t = a * cols + b
            screening = lane_sums(sums_ref[t * per_tile : (t + 1) * per_tile])
            rho = r_ref[a, b : b + 1, :]
            born_ref[a, b : b + 1, :] = rho * (1.0 + rho * screening)
    for rz in (-1, 0, 1):
        for rs in (-1, 0, 1):
            where = device_at(rz, rs, dom_count, sub_count)

            @pl.when(in_range(rz, dom_count))
            def _(rz=rz, rs=rs, where=where):
                for slot, (a, b) in enumerate(side_tiles(rz, rs, rows, cols)[:slots]):
                    send_ref[where, slot : slot + 1, :] = born_ref[a, b : b + 1, :]
                    line = slots + slot
                    send_ref[where, line : line + 1, :] = q_ref[a, b : b + 1, :]


def energy_body(dims, near_ref, recv_ref, halo_ref, pos_ref, q_ref, r_ref, born_ref,
                rgrad_ref, grad_ref, send_ref,
                turned_ref, near_tab, far_vol, far_q, pair_f, pair_s, far_acc, near_acc,
                sums_ref, rg_turned):
    rows, cols, dom_count, sub_count = dims
    devices = dom_count * sub_count
    slots = max(rows, cols)
    tiles = rows * cols
    per_tile = LANES // SUBLANES

    def own(c, a, b):
        at = slice(b, b + 1)
        if c < 3:
            return pos_ref[c, a, at, :]
        return r_ref[a, at, :]

    def own_late(c, a, b):
        at = slice(b, b + 1)
        return born_ref[a, at, :] if c == 0 else q_ref[a, at, :]

    zero = jnp.zeros((SUBLANES, LANES), jnp.float32)

    def put(d, carry):
        far_vol[d] = jnp.broadcast_to(recv_ref[d, 4:5, :], (tiles, LANES))
        far_q[d] = jnp.broadcast_to(0.5 * recv_ref[d, 3:4, :], (tiles, LANES))
        for c in range(3):
            far_acc[d, c] = zero
        return carry

    lax.fori_loop(0, devices, put, 0)
    mask_rows(dims, near_ref, far_vol)
    mask_rows(dims, near_ref, far_q)
    for a in range(rows):
        for b in range(cols):
            t = a * cols + b
            at = slice(b, b + 1)
            own_rows = [own(0, a, b), own(1, a, b), own(2, a, b), born_ref[a, at, :],
                        q_ref[a, at, :], r_ref[a, at, :]]
            for c, row in enumerate(own_rows):
                turned_ref[c, t * per_tile : (t + 1) * per_tile] = turned(row)
            for k in range(NEAR):
                x, y, z, rho = [near_row(dims, k, a, b, recv_ref, own, 8, c) for c in range(4)]
                born, charge = [near_row(dims, k, a, b, halo_ref, own_late, 0, c) for c in range(2)]
                volume = rho * rho * rho
                charge = 0.5 * charge
                if k < SELF:
                    flagged = near_ref[a, b, k] == 1
                    volume = jnp.where(flagged, volume, 0.0)
                    charge = jnp.where(flagged, charge, 0.0)
                lines = [x, y, z, born, (-0.25 * LOG2E) / born, charge, rho * rho, volume]
                for c, row in enumerate(lines):
                    near_tab[t * NEAR + k, c : c + 1, :] = row
                for c in range(3):
                    near_acc[t * NEAR + k, c] = zero

    unroll = far_unroll(devices)
    trips = devices // unroll

    def group(g, carry):
        t = g // (per_tile // WIDE)
        mine = [[turned_ref[c, g * WIDE + v] for c in range(6)] for v in range(WIDE)]
        inverse = [1.0 / mine[v][3] for v in range(WIDE)]

        def apart(v, x, y, z):
            return mine[v][0] - x, mine[v][1] - y, mine[v][2] - z

        def pair(v, x, y, z, other_born, other_inv):
            dx, dy, dz = apart(v, x, y, z)
            s = dx * dx + dy * dy + dz * dz
            power = s * (inverse[v] * other_inv)
            e = jnp.exp2(power)
            pe = (mine[v][3] * other_born) * e
            r = lax.rsqrt(s + pe)
            return s, 1.0 - LN2 * power, 1.0 - 0.25 * e, pe, r, r * r

        born_near = [zero] * WIDE
        for k in range(NEAR):
            x, y, z, other, other_inv, charge = [
                spread(near_tab, t * NEAR + k, c) for c in range(6)]
            for v in range(WIDE):
                s, grow, fade, pe, r, rr = pair(v, x, y, z, other, other_inv)
                q = jnp.where(own_pair_mask(g, t, v), 0.0, charge) if k == SELF else charge
                h = (q * (mine[v][4] * r)) * rr
                pair_f[devices + k, v] = h * fade
                pair_s[devices + k, v] = s
                born_near[v] = born_near[v] + (h * pe) * grow

        def far_energy(n, born_far):
            born_far = list(born_far)
            for j in range(unroll):
                d = n * unroll + j
                x, y, z = [spread(recv_ref, d, c) for c in range(3)]
                other, other_inv = spread(recv_ref, d, 5), spread(recv_ref, d, 6)
                charge = spread(far_q, d, t)
                for v in range(WIDE):
                    s, grow, fade, pe, r, rr = pair(v, x, y, z, other, other_inv)
                    inv = 1.0 / (s + SPAN)
                    qr = charge * (mine[v][4] * r)
                    wr = (s * inv) * rr
                    pair_f[d, v] = qr * (wr * fade - (2.0 * SPAN) * (inv * inv))
                    pair_s[d, v] = s
                    born_far[v] = born_far[v] + qr * ((wr * pe) * grow)
            return tuple(born_far)

        born_far = lax.fori_loop(0, trips, far_energy, tuple([zero] * WIDE))

        scale = []
        for v in range(WIDE):
            part = inverse[v] * (0.5 * born_far[v] + born_near[v])
            own_part = mine[v][4] * inverse[v]
            rg = jnp.sum(part, axis=1, keepdims=True) + 0.5 * (own_part * own_part)
            rg_turned[g * WIDE + v] = rg
            scale.append(4.0 * rg * (mine[v][5] * mine[v][5]))

        own_grad = [[zero] * 3 for _ in range(WIDE)]
        for k in range(NEAR):
            j = t * NEAR + k
            x, y, z = [spread(near_tab, j, c) for c in range(3)]
            rho_sq, volume = spread(near_tab, j, 6), spread(near_tab, j, 7)
            other_grad = [zero] * 3
            for v in range(WIDE):
                inv = 1.0 / (pair_s[devices + k, v] + rho_sq)
                f = pair_f[devices + k, v] - (scale[v] * volume) * (inv * inv * inv)
                for c, delta in enumerate(apart(v, x, y, z)):
                    part = f * delta
                    own_grad[v][c] = own_grad[v][c] + part
                    other_grad[c] = other_grad[c] + part
            for c in range(3):
                near_acc[j, c] = near_acc[j, c] + other_grad[c]

        def far_chain(n, flat):
            own_grad = [list(flat[3 * v : 3 * v + 3]) for v in range(WIDE)]
            for j in range(unroll):
                d = n * unroll + j
                x, y, z = [spread(recv_ref, d, c) for c in range(3)]
                rho_sq = spread(recv_ref, d, 7)
                volume = spread(far_vol, d, t)
                other_grad = [zero] * 3
                for v in range(WIDE):
                    s = pair_s[d, v]
                    wide, near = s + SPAN, s + rho_sq
                    inv = 1.0 / (wide * near)
                    slope = (0.5 * SPAN * near - s * wide) * ((inv * inv) * (inv * wide))
                    f = pair_f[d, v] + (scale[v] * volume) * slope
                    for c, delta in enumerate(apart(v, x, y, z)):
                        part = f * delta
                        own_grad[v][c] = own_grad[v][c] + part
                        other_grad[c] = other_grad[c] + part
                for c in range(3):
                    far_acc[d, c] = far_acc[d, c] + other_grad[c]
            return tuple(own_grad[v][c] for v in range(WIDE) for c in range(3))

        flat = lax.fori_loop(
            0, trips, far_chain, tuple(own_grad[v][c] for v in range(WIDE) for c in range(3)))
        for v in range(WIDE):
            for c in range(3):
                sums_ref[c, g * WIDE + v] = flat[3 * v + c]
        return carry

    lax.fori_loop(0, tiles * per_tile // WIDE, group, 0)

    def send_far(d, carry):
        for c in range(3):
            send_ref[d, c : c + 1, :] = -jnp.sum(far_acc[d, c], axis=0, keepdims=True)
        return carry

    lax.fori_loop(0, devices, send_far, 0)
    owed = {}
    for a in range(rows):
        for b in range(cols):
            for k in range(NEAR):
                rel, slot, tile = partner(a, b, k, rows, cols)
                key = (rel, slot) if slot is not None else tile
                owed.setdefault(key, []).append((a * cols + b) * NEAR + k)

    def partner_sum(places, c):
        total = near_acc[places[0], c]
        for place in places[1:]:
            total = total + near_acc[place, c]
        return jnp.sum(total, axis=0, keepdims=True)

    for a in range(rows):
        for b in range(cols):
            t = a * cols + b
            at = slice(t * per_tile, (t + 1) * per_tile)
            rgrad_ref[a, b : b + 1, :] = rg_turned[at].reshape(LANES, LANES).T[0:1]
            for c in range(3):
                grad_ref[c, a, b : b + 1, :] = (
                    lane_sums(sums_ref[c, at]) - partner_sum(owed[(a, b)], c))
    for rz in (-1, 0, 1):
        for rs in (-1, 0, 1):
            if rz == 0 and rs == 0:
                continue
            where = device_at(rz, rs, dom_count, sub_count)

            @pl.when(in_range(rz, dom_count))
            def _(rz=rz, rs=rs, where=where):
                for slot in range(len(side_tiles(rz, rs, rows, cols))):
                    for c in range(3):
                        line = 3 + c * slots + slot
                        send_ref[where, line : line + 1, :] = -partner_sum(
                            owed[((rz, rs), slot)], c)


def finish_body(dims, recv_ref, grad_ref, members_ref, seg_ref, force_ref):
    rows, cols, dom_count, sub_count = dims
    slots = max(rows, cols)

    def add(d, total):
        return total + recv_ref[d, 0:3, :]

    centre_grad = lax.fori_loop(
        0, dom_count * sub_count, add, jnp.zeros((3, LANES), jnp.float32))
    per_member = centre_grad / members_ref[0:3, :]
    per_member = jnp.concatenate([per_member, jnp.zeros((5, LANES), jnp.float32)], axis=0)
    for a in range(rows):
        for b in range(cols):
            spread_out = lax.dot_general(
                per_member, member_table(seg_ref, a, b, cols), (((1,), (0,)), ((), ())),
                precision=HIGHEST, preferred_element_type=jnp.float32)
            for c in range(3):
                force_ref[c, a, b : b + 1, :] = -(
                    grad_ref[c, a, b : b + 1, :] + spread_out[c : c + 1])
    for rz in (-1, 0, 1):
        for rs in (-1, 0, 1):
            if rz == 0 and rs == 0:
                continue
            where = device_at(rz, rs, dom_count, sub_count)

            @pl.when(in_range(rz, dom_count))
            def _(rz=rz, rs=rs, where=where):
                for slot, (a, b) in enumerate(side_tiles(rz, rs, rows, cols)):
                    for c in range(3):
                        line = 3 + c * slots + slot
                        force_ref[c, a, b : b + 1, :] = (
                            force_ref[c, a, b : b + 1, :] - recv_ref[where, line : line + 1, :])


def f32(*shape):
    return jax.ShapeDtypeStruct(shape, jnp.float32)


def local(positions, charge, radius, segment, near_tiles):
    rows, cols, width = charge.shape
    dom_count, sub_count = lax.axis_size("dom"), lax.axis_size("sub")
    dims = (rows, cols, dom_count, sub_count)
    devices = dom_count * sub_count
    tiles = rows * cols
    assert width == LANES and tiles * CT == LANES and sub_count > 2
    slots = max(rows, cols)
    vectors = tiles * LANES // SUBLANES
    vmem = pltpu.MemorySpace.VMEM
    vec = (SUBLANES, LANES)

    def call(body, ins, outs, scratch=()):
        return pl.pallas_call(
            lambda *refs: body(dims, *refs),
            out_shape=outs,
            in_specs=[pl.BlockSpec(memory_space=pltpu.MemorySpace.SMEM if x is near_tiles else vmem)
                      for x in ins],
            out_specs=[pl.BlockSpec(memory_space=vmem) for _ in outs],
            scratch_shapes=list(scratch),
            compiler_params=pltpu.CompilerParams(vmem_limit_bytes=48 << 20),
            name=body.__name__,
        )(*ins)

    def exchanged(blocks):
        return lax.all_to_all(blocks, AXES, 0, 0, tiled=True)

    send, members = call(
        pack_body, (positions, charge, radius, segment),
        [f32(devices, 8 + 4 * slots, LANES), f32(*vec)])
    table = exchanged(send)
    born_radii, send = call(
        screen_body, (near_tiles, table, positions, charge, radius),
        [f32(rows, cols, LANES), f32(devices, 2 * slots, LANES)],
        [pltpu.VMEM((3, vectors) + vec, jnp.float32),
         pltpu.VMEM((tiles * NEAR,) + vec, jnp.float32),
         pltpu.VMEM((devices, tiles, LANES), jnp.float32),
         pltpu.VMEM((vectors,) + vec, jnp.float32)])
    halo = exchanged(send)
    radius_grad, grad, send = call(
        energy_body, (near_tiles, table, halo, positions, charge, radius, born_radii),
        [f32(rows, cols, LANES), f32(3, rows, cols, LANES), f32(devices, 4 + 3 * slots, LANES)],
        [pltpu.VMEM((6, vectors) + vec, jnp.float32),
         pltpu.VMEM((tiles * NEAR,) + vec, jnp.float32),
         pltpu.VMEM((devices, tiles, LANES), jnp.float32),
         pltpu.VMEM((devices, tiles, LANES), jnp.float32),
         pltpu.VMEM((devices + NEAR, WIDE) + vec, jnp.float32),
         pltpu.VMEM((devices + NEAR, WIDE) + vec, jnp.float32),
         pltpu.VMEM((devices, 3) + vec, jnp.float32),
         pltpu.VMEM((tiles * NEAR, 3) + vec, jnp.float32),
         pltpu.VMEM((3, vectors) + vec, jnp.float32),
         pltpu.VMEM((vectors,) + vec, jnp.float32)])
    back = exchanged(send)
    forces = call(
        finish_body, (back, grad, members, segment), [f32(3, rows, cols, LANES)])[0]
    return born_radii, radius_grad, forces


def solution(mesh):
    flat = P(("groups", "dom"), "sub", None)
    stacked = P(None, ("groups", "dom"), "sub", None)
    return jax.shard_map(
        local,
        mesh=mesh,
        in_specs=(stacked, flat, flat, flat, flat),
        out_specs=(flat, flat, stacked),
        check_vma=False,
    )
```

```python
import jax
import jax.numpy as jnp
from jax import lax
from jax.experimental import pallas as pl
from jax.experimental.pallas import tpu as pltpu
from jax.sharding import PartitionSpec as P

CT = 16
LANES = 128
SUBLANES = 8
UNIT = 128.0
KROWS = 48
WROWS = 16
SPAN = 64.0
CHARGE_UNIT = 0.5 * UNIT ** -1.5
RADIUS_FACTOR = 1.5
LOG2E = 1.4426950408889634
LN2 = 0.6931471805599453
HIGHEST = lax.Precision.HIGHEST
AXES = ("dom", "sub")
STEPS = ((-1, -1), (-1, 0), (-1, 1), (0, -1), (0, 1), (1, -1), (1, 0), (1, 1))
SELF = len(STEPS)
NEAR = len(STEPS) + 1


def side_tiles(rz, rs, rows, cols):
    along = {0: range(rows), 1: [rows - 1], -1: [0]}[rz]
    around = {0: range(cols), 1: [cols - 1], -1: [0]}[rs]
    return [(a, b) for a in along for b in around]


def partner(a, b, k, rows, cols):
    dz, ds = STEPS[k] if k < SELF else (0, 0)
    az, bs = a + dz, b + ds
    rz = -1 if az < 0 else 1 if az >= rows else 0
    rs = -1 if bs < 0 else 1 if bs >= cols else 0
    tile = (az % rows, bs % cols)
    if rz == 0 and rs == 0:
        return (0, 0), None, tile
    return (rz, rs), side_tiles(-rz, -rs, rows, cols).index(tile), tile


def device_at(rz, rs, dom_count, sub_count):
    along = jnp.clip(lax.axis_index("dom") + rz, 0, dom_count - 1)
    around = lax.rem(lax.axis_index("sub") + rs + sub_count, sub_count)
    return along * sub_count + around


def in_range(rz, dom_count):
    at = lax.axis_index("dom") + rz
    return (at >= 0) & (at < dom_count)


def far_unroll(devices):
    return 16 if devices % 16 == 0 else 1


def pieces(value):
    first = value.astype(jnp.bfloat16).astype(jnp.float32)
    left = value - first
    second = left.astype(jnp.bfloat16).astype(jnp.float32)
    return first, second, left - second


def line_of(shape=(SUBLANES, LANES)):
    return lax.broadcasted_iota(jnp.int32, shape, 0)


def side_block(points, ones_line, norm_line, factor):
    norm = jnp.sum(points * points, axis=0, keepdims=True) * (1.0 / UNIT)
    line = line_of()
    block = jnp.where(line == norm_line, norm, jnp.where(line == ones_line, 1.0, factor * points))
    return pieces(block)


def weight_rows(first, second, third):
    rows = jnp.concatenate(
        [first, second[0:3], third[0:3], jnp.zeros((2, LANES), jnp.float32)], axis=0)
    return jnp.concatenate([rows, rows], axis=1).astype(jnp.bfloat16)


def other_tables(points):
    c1, c2, c3 = side_block(points, 4, 3, 1.0)
    table = jnp.concatenate([c1, c2, c1, c2, c3, c1], axis=0).astype(jnp.bfloat16)
    return table, weight_rows(c1, c2, c3)


def own_tables(points):
    x1, x2, x3 = side_block(points, 3, 4, -2.0 / UNIT)
    stack = jnp.concatenate(
        [x1, x1, x2, x2, x1, x3, jnp.zeros((LANES - KROWS, LANES), jnp.float32)], axis=0)
    w1, w2, w3 = side_block(points, 4, 3, 1.0)
    return stack.T[:, 0:KROWS].astype(jnp.bfloat16), weight_rows(w1, w2, w3)


def product(a, b):
    return jnp.dot(a, b, preferred_element_type=jnp.float32)


def product_turned(a, b):
    return lax.dot_general(a, b, (((1,), (1,)), ((), ())), preferred_element_type=jnp.float32)


def weighted(block):
    return block[4:5], block[0:3] + block[8:11] + block[11:14]


def member_table(seg_ref, a, b, cols):
    comp = lax.broadcasted_iota(jnp.int32, (LANES, LANES), 0)
    owner = seg_ref[a, b : b + 1, :] + (a * cols + b) * CT
    return (comp == owner).astype(jnp.float32)


def turned(row):
    return jnp.broadcast_to(row, (LANES, LANES)).T


def lane_sums(block):
    return jnp.sum(block.T, axis=0, keepdims=True)


def pack_body(dims, pos_ref, q_ref, r_ref, seg_ref, send_ref, members_ref):
    rows, cols, dom_count, sub_count = dims
    slots = max(rows, cols)
    total = jnp.zeros((SUBLANES, LANES), jnp.float32)
    one = jnp.ones((1, LANES), jnp.float32)
    for a in range(rows):
        for b in range(cols):
            at = slice(b, b + 1)
            rho = r_ref[a, at, :]
            values = jnp.concatenate(
                [pos_ref[0, a, at, :], pos_ref[1, a, at, :], pos_ref[2, a, at, :],
                 q_ref[a, at, :], rho * rho * rho, rho, one, one], axis=0)
            total = total + lax.dot_general(
                values, member_table(seg_ref, a, b, cols), (((1,), (1,)), ((), ())),
                precision=HIGHEST, preferred_element_type=jnp.float32)
    members = total[6:7]
    comp_radius = RADIUS_FACTOR * total[5:6] / members
    table = jnp.concatenate(
        [total[0:3] / members, CHARGE_UNIT * total[3:4], total[4:5],
         comp_radius * (1.0 / UNIT), (-0.25 * LOG2E * UNIT) / comp_radius,
         comp_radius * comp_radius * (1.0 / UNIT)], axis=0)
    members_ref[...] = jnp.broadcast_to(members, (SUBLANES, LANES))

    def put(d, carry):
        send_ref[d, 0:8, :] = table
        return carry

    lax.fori_loop(0, dom_count * sub_count, put, 0)
    for rz in (-1, 0, 1):
        for rs in (-1, 0, 1):
            where = device_at(rz, rs, dom_count, sub_count)

            @pl.when(in_range(rz, dom_count))
            def _(rz=rz, rs=rs, where=where):
                for slot, (a, b) in enumerate(side_tiles(rz, rs, rows, cols)[:slots]):
                    at = slice(b, b + 1)
                    for c in range(3):
                        line = 8 + c * slots + slot
                        send_ref[where, line : line + 1, :] = pos_ref[c, a, at, :]
                    line = 8 + 3 * slots + slot
                    send_ref[where, line : line + 1, :] = r_ref[a, at, :]


def mask_rows(dims, near_ref, table_ref):
    rows, cols, dom_count, sub_count = dims
    tile_of = lax.broadcasted_iota(jnp.int32, (1, LANES), 1) // CT
    for a in range(rows):
        for b in range(cols):
            t = a * cols + b
            for k in range(NEAR):
                (rz, rs), _, (pa, pb) = partner(a, b, k, rows, cols)
                where = device_at(rz, rs, dom_count, sub_count)
                struck = tile_of == pa * cols + pb
                if k < SELF:
                    struck = struck & (near_ref[a, b, k] == 1)
                kept = table_ref[where, t : t + 1, :]
                table_ref[where, t : t + 1, :] = jnp.where(struck, 0.0, kept)


def near_source(dims, rz, rs):
    rows, cols, dom_count, sub_count = dims
    return device_at(rz, rs, dom_count, sub_count)


def window_source(dims, place, recv_ref, own, base, c):
    rows, cols, _, _ = dims
    az, bs = place // (cols + 2) - 1, place % (cols + 2) - 1
    rz = -1 if az < 0 else 1 if az >= rows else 0
    rs = -1 if bs < 0 else 1 if bs >= cols else 0
    tile = (az % rows, bs % cols)
    if rz == 0 and rs == 0:
        return own(c, *tile)
    line = base + c * max(rows, cols) + side_tiles(-rz, -rs, rows, cols).index(tile)
    return recv_ref[near_source(dims, rz, rs), line : line + 1, :]


def window_place(t, k, cols):
    dz, ds = STEPS[k] if k < SELF else (0, 0)
    return (t // cols + 1 + dz) * (cols + 2) + t % cols + 1 + ds


def flagged(near_ref, t, k, cols, row):
    if k == SELF:
        return row
    return jnp.where(near_ref[t // cols, t % cols, k] == 1, row, 0.0)


def own_pair():
    shape = (LANES, LANES)
    return lax.broadcasted_iota(jnp.int32, shape, 0) == lax.broadcasted_iota(jnp.int32, shape, 1)


def over_far(devices, step, carry):
    unroll = far_unroll(devices)

    def chunk(n, carry):
        for j in range(unroll):
            carry = step(n * unroll + j, carry)
        return carry

    if devices == unroll:
        return chunk(0, carry)
    return lax.fori_loop(0, devices // unroll, chunk, carry)


def screen_body(dims, near_ref, recv_ref, pos_ref, q_ref, r_ref, born_ref, send_ref,
                own_k, own_w, win_k, win_w, win_c, win_r, far_k, far_w, far_c, far_vol):
    rows, cols, dom_count, sub_count = dims
    devices = dom_count * sub_count
    slots = max(rows, cols)
    line = line_of()

    middle = jnp.zeros((SUBLANES, LANES), jnp.float32)
    for c in range(3):
        mean = jnp.sum(pos_ref[c]) * (1.0 / (rows * cols * LANES))
        middle = jnp.where(line == c, mean, middle)

    def own(c, a, b):
        if c < 3:
            return pos_ref[c, a, b : b + 1, :]
        return r_ref[a, b : b + 1, :]

    def put(d, carry):
        far_vol[d] = jnp.broadcast_to(recv_ref[d, 4:5, :], (rows * cols, LANES))
        points = jnp.where(line < 3, recv_ref[d, 0:8, :] - middle, 0.0)
        far_c[d] = points
        far_k[d], far_w[d] = other_tables(points)
        return carry

    lax.fori_loop(0, devices, put, 0)
    mask_rows(dims, near_ref, far_vol)
    none = jnp.zeros((SUBLANES - 3, LANES), jnp.float32)
    for place in range((rows + 2) * (cols + 2)):
        x, y, z, rho = [window_source(dims, place, recv_ref, own, 8, c) for c in range(4)]
        points = jnp.concatenate([x, y, z, none], axis=0) - middle
        win_c[place] = points
        win_k[place], win_w[place] = other_tables(points)
        win_r[place, 0:1, :] = rho * rho * (1.0 / UNIT)
        win_r[place, 1:2, :] = rho * rho * rho
        az, bs = place // (cols + 2) - 1, place % (cols + 2) - 1
        if 0 <= az < rows and 0 <= bs < cols:
            own_k[az * cols + bs], own_w[az * cols + bs] = own_tables(points)

    def tile(t, carry):
        x = own_k[t]
        sums = jnp.zeros((LANES, LANES), jnp.float32)
        for k in range(NEAR):
            place = window_place(t, k, cols)
            volume = flagged(near_ref, t, k, cols, win_r[place, 1:2, :])
            if k == SELF:
                volume = jnp.where(own_pair(), 0.0, volume)
            near = product(x, win_k[place]) + win_r[place, 0:1, :]
            sums = sums + volume / (near * near)

        def far(d, sums):
            s = product(x, far_k[d])
            near = s + recv_ref[d, 7:8, :]
            volume = far_vol[d, pl.ds(t, 1), :]
            return sums + (volume * s) / ((s + SPAN / UNIT) * (near * near))

        sums = over_far(devices, far, sums)
        screening = lane_sums(sums) * (1.0 / (UNIT * UNIT))
        a, b = t // cols, t % cols
        rho = r_ref[a, pl.ds(b, 1), :]
        born_ref[a, pl.ds(b, 1), :] = rho * (1.0 + rho * screening)
        return carry

    lax.fori_loop(0, rows * cols, tile, 0)
    for rz in (-1, 0, 1):
        for rs in (-1, 0, 1):
            where = device_at(rz, rs, dom_count, sub_count)

            @pl.when(in_range(rz, dom_count))
            def _(rz=rz, rs=rs, where=where):
                for slot, (a, b) in enumerate(side_tiles(rz, rs, rows, cols)[:slots]):
                    send_ref[where, slot : slot + 1, :] = born_ref[a, b : b + 1, :]
                    line = slots + slot
                    send_ref[where, line : line + 1, :] = q_ref[a, b : b + 1, :]


def energy_body(dims, near_ref, recv_ref, halo_ref, q_ref, r_ref, born_ref,
                own_k, own_w, win_k, win_w, win_c, win_r, far_k, far_w, far_c, far_vol,
                rgrad_ref, grad_ref, send_ref,
                turned_ref, win_e, far_q, pair_f, pair_s, far_acc, win_acc):
    rows, cols, dom_count, sub_count = dims
    devices = dom_count * sub_count
    slots = max(rows, cols)
    tiles = rows * cols
    places = (rows + 2) * (cols + 2)

    def own(c, a, b):
        at = slice(b, b + 1)
        return born_ref[a, at, :] if c == 0 else q_ref[a, at, :]

    zero = jnp.zeros((LANES, LANES), jnp.float32)
    no_force = jnp.zeros((WROWS, LANES), jnp.float32)

    def put(d, carry):
        far_q[d] = jnp.broadcast_to(recv_ref[d, 3:4, :], (tiles, LANES))
        far_acc[d] = no_force
        return carry

    lax.fori_loop(0, devices, put, 0)
    mask_rows(dims, near_ref, far_q)
    for place in range(places):
        born, charge = [window_source(dims, place, halo_ref, own, 0, c) for c in range(2)]
        win_e[place, 0:1, :] = born * (1.0 / UNIT)
        win_e[place, 1:2, :] = (-0.25 * LOG2E * UNIT) / born
        win_e[place, 2:3, :] = CHARGE_UNIT * charge
        win_acc[place] = no_force
    for a in range(rows):
        for b in range(cols):
            at = slice(b, b + 1)
            for c, row in enumerate([born_ref[a, at, :], q_ref[a, at, :], r_ref[a, at, :]]):
                turned_ref[a * cols + b, c] = turned(row)

    def tile(t, carry):
        x = own_k[t]
        own_born, own_q, own_rho = [turned_ref[t, c] for c in range(3)]
        own_inv = 1.0 / own_born

        def pair(s, other_born, other_inv, charge):
            e = jnp.exp2(s * (own_inv * other_inv))
            r = lax.rsqrt(s + (own_born * other_born) * e)
            return charge * (own_q * r), (r * r) * (1.0 - 0.25 * e)

        born_near = zero
        for k in range(NEAR):
            place = window_place(t, k, cols)
            other_born, other_inv, charge = [win_e[place, c : c + 1, :] for c in range(3)]
            charge = flagged(near_ref, t, k, cols, charge)
            if k == SELF:
                charge = jnp.where(own_pair(), 0.0, charge)
            s = product(x, win_k[place])
            qr, slope = pair(s, other_born, other_inv, charge)
            f = qr * slope
            pair_f[devices + k] = f
            pair_s[devices + k] = s
            born_near = born_near + (qr - s * f)

        def far_energy(d, born_far):
            other_born, other_inv = recv_ref[d, 5:6, :], recv_ref[d, 6:7, :]
            charge = far_q[d, pl.ds(t, 1), :]
            s = product(x, far_k[d])
            qr, slope = pair(s, other_born, other_inv, charge)
            inv = 1.0 / (s + SPAN / UNIT)
            weight = s * inv
            falling = weight * slope
            pair_f[d] = qr * (falling - inv * inv)
            pair_s[d] = s
            return born_far + qr * (weight - s * falling)

        born_far = over_far(devices, far_energy, zero)
        part = own_inv * (UNIT * (0.5 * born_far + born_near))
        own_part = own_q * own_inv
        rg = jnp.sum(part, axis=1, keepdims=True) + 0.5 * (own_part * own_part)
        scale = rg * (own_rho * own_rho) * (1.0 / UNIT ** 3)

        x_twice = own_w[t]

        def force_sums(f, other_w, own_sum):
            high = f.astype(jnp.bfloat16)
            low = (f - high.astype(jnp.float32)).astype(jnp.bfloat16)
            own_sum = own_sum + product_turned(other_w, jnp.concatenate([high, low], axis=1))
            return own_sum, product(x_twice, jnp.concatenate([high, low], axis=0))

        own_sum = no_force
        for k in range(NEAR):
            place = window_place(t, k, cols)
            volume = flagged(near_ref, t, k, cols, 4.0 * win_r[place, 1:2, :])
            inv = 1.0 / (pair_s[devices + k] + win_r[place, 0:1, :])
            f = pair_f[devices + k] - (scale * volume) * (inv * inv * inv)
            if k == SELF:
                f = jnp.where(own_pair(), 0.0, f)
            own_sum, other_sum = force_sums(f, win_w[place], own_sum)
            win_acc[place] = win_acc[place] + other_sum

        def far_chain(d, own_sum):
            s = pair_s[d]
            volume = far_vol[d, pl.ds(t, 1), :]
            inv = 1.0 / (s + SPAN / UNIT)
            near = 1.0 / (s + recv_ref[d, 7:8, :])
            slope = (inv - (4.0 * s) * near) * (inv * (near * near))
            f = pair_f[d] + (scale * volume) * slope
            own_sum, other_sum = force_sums(f, far_w[d], own_sum)
            far_acc[d] = far_acc[d] + other_sum
            return own_sum

        own_sum = over_far(devices, far_chain, own_sum)
        a, b = t // cols, t % cols
        rgrad_ref[a, pl.ds(b, 1), :] = rg.T[0:1]
        total, moment = weighted(own_sum)
        grad = win_c[window_place(t, SELF, cols), 0:3, :] * total - moment
        for c in range(3):
            grad_ref[c, a, pl.ds(b, 1), :] = grad[c : c + 1]
        return carry

    lax.fori_loop(0, tiles, tile, 0)

    def send_far(d, carry):
        total, moment = weighted(far_acc[d])
        send_ref[d, 0:3, :] = far_c[d, 0:3, :] * total - moment
        return carry

    lax.fori_loop(0, devices, send_far, 0)

    def partner_grad(az, bs):
        place = (az + 1) * (cols + 2) + bs + 1
        total, moment = weighted(win_acc[place])
        return win_c[place, 0:3, :] * total - moment

    for a in range(rows):
        for b in range(cols):
            grad = partner_grad(a, b)
            for c in range(3):
                grad_ref[c, a, b : b + 1, :] = grad_ref[c, a, b : b + 1, :] + grad[c : c + 1]
    for rz in (-1, 0, 1):
        for rs in (-1, 0, 1):
            if rz == 0 and rs == 0:
                continue
            where = device_at(rz, rs, dom_count, sub_count)

            @pl.when(in_range(rz, dom_count))
            def _(rz=rz, rs=rs, where=where):
                for slot, (pa, pb) in enumerate(side_tiles(-rz, -rs, rows, cols)):
                    az = {0: pa, 1: rows, -1: -1}[rz]
                    bs = {0: pb, 1: cols, -1: -1}[rs]
                    grad = partner_grad(az, bs)
                    for c in range(3):
                        line = 3 + c * slots + slot
                        send_ref[where, line : line + 1, :] = grad[c : c + 1]


def finish_body(dims, recv_ref, grad_ref, members_ref, seg_ref, force_ref):
    rows, cols, dom_count, sub_count = dims
    slots = max(rows, cols)

    def add(d, total):
        return total + recv_ref[d, 0:3, :]

    centre_grad = lax.fori_loop(
        0, dom_count * sub_count, add, jnp.zeros((3, LANES), jnp.float32))
    per_member = centre_grad / members_ref[0:3, :]
    per_member = jnp.concatenate([per_member, jnp.zeros((5, LANES), jnp.float32)], axis=0)
    for a in range(rows):
        for b in range(cols):
            spread_out = lax.dot_general(
                per_member, member_table(seg_ref, a, b, cols), (((1,), (0,)), ((), ())),
                precision=HIGHEST, preferred_element_type=jnp.float32)
            for c in range(3):
                force_ref[c, a, b : b + 1, :] = -(
                    grad_ref[c, a, b : b + 1, :] + spread_out[c : c + 1])
    for rz in (-1, 0, 1):
        for rs in (-1, 0, 1):
            if rz == 0 and rs == 0:
                continue
            where = device_at(rz, rs, dom_count, sub_count)

            @pl.when(in_range(rz, dom_count))
            def _(rz=rz, rs=rs, where=where):
                for slot, (a, b) in enumerate(side_tiles(rz, rs, rows, cols)):
                    for c in range(3):
                        line = 3 + c * slots + slot
                        force_ref[c, a, b : b + 1, :] = (
                            force_ref[c, a, b : b + 1, :] - recv_ref[where, line : line + 1, :])


def f32(*shape):
    return jax.ShapeDtypeStruct(shape, jnp.float32)


def bf16(*shape):
    return jax.ShapeDtypeStruct(shape, jnp.bfloat16)


def local(positions, charge, radius, segment, near_tiles):
    rows, cols, width = charge.shape
    dom_count, sub_count = lax.axis_size("dom"), lax.axis_size("sub")
    dims = (rows, cols, dom_count, sub_count)
    devices = dom_count * sub_count
    tiles = rows * cols
    assert width == LANES and tiles * CT == LANES and sub_count > 2
    slots = max(rows, cols)
    places = (rows + 2) * (cols + 2)
    vmem = pltpu.MemorySpace.VMEM
    vec = (SUBLANES, LANES)

    def call(body, ins, outs, scratch=(), room=8 << 20):
        return pl.pallas_call(
            lambda *refs: body(dims, *refs),
            out_shape=outs,
            in_specs=[pl.BlockSpec(memory_space=pltpu.MemorySpace.SMEM if x is near_tiles else vmem)
                      for x in ins],
            out_specs=[pl.BlockSpec(memory_space=vmem) for _ in outs],
            scratch_shapes=list(scratch),
            compiler_params=pltpu.CompilerParams(vmem_limit_bytes=room),
            name=body.__name__,
        )(*ins)

    def exchanged(blocks):
        return lax.all_to_all(blocks, AXES, 0, 0, tiled=True)

    send, members = call(
        pack_body, (positions, charge, radius, segment),
        [f32(devices, 8 + 4 * slots, LANES), f32(*vec)])
    table = exchanged(send)
    born_radii, send, *tables = call(
        screen_body, (near_tiles, table, positions, charge, radius),
        [f32(rows, cols, LANES), f32(devices, 2 * slots, LANES),
         bf16(tiles, LANES, KROWS), bf16(tiles, WROWS, 2 * LANES),
         bf16(places, KROWS, LANES), bf16(places, WROWS, 2 * LANES),
         f32(places, *vec), f32(places, *vec),
         bf16(devices, KROWS, LANES), bf16(devices, WROWS, 2 * LANES),
         f32(devices, *vec), f32(devices, tiles, LANES)],
        room=(8 << 20) + devices * (1 << 16))
    halo = exchanged(send)
    radius_grad, grad, send = call(
        energy_body, (near_tiles, table, halo, charge, radius, born_radii, *tables),
        [f32(rows, cols, LANES), f32(3, rows, cols, LANES), f32(devices, 4 + 3 * slots, LANES)],
        [pltpu.VMEM((tiles, 3, LANES, LANES), jnp.float32),
         pltpu.VMEM((places,) + vec, jnp.float32),
         pltpu.VMEM((devices, tiles, LANES), jnp.float32),
         pltpu.VMEM((devices + NEAR, LANES, LANES), jnp.float32),
         pltpu.VMEM((devices + NEAR, LANES, LANES), jnp.float32),
         pltpu.VMEM((devices, WROWS, LANES), jnp.float32),
         pltpu.VMEM((places, WROWS, LANES), jnp.float32)],
        room=(12 << 20) + devices * (3 << 16))
    back = exchanged(send)
    forces = call(
        finish_body, (back, grad, members, segment), [f32(3, rows, cols, LANES)])[0]
    return born_radii, radius_grad, forces


def solution(mesh):
    flat = P(("groups", "dom"), "sub", None)
    stacked = P(None, ("groups", "dom"), "sub", None)
    return jax.shard_map(
        local,
        mesh=mesh,
        in_specs=(stacked, flat, flat, flat, flat),
        out_specs=(flat, flat, stacked),
        check_vma=False,
    )
```

```python
import jax
import jax.numpy as jnp
from jax import lax
from jax.experimental import pallas as pl
from jax.experimental.pallas import tpu as pltpu
from jax.sharding import PartitionSpec as P

CT = 16
LANES = 128
SUBLANES = 8
UNIT = 128.0
TOGETHER = 4
KROWS = 48
WROWS = 16
SPAN = 64.0
CHARGE_UNIT = 0.5 * UNIT ** -1.5
RADIUS_FACTOR = 1.5
LOG2E = 1.4426950408889634
LN2 = 0.6931471805599453
HIGHEST = lax.Precision.HIGHEST
AXES = ("dom", "sub")
STEPS = ((-1, -1), (-1, 0), (-1, 1), (0, -1), (0, 1), (1, -1), (1, 0), (1, 1))
SELF = len(STEPS)
NEAR = len(STEPS) + 1


def side_tiles(rz, rs, rows, cols):
    along = {0: range(rows), 1: [rows - 1], -1: [0]}[rz]
    around = {0: range(cols), 1: [cols - 1], -1: [0]}[rs]
    return [(a, b) for a in along for b in around]


def partner(a, b, k, rows, cols):
    dz, ds = STEPS[k] if k < SELF else (0, 0)
    az, bs = a + dz, b + ds
    rz = -1 if az < 0 else 1 if az >= rows else 0
    rs = -1 if bs < 0 else 1 if bs >= cols else 0
    tile = (az % rows, bs % cols)
    if rz == 0 and rs == 0:
        return (0, 0), None, tile
    return (rz, rs), side_tiles(-rz, -rs, rows, cols).index(tile), tile


def device_at(rz, rs, dom_count, sub_count):
    along = jnp.clip(lax.axis_index("dom") + rz, 0, dom_count - 1)
    around = lax.rem(lax.axis_index("sub") + rs + sub_count, sub_count)
    return along * sub_count + around


def in_range(rz, dom_count):
    at = lax.axis_index("dom") + rz
    return (at >= 0) & (at < dom_count)


def far_unroll(devices):
    return 16 if devices % 16 == 0 else 1


def pieces(value):
    first = value.astype(jnp.bfloat16).astype(jnp.float32)
    left = value - first
    second = left.astype(jnp.bfloat16).astype(jnp.float32)
    return first, second, left - second


def line_of(shape=(SUBLANES, LANES)):
    return lax.broadcasted_iota(jnp.int32, shape, 0)


def side_block(points, ones_line, norm_line, factor):
    norm = jnp.sum(points * points, axis=0, keepdims=True) * (1.0 / UNIT)
    line = line_of()
    block = jnp.where(line == norm_line, norm, jnp.where(line == ones_line, 1.0, factor * points))
    return pieces(block)


def weight_rows(first, second, third):
    rows = jnp.concatenate(
        [first, second[0:3], third[0:3], jnp.zeros((2, LANES), jnp.float32)], axis=0)
    return jnp.concatenate([rows, rows], axis=1).astype(jnp.bfloat16)


def other_tables(points):
    c1, c2, c3 = side_block(points, 4, 3, 1.0)
    table = jnp.concatenate([c1, c2, c1, c2, c3, c1], axis=0).astype(jnp.bfloat16)
    return table, weight_rows(c1, c2, c3)


def own_tables(points):
    x1, x2, x3 = side_block(points, 3, 4, -2.0 / UNIT)
    stack = jnp.concatenate(
        [x1, x1, x2, x2, x1, x3, jnp.zeros((LANES - KROWS, LANES), jnp.float32)], axis=0)
    w1, w2, w3 = side_block(points, 4, 3, 1.0)
    return stack.T[:, 0:KROWS].astype(jnp.bfloat16), weight_rows(w1, w2, w3)


def product(a, b):
    return jnp.dot(a, b, preferred_element_type=jnp.float32)


def product_turned(a, b):
    return lax.dot_general(a, b, (((1,), (1,)), ((), ())), preferred_element_type=jnp.float32)


def weighted(block):
    return block[4:5], block[0:3] + block[8:11] + block[11:14]


def member_table(seg_ref, a, b, cols):
    comp = lax.broadcasted_iota(jnp.int32, (LANES, LANES), 0)
    owner = seg_ref[a, b : b + 1, :] + (a * cols + b) * CT
    return (comp == owner).astype(jnp.float32)


def turned(row):
    return jnp.broadcast_to(row, (LANES, LANES)).T


def lane_sums(block):
    return jnp.sum(block.T, axis=0, keepdims=True)


def pack_body(dims, pos_hbm, q_hbm, r_hbm, seg_hbm, send_ref, members_ref,
              pos_ref, q_ref, r_ref, seg_ref, arrived):
    rows, cols, dom_count, sub_count = dims
    copies = [
        pltpu.make_async_copy(source, place, arrived.at[n])
        for n, (source, place) in enumerate(
            [(pos_hbm, pos_ref), (q_hbm, q_ref), (r_hbm, r_ref), (seg_hbm, seg_ref)])]
    for copy in copies:
        copy.start()
    for copy in copies:
        copy.wait()
    slots = max(rows, cols)
    total = jnp.zeros((SUBLANES, LANES), jnp.float32)
    one = jnp.ones((1, LANES), jnp.float32)
    for a in range(rows):
        for b in range(cols):
            at = slice(b, b + 1)
            rho = r_ref[a, at, :]
            values = jnp.concatenate(
                [pos_ref[0, a, at, :], pos_ref[1, a, at, :], pos_ref[2, a, at, :],
                 q_ref[a, at, :], rho * rho * rho, rho, one, one], axis=0)
            total = total + lax.dot_general(
                values, member_table(seg_ref, a, b, cols), (((1,), (1,)), ((), ())),
                precision=HIGHEST, preferred_element_type=jnp.float32)
    members = total[6:7]
    comp_radius = RADIUS_FACTOR * total[5:6] / members
    table = jnp.concatenate(
        [total[0:3] / members, CHARGE_UNIT * total[3:4], total[4:5],
         comp_radius * (1.0 / UNIT), (-0.25 * LOG2E * UNIT) / comp_radius,
         comp_radius * comp_radius * (1.0 / UNIT)], axis=0)
    members_ref[...] = jnp.broadcast_to(members, (SUBLANES, LANES))

    def put(d, carry):
        send_ref[d, 0:8, :] = table
        return carry

    lax.fori_loop(0, dom_count * sub_count, put, 0)
    for rz in (-1, 0, 1):
        for rs in (-1, 0, 1):
            where = device_at(rz, rs, dom_count, sub_count)

            @pl.when(in_range(rz, dom_count))
            def _(rz=rz, rs=rs, where=where):
                for slot, (a, b) in enumerate(side_tiles(rz, rs, rows, cols)[:slots]):
                    at = slice(b, b + 1)
                    for c in range(3):
                        line = 8 + c * slots + slot
                        send_ref[where, line : line + 1, :] = pos_ref[c, a, at, :]
                    line = 8 + 3 * slots + slot
                    send_ref[where, line : line + 1, :] = r_ref[a, at, :]


def mask_rows(dims, near_ref, tables):
    rows, cols, dom_count, sub_count = dims
    shape = (rows * cols, LANES)
    row = lax.broadcasted_iota(jnp.int32, shape, 0)
    tile_of = lax.broadcasted_iota(jnp.int32, shape, 1) // CT
    struck = {}
    for a in range(rows):
        for b in range(cols):
            for k in range(NEAR):
                rel, _, (pa, pb) = partner(a, b, k, rows, cols)
                flag = near_ref[a, b, k] if k < SELF else 1
                at = jnp.where(row == a * cols + b, tile_of - (pa * cols + pb), 1)
                hit = jnp.where(at == 0, flag, 0)
                struck[rel] = struck[rel] | hit if rel in struck else hit
    for (rz, rs), hit in struck.items():
        where = device_at(rz, rs, dom_count, sub_count)
        for table in tables:
            table[where] = jnp.where(hit == 1, 0.0, table[where])


def near_source(dims, rz, rs):
    rows, cols, dom_count, sub_count = dims
    return device_at(rz, rs, dom_count, sub_count)


def window_source(dims, place, recv_ref, own, base, c):
    rows, cols, _, _ = dims
    az, bs = place // (cols + 2) - 1, place % (cols + 2) - 1
    rz = -1 if az < 0 else 1 if az >= rows else 0
    rs = -1 if bs < 0 else 1 if bs >= cols else 0
    tile = (az % rows, bs % cols)
    if rz == 0 and rs == 0:
        return own(c, *tile)
    line = base + c * max(rows, cols) + side_tiles(-rz, -rs, rows, cols).index(tile)
    return recv_ref[near_source(dims, rz, rs), line : line + 1, :]


def window_place(t, k, cols):
    dz, ds = STEPS[k] if k < SELF else (0, 0)
    return (t // cols + 1 + dz) * (cols + 2) + t % cols + 1 + ds


def flagged(near_ref, t, k, cols, row):
    if k == SELF:
        return row
    return jnp.where(near_ref[t // cols, t % cols, k] == 1, row, 0.0)


def own_pair():
    shape = (LANES, LANES)
    return lax.broadcasted_iota(jnp.int32, shape, 0) == lax.broadcasted_iota(jnp.int32, shape, 1)


def over_far(devices, step, carry):
    unroll = far_unroll(devices)

    def chunk(n, carry):
        for j in range(unroll):
            carry = step(n * unroll + j, carry)
        return carry

    if devices == unroll:
        return chunk(0, carry)
    return lax.fori_loop(0, devices // unroll, chunk, carry)


def screen_body(dims, near_ref, recv_ref, pos_ref, q_ref, r_ref, born_out, send_ref, born_ref,
                own_k, own_w, win_k, win_w, win_c, win_r, far_k, far_w, far_c, far_vol, far_q):
    rows, cols, dom_count, sub_count = dims
    devices = dom_count * sub_count
    slots = max(rows, cols)
    line = line_of()

    middle = jnp.zeros((SUBLANES, LANES), jnp.float32)
    for c in range(3):
        mean = jnp.sum(pos_ref[c]) * (1.0 / (rows * cols * LANES))
        middle = jnp.where(line == c, mean, middle)

    def own(c, a, b):
        if c < 3:
            return pos_ref[c, a, b : b + 1, :]
        return r_ref[a, b : b + 1, :]

    def put(d, carry):
        far_q[d] = jnp.broadcast_to(recv_ref[d, 3:4, :], (rows * cols, LANES))
        far_vol[d] = jnp.broadcast_to(recv_ref[d, 4:5, :], (rows * cols, LANES))
        points = jnp.where(line < 3, recv_ref[d, 0:8, :] - middle, 0.0)
        far_c[d] = points
        far_k[d], far_w[d] = other_tables(points)
        return carry

    lax.fori_loop(0, devices, put, 0)
    mask_rows(dims, near_ref, (far_vol, far_q))
    none = jnp.zeros((SUBLANES - 3, LANES), jnp.float32)
    for place in range((rows + 2) * (cols + 2)):
        x, y, z, rho = [window_source(dims, place, recv_ref, own, 8, c) for c in range(4)]
        points = jnp.concatenate([x, y, z, none], axis=0) - middle
        win_c[place] = points
        win_k[place], win_w[place] = other_tables(points)
        win_r[place, 0:1, :] = rho * rho * (1.0 / UNIT)
        win_r[place, 1:2, :] = rho * rho * rho
        az, bs = place // (cols + 2) - 1, place % (cols + 2) - 1
        if 0 <= az < rows and 0 <= bs < cols:
            own_k[az * cols + bs], own_w[az * cols + bs] = own_tables(points)

    def tiles(n, carry):
        pair = [n * TOGETHER + i for i in range(TOGETHER)]
        x = [own_k[t] for t in pair]
        sums = []
        for i, t in enumerate(pair):
            total = jnp.zeros((LANES, LANES), jnp.float32)
            for k in range(NEAR):
                place = window_place(t, k, cols)
                volume = flagged(near_ref, t, k, cols, win_r[place, 1:2, :])
                if k == SELF:
                    volume = jnp.where(own_pair(), 0.0, volume)
                near = product(x[i], win_k[place]) + win_r[place, 0:1, :]
                total = total + volume / (near * near)
            sums.append(total)
        x_all = jnp.concatenate(x, axis=0)

        def far(d, sums):
            s_all = product(x_all, far_k[d])
            out = []
            for i, t in enumerate(pair):
                s = s_all[i * LANES : (i + 1) * LANES]
                near = s + recv_ref[d, 7:8, :]
                volume = far_vol[d, pl.ds(t, 1), :]
                out.append(sums[i] + (volume * s) / ((s + SPAN / UNIT) * (near * near)))
            return tuple(out)

        sums = over_far(devices, far, tuple(sums))
        for i, t in enumerate(pair):
            screening = lane_sums(sums[i]) * (1.0 / (UNIT * UNIT))
            a, b = t // cols, t % cols
            rho = r_ref[a, pl.ds(b, 1), :]
            born_ref[a, pl.ds(b, 1), :] = rho * (1.0 + rho * screening)
        return carry

    lax.fori_loop(0, rows * cols // TOGETHER, tiles, 0)
    born_out[...] = born_ref[...]
    for rz in (-1, 0, 1):
        for rs in (-1, 0, 1):
            where = device_at(rz, rs, dom_count, sub_count)

            @pl.when(in_range(rz, dom_count))
            def _(rz=rz, rs=rs, where=where):
                for slot, (a, b) in enumerate(side_tiles(rz, rs, rows, cols)[:slots]):
                    send_ref[where, slot : slot + 1, :] = born_ref[a, b : b + 1, :]
                    line = slots + slot
                    send_ref[where, line : line + 1, :] = q_ref[a, b : b + 1, :]


def energy_body(dims, near_ref, recv_ref, halo_ref, q_ref, r_ref, born_ref,
                own_k, own_w, win_k, win_w, win_c, win_r, far_k, far_w, far_c, far_vol, far_q,
                rgrad_ref, grad_ref, send_ref,
                turned_ref, win_e, pair_f, pair_s, far_acc, win_acc):
    rows, cols, dom_count, sub_count = dims
    together = pair_f.shape[0]
    devices = dom_count * sub_count
    slots = max(rows, cols)
    tiles = rows * cols
    places = (rows + 2) * (cols + 2)

    def own(c, a, b):
        at = slice(b, b + 1)
        return born_ref[a, at, :] if c == 0 else q_ref[a, at, :]

    zero = jnp.zeros((LANES, LANES), jnp.float32)
    no_force = jnp.zeros((WROWS, LANES), jnp.float32)

    def put(d, carry):
        far_acc[d] = no_force
        return carry

    lax.fori_loop(0, devices, put, 0)
    for place in range(places):
        born, charge = [window_source(dims, place, halo_ref, own, 0, c) for c in range(2)]
        win_e[place, 0:1, :] = born * (1.0 / UNIT)
        win_e[place, 1:2, :] = (-0.25 * LOG2E * UNIT) / born
        win_e[place, 2:3, :] = CHARGE_UNIT * charge
        win_acc[place] = no_force
    for a in range(rows):
        for b in range(cols):
            at = slice(b, b + 1)
            for c, row in enumerate([born_ref[a, at, :], q_ref[a, at, :], r_ref[a, at, :]]):
                turned_ref[a * cols + b, c] = turned(row)

    def group(n, carry):
        members = [n * together + i for i in range(together)]
        own_rows = [[turned_ref[t, c] for c in range(3)] for t in members]
        own_inv = [1.0 / rows_of[0] for rows_of in own_rows]

        def pair(i, s, other_born, other_inv, charge):
            own_born, own_q, _ = own_rows[i]
            e = jnp.exp2(s * (own_inv[i] * other_inv))
            r = lax.rsqrt(s + (own_born * other_born) * e)
            return charge * (own_q * r), (r * r) * (1.0 - 0.25 * e)

        born_near = []
        for i, t in enumerate(members):
            x, total = own_k[t], zero
            for k in range(NEAR):
                place = window_place(t, k, cols)
                other_born, other_inv, charge = [win_e[place, c : c + 1, :] for c in range(3)]
                charge = flagged(near_ref, t, k, cols, charge)
                if k == SELF:
                    charge = jnp.where(own_pair(), 0.0, charge)
                s = product(x, win_k[place])
                qr, slope = pair(i, s, other_born, other_inv, charge)
                f = qr * slope
                pair_f[i, devices + k] = f
                pair_s[i, devices + k] = s
                total = total + (qr - s * f)
            born_near.append(total)
        def far_energy(d, born_far):
            x_all = jnp.concatenate([own_k[t] for t in members], axis=0)
            other_born, other_inv = recv_ref[d, 5:6, :], recv_ref[d, 6:7, :]
            s_all = product(x_all, far_k[d])
            out = []
            for i, t in enumerate(members):
                charge = far_q[d, pl.ds(t, 1), :]
                s = s_all[i * LANES : (i + 1) * LANES]
                qr, slope = pair(i, s, other_born, other_inv, charge)
                inv = 1.0 / (s + SPAN / UNIT)
                weight = s * inv
                falling = weight * slope
                pair_f[i, d] = qr * (falling - inv * inv)
                pair_s[i, d] = s
                out.append(born_far[i] + qr * (weight - s * falling))
            return tuple(out)

        born_far = over_far(devices, far_energy, tuple([zero] * together))
        scale = []
        for i, t in enumerate(members):
            _, own_q, own_rho = own_rows[i]
            part = own_inv[i] * (UNIT * (0.5 * born_far[i] + born_near[i]))
            own_part = own_q * own_inv[i]
            rg = jnp.sum(part, axis=1, keepdims=True) + 0.5 * (own_part * own_part)
            scale.append(rg * (own_rho * own_rho) * (1.0 / UNIT ** 3))
            rgrad_ref[t // cols, pl.ds(t % cols, 1), :] = rg.T[0:1]

        def halves(f):
            high = f.astype(jnp.bfloat16)
            return high, (f - high.astype(jnp.float32)).astype(jnp.bfloat16)

        own_near = []
        for i, t in enumerate(members):
            total = no_force
            for k in range(NEAR):
                place = window_place(t, k, cols)
                volume = flagged(near_ref, t, k, cols, 4.0 * win_r[place, 1:2, :])
                inv = 1.0 / (pair_s[i, devices + k] + win_r[place, 0:1, :])
                f = pair_f[i, devices + k] - (scale[i] * volume) * (inv * inv * inv)
                if k == SELF:
                    f = jnp.where(own_pair(), 0.0, f)
                high, low = halves(f)
                total = total + product_turned(win_w[place], jnp.concatenate([high, low], axis=1))
                win_acc[place] = win_acc[place] + product(
                    own_w[t], jnp.concatenate([high, low], axis=0))
            own_near.append(total)
        x_sums = jnp.concatenate([own_w[t] for t in members], axis=1)

        def far_chain(d, own_sum):
            stack, turned_stack = [], []
            for i, t in enumerate(members):
                s = pair_s[i, d]
                volume = far_vol[d, pl.ds(t, 1), :]
                inv = 1.0 / (s + SPAN / UNIT)
                near = 1.0 / (s + recv_ref[d, 7:8, :])
                slope = (inv - (4.0 * s) * near) * (inv * (near * near))
                high, low = halves(pair_f[i, d] + (scale[i] * volume) * slope)
                stack.extend([high, low])
                turned_stack.append(jnp.concatenate([high, low], axis=1))
            far_acc[d] = far_acc[d] + product(x_sums, jnp.concatenate(stack, axis=0))
            return own_sum + product_turned(far_w[d], jnp.concatenate(turned_stack, axis=0))

        own_sum = over_far(devices, far_chain, jnp.concatenate(own_near, axis=1))
        for i, t in enumerate(members):
            total, moment = weighted(own_sum[:, i * LANES : (i + 1) * LANES])
            grad = win_c[window_place(t, SELF, cols), 0:3, :] * total - moment
            for c in range(3):
                grad_ref[c, t // cols, pl.ds(t % cols, 1), :] = grad[c : c + 1]
        return carry

    lax.fori_loop(0, tiles // together, group, 0)

    def send_far(d, carry):
        total, moment = weighted(far_acc[d])
        send_ref[d, 0:3, :] = far_c[d, 0:3, :] * total - moment
        return carry

    lax.fori_loop(0, devices, send_far, 0)

    def partner_grad(az, bs):
        place = (az + 1) * (cols + 2) + bs + 1
        total, moment = weighted(win_acc[place])
        return win_c[place, 0:3, :] * total - moment

    for a in range(rows):
        for b in range(cols):
            grad = partner_grad(a, b)
            for c in range(3):
                grad_ref[c, a, b : b + 1, :] = grad_ref[c, a, b : b + 1, :] + grad[c : c + 1]
    for rz in (-1, 0, 1):
        for rs in (-1, 0, 1):
            if rz == 0 and rs == 0:
                continue
            where = device_at(rz, rs, dom_count, sub_count)

            @pl.when(in_range(rz, dom_count))
            def _(rz=rz, rs=rs, where=where):
                for slot, (pa, pb) in enumerate(side_tiles(-rz, -rs, rows, cols)):
                    az = {0: pa, 1: rows, -1: -1}[rz]
                    bs = {0: pb, 1: cols, -1: -1}[rs]
                    grad = partner_grad(az, bs)
                    for c in range(3):
                        line = 3 + c * slots + slot
                        send_ref[where, line : line + 1, :] = grad[c : c + 1]


def finish_body(dims, recv_ref, grad_ref, members_ref, seg_ref, force_ref):
    rows, cols, dom_count, sub_count = dims
    slots = max(rows, cols)

    def add(d, total):
        return total + recv_ref[d, 0:3, :]

    centre_grad = lax.fori_loop(
        0, dom_count * sub_count, add, jnp.zeros((3, LANES), jnp.float32))
    per_member = centre_grad / members_ref[0:3, :]
    per_member = jnp.concatenate([per_member, jnp.zeros((5, LANES), jnp.float32)], axis=0)
    for a in range(rows):
        for b in range(cols):
            spread_out = lax.dot_general(
                per_member, member_table(seg_ref, a, b, cols), (((1,), (0,)), ((), ())),
                precision=HIGHEST, preferred_element_type=jnp.float32)
            for c in range(3):
                force_ref[c, a, b : b + 1, :] = -(
                    grad_ref[c, a, b : b + 1, :] + spread_out[c : c + 1])
    for rz in (-1, 0, 1):
        for rs in (-1, 0, 1):
            if rz == 0 and rs == 0:
                continue
            where = device_at(rz, rs, dom_count, sub_count)

            @pl.when(in_range(rz, dom_count))
            def _(rz=rz, rs=rs, where=where):
                for slot, (a, b) in enumerate(side_tiles(rz, rs, rows, cols)):
                    for c in range(3):
                        line = 3 + c * slots + slot
                        force_ref[c, a, b : b + 1, :] = (
                            force_ref[c, a, b : b + 1, :] - recv_ref[where, line : line + 1, :])


def f32(*shape):
    return jax.ShapeDtypeStruct(shape, jnp.float32)


def bf16(*shape):
    return jax.ShapeDtypeStruct(shape, jnp.bfloat16)


def local(positions, charge, radius, segment, near_tiles):
    rows, cols, width = charge.shape
    dom_count, sub_count = lax.axis_size("dom"), lax.axis_size("sub")
    dims = (rows, cols, dom_count, sub_count)
    devices = dom_count * sub_count
    tiles = rows * cols
    assert width == LANES and tiles * CT == LANES and sub_count > 2
    slots = max(rows, cols)
    places = (rows + 2) * (cols + 2)
    together = 2 if devices <= 64 else 1
    vmem = pltpu.MemorySpace.VMEM
    vec = (SUBLANES, LANES)

    def call(body, ins, outs, scratch=(), room=8 << 20, space=vmem):
        return pl.pallas_call(
            lambda *refs: body(dims, *refs),
            out_shape=outs,
            in_specs=[pl.BlockSpec(memory_space=pltpu.MemorySpace.SMEM if x is near_tiles else space)
                      for x in ins],
            out_specs=[pl.BlockSpec(memory_space=vmem) for _ in outs],
            scratch_shapes=list(scratch),
            compiler_params=pltpu.CompilerParams(vmem_limit_bytes=room),
            name=body.__name__,
        )(*[pltpu.with_memory_space_constraint(x, space) if space is not vmem else x for x in ins])

    def exchanged(blocks):
        return lax.all_to_all(blocks, AXES, 0, 0, tiled=True)

    send, members = call(
        pack_body, (positions, charge, radius, segment),
        [f32(devices, 8 + 4 * slots, LANES), f32(*vec)],
        [pltpu.VMEM(positions.shape, jnp.float32), pltpu.VMEM(charge.shape, jnp.float32),
         pltpu.VMEM(radius.shape, jnp.float32), pltpu.VMEM(segment.shape, jnp.int32),
         pltpu.SemaphoreType.DMA((4,))],
        space=pltpu.MemorySpace.HBM)
    table = exchanged(send)
    born_radii, send, *tables = call(
        screen_body, (near_tiles, table, positions, charge, radius),
        [f32(rows, cols, LANES), f32(devices, 2 * slots, LANES), f32(rows, cols, LANES),
         bf16(tiles, LANES, KROWS), bf16(tiles, WROWS, 2 * LANES),
         bf16(places, KROWS, LANES), bf16(places, WROWS, 2 * LANES),
         f32(places, *vec), f32(places, *vec),
         bf16(devices, KROWS, LANES), bf16(devices, WROWS, 2 * LANES),
         f32(devices, *vec), f32(devices, tiles, LANES), f32(devices, tiles, LANES)],
        room=(8 << 20) + devices * (1 << 16))
    halo = exchanged(send)
    radius_grad, grad, send = call(
        energy_body, (near_tiles, table, halo, charge, radius, *tables),
        [f32(rows, cols, LANES), f32(3, rows, cols, LANES), f32(devices, 4 + 3 * slots, LANES)],
        [pltpu.VMEM((tiles, 3, LANES, LANES), jnp.float32),
         pltpu.VMEM((places,) + vec, jnp.float32),
         pltpu.VMEM((together, devices + NEAR, LANES, LANES), jnp.float32),
         pltpu.VMEM((together, devices + NEAR, LANES, LANES), jnp.float32),
         pltpu.VMEM((devices, WROWS, LANES), jnp.float32),
         pltpu.VMEM((places, WROWS, LANES), jnp.float32)],
        room=(12 << 20) + together * devices * (3 << 16))
    back = exchanged(send)
    forces = call(
        finish_body, (back, grad, members, segment), [f32(3, rows, cols, LANES)])[0]
    return born_radii, radius_grad, forces


def solution(mesh):
    flat = P(("groups", "dom"), "sub", None)
    stacked = P(None, ("groups", "dom"), "sub", None)
    return jax.shard_map(
        local,
        mesh=mesh,
        in_specs=(stacked, flat, flat, flat, flat),
        out_specs=(flat, flat, stacked),
        check_vma=False,
    )
```

```python
import jax
import jax.numpy as jnp
from jax import lax
from jax.experimental import pallas as pl
from jax.experimental.pallas import tpu as pltpu
from jax.sharding import PartitionSpec as P

CT = 16
LANES = 128
SUBLANES = 8
UNIT = 128.0
TOGETHER = 4
KROWS = 48
WROWS = 16
SPAN = 64.0
CHARGE_UNIT = 0.5 * UNIT ** -1.5
RADIUS_FACTOR = 1.5
LOG2E = 1.4426950408889634
LN2 = 0.6931471805599453
HIGHEST = lax.Precision.HIGHEST
AXES = ("dom", "sub")
STEPS = ((-1, -1), (-1, 0), (-1, 1), (0, -1), (0, 1), (1, -1), (1, 0), (1, 1))
SELF = len(STEPS)
NEAR = len(STEPS) + 1


def side_tiles(rz, rs, rows, cols):
    along = {0: range(rows), 1: [rows - 1], -1: [0]}[rz]
    around = {0: range(cols), 1: [cols - 1], -1: [0]}[rs]
    return [(a, b) for a in along for b in around]


def partner(a, b, k, rows, cols):
    dz, ds = STEPS[k] if k < SELF else (0, 0)
    az, bs = a + dz, b + ds
    rz = -1 if az < 0 else 1 if az >= rows else 0
    rs = -1 if bs < 0 else 1 if bs >= cols else 0
    tile = (az % rows, bs % cols)
    if rz == 0 and rs == 0:
        return (0, 0), None, tile
    return (rz, rs), side_tiles(-rz, -rs, rows, cols).index(tile), tile


def device_at(rz, rs, dom_count, sub_count):
    along = jnp.clip(lax.axis_index("dom") + rz, 0, dom_count - 1)
    around = lax.rem(lax.axis_index("sub") + rs + sub_count, sub_count)
    return along * sub_count + around


def in_range(rz, dom_count):
    at = lax.axis_index("dom") + rz
    return (at >= 0) & (at < dom_count)


def far_unroll(devices):
    return 16 if devices % 16 == 0 else 1


def pieces(value):
    first = value.astype(jnp.bfloat16).astype(jnp.float32)
    left = value - first
    second = left.astype(jnp.bfloat16).astype(jnp.float32)
    return first, second, left - second


def line_of(shape=(SUBLANES, LANES)):
    return lax.broadcasted_iota(jnp.int32, shape, 0)


def side_block(points, ones_line, norm_line, factor):
    norm = jnp.sum(points * points, axis=0, keepdims=True) * (1.0 / UNIT)
    line = line_of()
    block = jnp.where(line == norm_line, norm, jnp.where(line == ones_line, 1.0, factor * points))
    return pieces(block)


def weight_rows(first, second, third):
    rows = jnp.concatenate(
        [first, second[0:3], third[0:3], jnp.zeros((2, LANES), jnp.float32)], axis=0)
    return jnp.concatenate([rows, rows], axis=1).astype(jnp.bfloat16)


def other_tables(points):
    c1, c2, c3 = side_block(points, 4, 3, 1.0)
    table = jnp.concatenate([c1, c2, c1, c2, c3, c1], axis=0).astype(jnp.bfloat16)
    return table, weight_rows(c1, c2, c3)


def own_tables(points):
    x1, x2, x3 = side_block(points, 3, 4, -2.0 / UNIT)
    stack = jnp.concatenate(
        [x1, x1, x2, x2, x1, x3, jnp.zeros((LANES - KROWS, LANES), jnp.float32)], axis=0)
    w1, w2, w3 = side_block(points, 4, 3, 1.0)
    return stack.T[:, 0:KROWS].astype(jnp.bfloat16), weight_rows(w1, w2, w3)


def product(a, b):
    return jnp.dot(a, b, preferred_element_type=jnp.float32)


def product_turned(a, b):
    return lax.dot_general(a, b, (((1,), (1,)), ((), ())), preferred_element_type=jnp.float32)


def weighted(block):
    return block[4:5], block[0:3] + block[8:11] + block[11:14]


def member_table(seg_ref, a, b, cols):
    comp = lax.broadcasted_iota(jnp.int32, (LANES, LANES), 0)
    owner = seg_ref[a, b : b + 1, :] + (a * cols + b) * CT
    return (comp == owner).astype(jnp.float32).astype(jnp.bfloat16)


def turned(row):
    return jnp.broadcast_to(row, (LANES, LANES)).T


def lane_sums(block):
    return jnp.sum(block.T, axis=0, keepdims=True)


def pack_body(dims, pos_hbm, q_hbm, r_hbm, seg_hbm, send_ref, members_ref, member_ref,
              pos_ref, q_ref, r_ref, seg_ref, arrived):
    rows, cols, dom_count, sub_count = dims
    copies = [
        pltpu.make_async_copy(source, place, arrived.at[n])
        for n, (source, place) in enumerate(
            [(pos_hbm, pos_ref), (q_hbm, q_ref), (r_hbm, r_ref), (seg_hbm, seg_ref)])]
    for copy in copies:
        copy.start()
    for copy in copies:
        copy.wait()
    slots = max(rows, cols)
    one = jnp.ones((1, LANES), jnp.float32)
    values = []
    for a in range(rows):
        for b in range(cols):
            at, t = slice(b, b + 1), a * cols + b
            rho = r_ref[a, at, :]
            member_ref[:, t * LANES : (t + 1) * LANES] = member_table(seg_ref, a, b, cols)
            block = pieces(jnp.concatenate(
                [pos_ref[0, a, at, :], pos_ref[1, a, at, :], pos_ref[2, a, at, :],
                 q_ref[a, at, :], rho * rho * rho, rho, one, one], axis=0))
            values.append(jnp.concatenate(block + (jnp.zeros_like(block[0]),), axis=0))
    sums = product_turned(jnp.concatenate(values, axis=1).astype(jnp.bfloat16), member_ref[...])
    total = sums[0:8] + sums[8:16] + sums[16:24]
    members = total[6:7]
    comp_radius = RADIUS_FACTOR * total[5:6] / members
    table = jnp.concatenate(
        [total[0:3] / members, CHARGE_UNIT * total[3:4], total[4:5],
         comp_radius * (1.0 / UNIT), (-0.25 * LOG2E * UNIT) / comp_radius,
         comp_radius * comp_radius * (1.0 / UNIT)], axis=0)
    members_ref[...] = jnp.broadcast_to(members, (SUBLANES, LANES))

    def put(d, carry):
        send_ref[d, 0:8, :] = table
        return carry

    lax.fori_loop(0, dom_count * sub_count, put, 0)
    for rz in (-1, 0, 1):
        for rs in (-1, 0, 1):
            where = device_at(rz, rs, dom_count, sub_count)

            @pl.when(in_range(rz, dom_count))
            def _(rz=rz, rs=rs, where=where):
                for slot, (a, b) in enumerate(side_tiles(rz, rs, rows, cols)[:slots]):
                    at = slice(b, b + 1)
                    for c in range(3):
                        line = 8 + c * slots + slot
                        send_ref[where, line : line + 1, :] = pos_ref[c, a, at, :]
                    line = 8 + 3 * slots + slot
                    send_ref[where, line : line + 1, :] = r_ref[a, at, :]


def mask_rows(dims, near_ref, tables):
    rows, cols, dom_count, sub_count = dims
    shape = (rows * cols, LANES)
    row = lax.broadcasted_iota(jnp.int32, shape, 0)
    tile_of = lax.broadcasted_iota(jnp.int32, shape, 1) // CT
    struck = {}
    for a in range(rows):
        for b in range(cols):
            for k in range(NEAR):
                rel, _, (pa, pb) = partner(a, b, k, rows, cols)
                flag = near_ref[a, b, k] if k < SELF else 1
                at = jnp.where(row == a * cols + b, tile_of - (pa * cols + pb), 1)
                hit = jnp.where(at == 0, flag, 0)
                struck[rel] = struck[rel] | hit if rel in struck else hit
    for (rz, rs), hit in struck.items():
        where = device_at(rz, rs, dom_count, sub_count)
        for table in tables:
            table[where] = jnp.where(hit == 1, 0.0, table[where])


def near_source(dims, rz, rs):
    rows, cols, dom_count, sub_count = dims
    return device_at(rz, rs, dom_count, sub_count)


def window_source(dims, place, recv_ref, own, base, c):
    rows, cols, _, _ = dims
    az, bs = place // (cols + 2) - 1, place % (cols + 2) - 1
    rz = -1 if az < 0 else 1 if az >= rows else 0
    rs = -1 if bs < 0 else 1 if bs >= cols else 0
    tile = (az % rows, bs % cols)
    if rz == 0 and rs == 0:
        return own(c, *tile)
    line = base + c * max(rows, cols) + side_tiles(-rz, -rs, rows, cols).index(tile)
    return recv_ref[near_source(dims, rz, rs), line : line + 1, :]


def window_place(t, k, cols):
    dz, ds = STEPS[k] if k < SELF else (0, 0)
    return (t // cols + 1 + dz) * (cols + 2) + t % cols + 1 + ds


def flagged(near_ref, t, k, cols, row):
    if k == SELF:
        return row
    return jnp.where(near_ref[t // cols, t % cols, k] == 1, row, 0.0)


def own_pair():
    shape = (LANES, LANES)
    return lax.broadcasted_iota(jnp.int32, shape, 0) == lax.broadcasted_iota(jnp.int32, shape, 1)


def over_far(devices, step, carry):
    unroll = far_unroll(devices)

    def chunk(n, carry):
        for j in range(unroll):
            carry = step(n * unroll + j, carry)
        return carry

    if devices == unroll:
        return chunk(0, carry)
    return lax.fori_loop(0, devices // unroll, chunk, carry)


def screen_body(dims, near_ref, recv_ref, pos_ref, q_ref, r_ref, send_ref, born_ref,
                own_k, own_w, win_k, win_w, win_c, win_r, far_k, far_w, far_c, far_vol, far_q):
    rows, cols, dom_count, sub_count = dims
    devices = dom_count * sub_count
    slots = max(rows, cols)
    line = line_of()

    middle = jnp.zeros((SUBLANES, LANES), jnp.float32)
    for c in range(3):
        mean = jnp.sum(pos_ref[c]) * (1.0 / (rows * cols * LANES))
        middle = jnp.where(line == c, mean, middle)

    def own(c, a, b):
        if c < 3:
            return pos_ref[c, a, b : b + 1, :]
        return r_ref[a, b : b + 1, :]

    def put(d, carry):
        far_q[d] = jnp.broadcast_to(recv_ref[d, 3:4, :], (rows * cols, LANES))
        far_vol[d] = jnp.broadcast_to(recv_ref[d, 4:5, :], (rows * cols, LANES))
        points = jnp.where(line < 3, recv_ref[d, 0:8, :] - middle, 0.0)
        far_c[d] = points
        far_k[d], far_w[d] = other_tables(points)
        return carry

    lax.fori_loop(0, devices, put, 0)
    mask_rows(dims, near_ref, (far_vol, far_q))
    none = jnp.zeros((SUBLANES - 3, LANES), jnp.float32)
    for place in range((rows + 2) * (cols + 2)):
        x, y, z, rho = [window_source(dims, place, recv_ref, own, 8, c) for c in range(4)]
        points = jnp.concatenate([x, y, z, none], axis=0) - middle
        win_c[place] = points
        win_k[place], win_w[place] = other_tables(points)
        win_r[place, 0:1, :] = rho * rho * (1.0 / UNIT)
        win_r[place, 1:2, :] = rho * rho * rho
        az, bs = place // (cols + 2) - 1, place % (cols + 2) - 1
        if 0 <= az < rows and 0 <= bs < cols:
            own_k[az * cols + bs], own_w[az * cols + bs] = own_tables(points)

    def tiles(n, carry):
        pair = [n * TOGETHER + i for i in range(TOGETHER)]
        x = [own_k[t] for t in pair]
        sums = []
        for i, t in enumerate(pair):
            total = jnp.zeros((LANES, LANES), jnp.float32)
            for k in range(NEAR):
                place = window_place(t, k, cols)
                volume = flagged(near_ref, t, k, cols, win_r[place, 1:2, :])
                if k == SELF:
                    volume = jnp.where(own_pair(), 0.0, volume)
                near = product(x[i], win_k[place]) + win_r[place, 0:1, :]
                total = total + volume / (near * near)
            sums.append(total)
        x_all = jnp.concatenate(x, axis=0)

        def far(d, sums):
            s_all = product(x_all, far_k[d])
            out = []
            for i, t in enumerate(pair):
                s = s_all[i * LANES : (i + 1) * LANES]
                near = s + recv_ref[d, 7:8, :]
                volume = far_vol[d, pl.ds(t, 1), :]
                out.append(sums[i] + (volume * s) / ((s + SPAN / UNIT) * (near * near)))
            return tuple(out)

        sums = over_far(devices, far, tuple(sums))
        for i, t in enumerate(pair):
            screening = lane_sums(sums[i]) * (1.0 / (UNIT * UNIT))
            a, b = t // cols, t % cols
            rho = r_ref[a, pl.ds(b, 1), :]
            born_ref[a, pl.ds(b, 1), :] = rho * (1.0 + rho * screening)
        return carry

    lax.fori_loop(0, rows * cols // TOGETHER, tiles, 0)
    for rz in (-1, 0, 1):
        for rs in (-1, 0, 1):
            where = device_at(rz, rs, dom_count, sub_count)

            @pl.when(in_range(rz, dom_count))
            def _(rz=rz, rs=rs, where=where):
                for slot, (a, b) in enumerate(side_tiles(rz, rs, rows, cols)[:slots]):
                    send_ref[where, slot : slot + 1, :] = born_ref[a, b : b + 1, :]
                    line = slots + slot
                    send_ref[where, line : line + 1, :] = q_ref[a, b : b + 1, :]


def energy_body(dims, near_ref, recv_ref, halo_ref, q_ref, r_ref, born_ref,
                own_k, own_w, win_k, win_w, win_c, win_r, far_k, far_w, far_c, far_vol, far_q,
                rgrad_ref, grad_ref, send_ref,
                turned_ref, win_e, pair_f, pair_s, far_acc, win_acc):
    rows, cols, dom_count, sub_count = dims
    together = pair_f.shape[0]
    devices = dom_count * sub_count
    slots = max(rows, cols)
    tiles = rows * cols
    places = (rows + 2) * (cols + 2)

    def own(c, a, b):
        at = slice(b, b + 1)
        return born_ref[a, at, :] if c == 0 else q_ref[a, at, :]

    zero = jnp.zeros((LANES, LANES), jnp.float32)
    no_force = jnp.zeros((WROWS, LANES), jnp.float32)

    def put(d, carry):
        far_acc[d] = no_force
        return carry

    lax.fori_loop(0, devices, put, 0)
    for place in range(places):
        born, charge = [window_source(dims, place, halo_ref, own, 0, c) for c in range(2)]
        win_e[place, 0:1, :] = born * (1.0 / UNIT)
        win_e[place, 1:2, :] = (-0.25 * LOG2E * UNIT) / born
        win_e[place, 2:3, :] = CHARGE_UNIT * charge
        win_acc[place] = no_force
    for a in range(rows):
        for b in range(cols):
            at = slice(b, b + 1)
            for c, row in enumerate([born_ref[a, at, :], q_ref[a, at, :], r_ref[a, at, :]]):
                turned_ref[a * cols + b, c] = turned(row)

    def group(n, carry):
        members = [n * together + i for i in range(together)]
        own_rows = [[turned_ref[t, c] for c in range(3)] for t in members]
        own_inv = [1.0 / rows_of[0] for rows_of in own_rows]

        def pair(i, s, other_born, other_inv, charge):
            own_born, own_q, _ = own_rows[i]
            e = jnp.exp2(s * (own_inv[i] * other_inv))
            r = lax.rsqrt(s + (own_born * other_born) * e)
            return charge * (own_q * r), (r * r) * (1.0 - 0.25 * e)

        born_near = []
        for i, t in enumerate(members):
            x, total = own_k[t], zero
            for k in range(NEAR):
                place = window_place(t, k, cols)
                other_born, other_inv, charge = [win_e[place, c : c + 1, :] for c in range(3)]
                charge = flagged(near_ref, t, k, cols, charge)
                if k == SELF:
                    charge = jnp.where(own_pair(), 0.0, charge)
                s = product(x, win_k[place])
                qr, slope = pair(i, s, other_born, other_inv, charge)
                f = qr * slope
                pair_f[i, devices + k] = f
                pair_s[i, devices + k] = s
                total = total + (qr - s * f)
            born_near.append(total)
        def far_energy(d, born_far):
            x_all = jnp.concatenate([own_k[t] for t in members], axis=0)
            other_born, other_inv = recv_ref[d, 5:6, :], recv_ref[d, 6:7, :]
            s_all = product(x_all, far_k[d])
            out = []
            for i, t in enumerate(members):
                charge = far_q[d, pl.ds(t, 1), :]
                s = s_all[i * LANES : (i + 1) * LANES]
                qr, slope = pair(i, s, other_born, other_inv, charge)
                inv = 1.0 / (s + SPAN / UNIT)
                weight = s * inv
                falling = weight * slope
                pair_f[i, d] = qr * (falling - inv * inv)
                pair_s[i, d] = s
                out.append(born_far[i] + qr * (weight - s * falling))
            return tuple(out)

        born_far = over_far(devices, far_energy, tuple([zero] * together))
        scale = []
        for i, t in enumerate(members):
            _, own_q, own_rho = own_rows[i]
            part = own_inv[i] * (UNIT * (0.5 * born_far[i] + born_near[i]))
            own_part = own_q * own_inv[i]
            rg = jnp.sum(part, axis=1, keepdims=True) + 0.5 * (own_part * own_part)
            scale.append(rg * (own_rho * own_rho) * (1.0 / UNIT ** 3))
            rgrad_ref[t // cols, pl.ds(t % cols, 1), :] = rg.T[0:1]

        def halves(f):
            high = f.astype(jnp.bfloat16)
            return high, (f - high.astype(jnp.float32)).astype(jnp.bfloat16)

        own_near = []
        for i, t in enumerate(members):
            total = no_force
            for k in range(NEAR):
                place = window_place(t, k, cols)
                volume = flagged(near_ref, t, k, cols, 4.0 * win_r[place, 1:2, :])
                inv = 1.0 / (pair_s[i, devices + k] + win_r[place, 0:1, :])
                f = pair_f[i, devices + k] - (scale[i] * volume) * (inv * inv * inv)
                if k == SELF:
                    f = jnp.where(own_pair(), 0.0, f)
                high, low = halves(f)
                total = total + product_turned(win_w[place], jnp.concatenate([high, low], axis=1))
                win_acc[place] = win_acc[place] + product(
                    own_w[t], jnp.concatenate([high, low], axis=0))
            own_near.append(total)
        x_sums = jnp.concatenate([own_w[t] for t in members], axis=1)

        def far_chain(d, own_sum):
            stack, turned_stack = [], []
            for i, t in enumerate(members):
                s = pair_s[i, d]
                volume = far_vol[d, pl.ds(t, 1), :]
                inv = 1.0 / (s + SPAN / UNIT)
                near = 1.0 / (s + recv_ref[d, 7:8, :])
                slope = (inv - (4.0 * s) * near) * (inv * (near * near))
                high, low = halves(pair_f[i, d] + (scale[i] * volume) * slope)
                stack.extend([high, low])
                turned_stack.append(jnp.concatenate([high, low], axis=1))
            far_acc[d] = far_acc[d] + product(x_sums, jnp.concatenate(stack, axis=0))
            return own_sum + product_turned(far_w[d], jnp.concatenate(turned_stack, axis=0))

        own_sum = over_far(devices, far_chain, jnp.concatenate(own_near, axis=1))
        for i, t in enumerate(members):
            total, moment = weighted(own_sum[:, i * LANES : (i + 1) * LANES])
            grad = win_c[window_place(t, SELF, cols), 0:3, :] * total - moment
            for c in range(3):
                grad_ref[c, t // cols, pl.ds(t % cols, 1), :] = grad[c : c + 1]
        return carry

    lax.fori_loop(0, tiles // together, group, 0)

    def send_far(d, carry):
        total, moment = weighted(far_acc[d])
        send_ref[d, 0:3, :] = far_c[d, 0:3, :] * total - moment
        return carry

    lax.fori_loop(0, devices, send_far, 0)

    def partner_grad(az, bs):
        place = (az + 1) * (cols + 2) + bs + 1
        total, moment = weighted(win_acc[place])
        return win_c[place, 0:3, :] * total - moment

    for a in range(rows):
        for b in range(cols):
            grad = partner_grad(a, b)
            for c in range(3):
                grad_ref[c, a, b : b + 1, :] = grad_ref[c, a, b : b + 1, :] + grad[c : c + 1]
    for rz in (-1, 0, 1):
        for rs in (-1, 0, 1):
            if rz == 0 and rs == 0:
                continue
            where = device_at(rz, rs, dom_count, sub_count)

            @pl.when(in_range(rz, dom_count))
            def _(rz=rz, rs=rs, where=where):
                for slot, (pa, pb) in enumerate(side_tiles(-rz, -rs, rows, cols)):
                    az = {0: pa, 1: rows, -1: -1}[rz]
                    bs = {0: pb, 1: cols, -1: -1}[rs]
                    grad = partner_grad(az, bs)
                    for c in range(3):
                        line = 3 + c * slots + slot
                        send_ref[where, line : line + 1, :] = grad[c : c + 1]


def finish_body(dims, recv_ref, grad_ref, members_ref, member_ref, born_ref, rgrad_ref,
                force_ref, born_out, rgrad_out):
    rows, cols, dom_count, sub_count = dims
    slots = max(rows, cols)

    def add(d, total):
        return total + recv_ref[d, 0:3, :]

    centre_grad = lax.fori_loop(
        0, dom_count * sub_count, add, jnp.zeros((3, LANES), jnp.float32))
    per_member = centre_grad / members_ref[0:3, :]
    born_out[...] = born_ref[...]
    rgrad_out[...] = rgrad_ref[...]
    block = pieces(jnp.concatenate([per_member, jnp.zeros((5, LANES), jnp.float32)], axis=0))
    block = jnp.concatenate(block + (jnp.zeros_like(block[0]),), axis=0).astype(jnp.bfloat16)
    back = product(block, member_ref[...])
    back = back[0:8] + back[8:16] + back[16:24]
    for a in range(rows):
        for b in range(cols):
            t = a * cols + b
            spread_out = back[:, t * LANES : (t + 1) * LANES]
            for c in range(3):
                force_ref[c, a, b : b + 1, :] = -(
                    grad_ref[c, a, b : b + 1, :] + spread_out[c : c + 1])
    for rz in (-1, 0, 1):
        for rs in (-1, 0, 1):
            if rz == 0 and rs == 0:
                continue
            where = device_at(rz, rs, dom_count, sub_count)

            @pl.when(in_range(rz, dom_count))
            def _(rz=rz, rs=rs, where=where):
                for slot, (a, b) in enumerate(side_tiles(rz, rs, rows, cols)):
                    for c in range(3):
                        line = 3 + c * slots + slot
                        force_ref[c, a, b : b + 1, :] = (
                            force_ref[c, a, b : b + 1, :] - recv_ref[where, line : line + 1, :])


def f32(*shape):
    return jax.ShapeDtypeStruct(shape, jnp.float32)


def bf16(*shape):
    return jax.ShapeDtypeStruct(shape, jnp.bfloat16)


def local(positions, charge, radius, segment, near_tiles):
    rows, cols, width = charge.shape
    dom_count, sub_count = lax.axis_size("dom"), lax.axis_size("sub")
    dims = (rows, cols, dom_count, sub_count)
    devices = dom_count * sub_count
    tiles = rows * cols
    assert width == LANES and tiles * CT == LANES and sub_count > 2
    slots = max(rows, cols)
    places = (rows + 2) * (cols + 2)
    together = 2 if devices <= 64 else 1
    vmem = pltpu.MemorySpace.VMEM
    vec = (SUBLANES, LANES)

    def call(body, ins, outs, scratch=(), room=8 << 20, space=vmem):
        return pl.pallas_call(
            lambda *refs: body(dims, *refs),
            out_shape=outs,
            in_specs=[pl.BlockSpec(memory_space=pltpu.MemorySpace.SMEM if x is near_tiles else space)
                      for x in ins],
            out_specs=[pl.BlockSpec(memory_space=vmem) for _ in outs],
            scratch_shapes=list(scratch),
            compiler_params=pltpu.CompilerParams(vmem_limit_bytes=room),
            name=body.__name__,
        )(*[pltpu.with_memory_space_constraint(x, space) if space is not vmem else x for x in ins])

    def exchanged(blocks):
        return lax.all_to_all(blocks, AXES, 0, 0, tiled=True)

    send, members, member = call(
        pack_body, (positions, charge, radius, segment),
        [f32(devices, 8 + 4 * slots, LANES), f32(*vec), bf16(LANES, tiles * LANES)],
        [pltpu.VMEM(positions.shape, jnp.float32), pltpu.VMEM(charge.shape, jnp.float32),
         pltpu.VMEM(radius.shape, jnp.float32), pltpu.VMEM(segment.shape, jnp.int32),
         pltpu.SemaphoreType.DMA((4,))],
        space=pltpu.MemorySpace.HBM)
    table = exchanged(send)
    send, born, *tables = call(
        screen_body, (near_tiles, table, positions, charge, radius),
        [f32(devices, 2 * slots, LANES), f32(rows, cols, LANES),
         bf16(tiles, LANES, KROWS), bf16(tiles, WROWS, 2 * LANES),
         bf16(places, KROWS, LANES), bf16(places, WROWS, 2 * LANES),
         f32(places, *vec), f32(places, *vec),
         bf16(devices, KROWS, LANES), bf16(devices, WROWS, 2 * LANES),
         f32(devices, *vec), f32(devices, tiles, LANES), f32(devices, tiles, LANES)],
        room=(8 << 20) + devices * (1 << 16))
    halo = exchanged(send)
    radius_grad, grad, send = call(
        energy_body, (near_tiles, table, halo, charge, radius, born, *tables),
        [f32(rows, cols, LANES), f32(3, rows, cols, LANES), f32(devices, 4 + 3 * slots, LANES)],
        [pltpu.VMEM((tiles, 3, LANES, LANES), jnp.float32),
         pltpu.VMEM((places,) + vec, jnp.float32),
         pltpu.VMEM((together, devices + NEAR, LANES, LANES), jnp.float32),
         pltpu.VMEM((together, devices + NEAR, LANES, LANES), jnp.float32),
         pltpu.VMEM((devices, WROWS, LANES), jnp.float32),
         pltpu.VMEM((places, WROWS, LANES), jnp.float32)],
        room=(12 << 20) + together * devices * (3 << 16))
    back = exchanged(send)
    shape = f32(rows, cols, LANES)
    forces, born_radii, radius_grad = call(
        finish_body, (back, grad, members, member, born, radius_grad),
        [f32(3, rows, cols, LANES), shape, shape])
    return born_radii, radius_grad, forces


def solution(mesh):
    flat = P(("groups", "dom"), "sub", None)
    stacked = P(None, ("groups", "dom"), "sub", None)
    return jax.shard_map(
        local,
        mesh=mesh,
        in_specs=(stacked, flat, flat, flat, flat),
        out_specs=(flat, flat, stacked),
        check_vma=False,
    )
```

```python
import jax
import jax.numpy as jnp
from jax import lax
from jax.experimental import pallas as pl
from jax.experimental.pallas import tpu as pltpu
from jax.sharding import PartitionSpec as P

CT = 16
LANES = 128
SUBLANES = 8
UNIT = 128.0
TOGETHER = 4
KROWS = 48
WROWS = 16
SPAN = 64.0
CHARGE_UNIT = 0.5 * UNIT ** -1.5
RADIUS_FACTOR = 1.5
LOG2E = 1.4426950408889634
LN2 = 0.6931471805599453
HIGHEST = lax.Precision.HIGHEST
AXES = ("dom", "sub")
STEPS = ((-1, -1), (-1, 0), (-1, 1), (0, -1), (0, 1), (1, -1), (1, 0), (1, 1))
SELF = len(STEPS)
NEAR = len(STEPS) + 1


def side_tiles(rz, rs, rows, cols):
    along = {0: range(rows), 1: [rows - 1], -1: [0]}[rz]
    around = {0: range(cols), 1: [cols - 1], -1: [0]}[rs]
    return [(a, b) for a in along for b in around]


def partner(a, b, k, rows, cols):
    dz, ds = STEPS[k] if k < SELF else (0, 0)
    az, bs = a + dz, b + ds
    rz = -1 if az < 0 else 1 if az >= rows else 0
    rs = -1 if bs < 0 else 1 if bs >= cols else 0
    tile = (az % rows, bs % cols)
    if rz == 0 and rs == 0:
        return (0, 0), None, tile
    return (rz, rs), side_tiles(-rz, -rs, rows, cols).index(tile), tile


def device_at(rz, rs, dom_count, sub_count):
    along = jnp.clip(lax.axis_index("dom") + rz, 0, dom_count - 1)
    around = lax.rem(lax.axis_index("sub") + rs + sub_count, sub_count)
    return along * sub_count + around


def in_range(rz, dom_count):
    at = lax.axis_index("dom") + rz
    return (at >= 0) & (at < dom_count)


def far_unroll(pairs):
    return 8 if pairs % 8 == 0 else 1


def pieces(value):
    first = value.astype(jnp.bfloat16).astype(jnp.float32)
    left = value - first
    second = left.astype(jnp.bfloat16).astype(jnp.float32)
    return first, second, left - second


def line_of(shape=(SUBLANES, LANES)):
    return lax.broadcasted_iota(jnp.int32, shape, 0)


def side_block(points, ones_line, norm_line, factor):
    norm = jnp.sum(points * points, axis=0, keepdims=True) * (1.0 / UNIT)
    line = line_of()
    block = jnp.where(line == norm_line, norm, jnp.where(line == ones_line, 1.0, factor * points))
    return pieces(block)


def weight_rows(first, second, third):
    rows = jnp.concatenate(
        [first, second[0:3], third[0:3], jnp.zeros((2, LANES), jnp.float32)], axis=0)
    return jnp.concatenate([rows, rows], axis=1).astype(jnp.bfloat16)


def other_tables(points):
    c1, c2, c3 = side_block(points, 4, 3, 1.0)
    table = jnp.concatenate([c1, c2, c1, c2, c3, c1], axis=0).astype(jnp.bfloat16)
    return table, weight_rows(c1, c2, c3)


def own_tables(points):
    x1, x2, x3 = side_block(points, 3, 4, -2.0 / UNIT)
    stack = jnp.concatenate(
        [x1, x1, x2, x2, x1, x3, jnp.zeros((LANES - KROWS, LANES), jnp.float32)], axis=0)
    w1, w2, w3 = side_block(points, 4, 3, 1.0)
    return stack.T[:, 0:KROWS].astype(jnp.bfloat16), weight_rows(w1, w2, w3)


def product(a, b):
    return jnp.dot(a, b, preferred_element_type=jnp.float32)


def product_turned(a, b):
    return lax.dot_general(a, b, (((1,), (1,)), ((), ())), preferred_element_type=jnp.float32)


def weighted(block):
    return block[4:5], block[0:3] + block[8:11] + block[11:14]


def member_table(seg_ref, a, b, cols):
    comp = lax.broadcasted_iota(jnp.int32, (LANES, LANES), 0)
    owner = seg_ref[a, b : b + 1, :] + (a * cols + b) * CT
    return (comp == owner).astype(jnp.float32).astype(jnp.bfloat16)


def turned(row):
    return jnp.broadcast_to(row, (LANES, LANES)).T


def lane_sums(block):
    return jnp.sum(block.T, axis=0, keepdims=True)


def pack_body(dims, pos_hbm, q_hbm, r_hbm, seg_hbm, send_ref, members_ref, member_ref,
              pos_ref, q_ref, r_ref, seg_ref, arrived):
    rows, cols, dom_count, sub_count = dims
    copies = [
        pltpu.make_async_copy(source, place, arrived.at[n])
        for n, (source, place) in enumerate(
            [(pos_hbm, pos_ref), (q_hbm, q_ref), (r_hbm, r_ref), (seg_hbm, seg_ref)])]
    for copy in copies:
        copy.start()
    for copy in copies:
        copy.wait()
    slots = max(rows, cols)
    one = jnp.ones((1, LANES), jnp.float32)
    values = []
    for a in range(rows):
        for b in range(cols):
            at, t = slice(b, b + 1), a * cols + b
            rho = r_ref[a, at, :]
            member_ref[:, t * LANES : (t + 1) * LANES] = member_table(seg_ref, a, b, cols)
            block = pieces(jnp.concatenate(
                [pos_ref[0, a, at, :], pos_ref[1, a, at, :], pos_ref[2, a, at, :],
                 q_ref[a, at, :], rho * rho * rho, rho, one, one], axis=0))
            values.append(jnp.concatenate(block + (jnp.zeros_like(block[0]),), axis=0))
    sums = product_turned(jnp.concatenate(values, axis=1).astype(jnp.bfloat16), member_ref[...])
    total = sums[0:8] + sums[8:16] + sums[16:24]
    members = total[6:7]
    comp_radius = RADIUS_FACTOR * total[5:6] / members
    table = jnp.concatenate(
        [total[0:3] / members, CHARGE_UNIT * total[3:4], total[4:5],
         comp_radius * (1.0 / UNIT), (-0.25 * LOG2E * UNIT) / comp_radius,
         comp_radius * comp_radius * (1.0 / UNIT)], axis=0)
    members_ref[...] = jnp.broadcast_to(members, (SUBLANES, LANES))

    def put(d, carry):
        send_ref[d, 0:8, :] = table
        return carry

    lax.fori_loop(0, dom_count * sub_count, put, 0)
    for rz in (-1, 0, 1):
        for rs in (-1, 0, 1):
            where = device_at(rz, rs, dom_count, sub_count)

            @pl.when(in_range(rz, dom_count))
            def _(rz=rz, rs=rs, where=where):
                for slot, (a, b) in enumerate(side_tiles(rz, rs, rows, cols)[:slots]):
                    at = slice(b, b + 1)
                    for c in range(3):
                        line = 8 + c * slots + slot
                        send_ref[where, line : line + 1, :] = pos_ref[c, a, at, :]
                    line = 8 + 3 * slots + slot
                    send_ref[where, line : line + 1, :] = r_ref[a, at, :]


def mask_rows(dims, near_ref, tables):
    rows, cols, dom_count, sub_count = dims
    shape = (rows * cols, LANES)
    row = lax.broadcasted_iota(jnp.int32, shape, 0)
    tile_of = lax.broadcasted_iota(jnp.int32, shape, 1) // CT
    struck = {}
    for a in range(rows):
        for b in range(cols):
            for k in range(NEAR):
                rel, _, (pa, pb) = partner(a, b, k, rows, cols)
                flag = near_ref[a, b, k] if k < SELF else 1
                at = jnp.where(row == a * cols + b, tile_of - (pa * cols + pb), 1)
                hit = jnp.where(at == 0, flag, 0)
                struck[rel] = struck[rel] | hit if rel in struck else hit
    for (rz, rs), hit in struck.items():
        where = device_at(rz, rs, dom_count, sub_count)
        for table in tables:
            table[where] = jnp.where(hit == 1, 0.0, table[where])


def near_source(dims, rz, rs):
    rows, cols, dom_count, sub_count = dims
    return device_at(rz, rs, dom_count, sub_count)


def window_source(dims, place, recv_ref, own, base, c):
    rows, cols, _, _ = dims
    az, bs = place // (cols + 2) - 1, place % (cols + 2) - 1
    rz = -1 if az < 0 else 1 if az >= rows else 0
    rs = -1 if bs < 0 else 1 if bs >= cols else 0
    tile = (az % rows, bs % cols)
    if rz == 0 and rs == 0:
        return own(c, *tile)
    line = base + c * max(rows, cols) + side_tiles(-rz, -rs, rows, cols).index(tile)
    return recv_ref[near_source(dims, rz, rs), line : line + 1, :]


def window_place(t, k, cols):
    dz, ds = STEPS[k] if k < SELF else (0, 0)
    return (t // cols + 1 + dz) * (cols + 2) + t % cols + 1 + ds


def flagged(near_ref, t, k, cols, row):
    if k == SELF:
        return row
    return jnp.where(near_ref[t // cols, t % cols, k] == 1, row, 0.0)


def own_pair():
    shape = (LANES, LANES)
    return lax.broadcasted_iota(jnp.int32, shape, 0) == lax.broadcasted_iota(jnp.int32, shape, 1)


def quarter_of(block, i, half):
    return block[i * LANES : (i + 1) * LANES, half * LANES : (half + 1) * LANES]


def over_far(pairs, begin, end, carry):
    unroll = far_unroll(pairs)

    def chunk(n, carry):
        begun = begin(n * unroll)
        for j in range(unroll):
            ahead = begin(n * unroll + j + 1) if j + 1 < unroll else None
            carry = end(n * unroll + j, begun, carry)
            begun = ahead
        return carry

    if pairs == unroll:
        return chunk(0, carry)
    return lax.fori_loop(0, pairs // unroll, chunk, carry)


def screen_body(dims, near_ref, recv_ref, pos_ref, q_ref, r_ref, send_ref, born_ref,
                own_k, own_w, win_k, win_w, win_c, win_r, far_k, far_w, far_c, far_vol, far_q):
    rows, cols, dom_count, sub_count = dims
    devices = dom_count * sub_count
    slots = max(rows, cols)
    line = line_of()

    middle = jnp.zeros((SUBLANES, LANES), jnp.float32)
    for c in range(3):
        mean = jnp.sum(pos_ref[c]) * (1.0 / (rows * cols * LANES))
        middle = jnp.where(line == c, mean, middle)

    def own(c, a, b):
        if c < 3:
            return pos_ref[c, a, b : b + 1, :]
        return r_ref[a, b : b + 1, :]

    def put(p, carry):
        for half in range(2):
            d = 2 * p + half
            far_q[d] = jnp.broadcast_to(recv_ref[d, 3:4, :], (rows * cols, LANES))
            far_vol[d] = jnp.broadcast_to(recv_ref[d, 4:5, :], (rows * cols, LANES))
            points = jnp.where(line < 3, recv_ref[d, 0:8, :] - middle, 0.0)
            far_c[d] = points
            table, weights = other_tables(points)
            far_k[p, :, half * LANES : (half + 1) * LANES] = table
            far_w[p, :, 2 * half * LANES : 2 * (half + 1) * LANES] = weights
        return carry

    lax.fori_loop(0, devices // 2, put, 0)
    mask_rows(dims, near_ref, (far_vol, far_q))
    none = jnp.zeros((SUBLANES - 3, LANES), jnp.float32)
    for place in range((rows + 2) * (cols + 2)):
        x, y, z, rho = [window_source(dims, place, recv_ref, own, 8, c) for c in range(4)]
        points = jnp.concatenate([x, y, z, none], axis=0) - middle
        win_c[place] = points
        win_k[place], win_w[place] = other_tables(points)
        win_r[place, 0:1, :] = rho * rho * (1.0 / UNIT)
        win_r[place, 1:2, :] = rho * rho * rho
        az, bs = place // (cols + 2) - 1, place % (cols + 2) - 1
        if 0 <= az < rows and 0 <= bs < cols:
            own_k[az * cols + bs], own_w[az * cols + bs] = own_tables(points)

    def tiles(n, carry):
        pair = [n * TOGETHER + i for i in range(TOGETHER)]
        x = [own_k[t] for t in pair]
        sums = []
        for i, t in enumerate(pair):
            total = jnp.zeros((LANES, LANES), jnp.float32)
            for k in range(NEAR):
                place = window_place(t, k, cols)
                volume = flagged(near_ref, t, k, cols, win_r[place, 1:2, :])
                if k == SELF:
                    volume = jnp.where(own_pair(), 0.0, volume)
                near = product(x[i], win_k[place]) + win_r[place, 0:1, :]
                total = total + volume / (near * near)
            sums.append(total)
        x_all = jnp.concatenate(x, axis=0)

        def far_square(p):
            return product(x_all, far_k[p])

        def far(p, s_all, sums):
            out = list(sums)
            for half in range(2):
                d = 2 * p + half
                for i, t in enumerate(pair):
                    s = quarter_of(s_all, i, half)
                    near = s + recv_ref[d, 7:8, :]
                    volume = far_vol[d, pl.ds(t, 1), :]
                    out[i] = out[i] + (volume * s) / ((s + SPAN / UNIT) * (near * near))
            return tuple(out)

        sums = over_far(devices // 2, far_square, far, tuple(sums))
        for i, t in enumerate(pair):
            screening = lane_sums(sums[i]) * (1.0 / (UNIT * UNIT))
            a, b = t // cols, t % cols
            rho = r_ref[a, pl.ds(b, 1), :]
            born_ref[a, pl.ds(b, 1), :] = rho * (1.0 + rho * screening)
        return carry

    lax.fori_loop(0, rows * cols // TOGETHER, tiles, 0)
    for rz in (-1, 0, 1):
        for rs in (-1, 0, 1):
            where = device_at(rz, rs, dom_count, sub_count)

            @pl.when(in_range(rz, dom_count))
            def _(rz=rz, rs=rs, where=where):
                for slot, (a, b) in enumerate(side_tiles(rz, rs, rows, cols)[:slots]):
                    send_ref[where, slot : slot + 1, :] = born_ref[a, b : b + 1, :]
                    line = slots + slot
                    send_ref[where, line : line + 1, :] = q_ref[a, b : b + 1, :]


def energy_body(dims, near_ref, recv_ref, halo_ref, q_ref, r_ref, born_ref,
                own_k, own_w, win_k, win_w, win_c, win_r, far_k, far_w, far_c, far_vol, far_q,
                rgrad_ref, grad_ref, send_ref,
                turned_ref, win_e, pair_f, pair_s, pair_i, pair_w, far_acc, win_acc):
    rows, cols, dom_count, sub_count = dims
    together = pair_f.shape[0]
    kept = pair_i.shape[1] == dom_count * sub_count
    devices = dom_count * sub_count
    slots = max(rows, cols)
    tiles = rows * cols
    places = (rows + 2) * (cols + 2)

    def own(c, a, b):
        at = slice(b, b + 1)
        return born_ref[a, at, :] if c == 0 else q_ref[a, at, :]

    zero = jnp.zeros((LANES, LANES), jnp.float32)
    no_force = jnp.zeros((WROWS, LANES), jnp.float32)

    def put(p, carry):
        far_acc[p] = jnp.zeros((WROWS, 2 * LANES), jnp.float32)
        return carry

    lax.fori_loop(0, devices // 2, put, 0)
    for place in range(places):
        born, charge = [window_source(dims, place, halo_ref, own, 0, c) for c in range(2)]
        win_e[place, 0:1, :] = born * (1.0 / UNIT)
        win_e[place, 1:2, :] = (-0.25 * LOG2E * UNIT) / born
        win_e[place, 2:3, :] = CHARGE_UNIT * charge
        win_acc[place] = no_force
    for a in range(rows):
        for b in range(cols):
            at = slice(b, b + 1)
            for c, row in enumerate([born_ref[a, at, :], q_ref[a, at, :], r_ref[a, at, :]]):
                turned_ref[a * cols + b, c] = turned(row)

    def group(n, carry):
        members = [n * together + i for i in range(together)]
        own_rows = [[turned_ref[t, c] for c in range(3)] for t in members]
        own_inv = [1.0 / rows_of[0] for rows_of in own_rows]

        def pair(i, s, other_born, other_inv, charge):
            own_born, own_q, _ = own_rows[i]
            e = jnp.exp2(s * (own_inv[i] * other_inv))
            r = lax.rsqrt(s + (own_born * other_born) * e)
            return charge * (own_q * r), (r * r) * (1.0 - 0.25 * e)

        born_near = []
        for i, t in enumerate(members):
            x, total = own_k[t], zero
            for k in range(NEAR):
                place = window_place(t, k, cols)
                other_born, other_inv, charge = [win_e[place, c : c + 1, :] for c in range(3)]
                charge = flagged(near_ref, t, k, cols, charge)
                if k == SELF:
                    charge = jnp.where(own_pair(), 0.0, charge)
                s = product(x, win_k[place])
                qr, slope = pair(i, s, other_born, other_inv, charge)
                f = qr * slope
                pair_f[i, devices + k] = f
                pair_s[i, devices + k] = s
                total = total + (qr - s * f)
            born_near.append(total)
        def far_square(p):
            return product(jnp.concatenate([own_k[t] for t in members], axis=0), far_k[p])

        def far_energy(p, s_all, born_far):
            out = list(born_far)
            for half in range(2):
                d = 2 * p + half
                other_born, other_inv = recv_ref[d, 5:6, :], recv_ref[d, 6:7, :]
                for i, t in enumerate(members):
                    charge = far_q[d, pl.ds(t, 1), :]
                    s = quarter_of(s_all, i, half)
                    qr, slope = pair(i, s, other_born, other_inv, charge)
                    inv = 1.0 / (s + SPAN / UNIT)
                    weight = s * inv
                    falling = weight * slope
                    square = inv * inv
                    pair_f[i, d] = qr * (falling - square)
                    pair_s[i, d] = s
                    if kept:
                        pair_i[i, d] = square
                        pair_w[i, d] = weight
                    out[i] = out[i] + qr * (weight - s * falling)
            return tuple(out)

        born_far = over_far(devices // 2, far_square, far_energy, tuple([zero] * together))
        scale = []
        for i, t in enumerate(members):
            _, own_q, own_rho = own_rows[i]
            part = own_inv[i] * (UNIT * (0.5 * born_far[i] + born_near[i]))
            own_part = own_q * own_inv[i]
            rg = jnp.sum(part, axis=1, keepdims=True) + 0.5 * (own_part * own_part)
            scale.append(rg * (own_rho * own_rho) * (1.0 / UNIT ** 3))
            rgrad_ref[t // cols, pl.ds(t % cols, 1), :] = rg.T[0:1]

        def halves(f):
            high = f.astype(jnp.bfloat16)
            return high, (f - high.astype(jnp.float32)).astype(jnp.bfloat16)

        own_near = []
        for i, t in enumerate(members):
            total = no_force
            for k in range(NEAR):
                place = window_place(t, k, cols)
                volume = flagged(near_ref, t, k, cols, 4.0 * win_r[place, 1:2, :])
                inv = 1.0 / (pair_s[i, devices + k] + win_r[place, 0:1, :])
                f = pair_f[i, devices + k] - (scale[i] * volume) * (inv * inv * inv)
                if k == SELF:
                    f = jnp.where(own_pair(), 0.0, f)
                high, low = halves(f)
                total = total + product_turned(win_w[place], jnp.concatenate([high, low], axis=1))
                win_acc[place] = win_acc[place] + product(
                    own_w[t], jnp.concatenate([high, low], axis=0))
            own_near.append(total)
        x_sums = jnp.concatenate([own_w[t] for t in members], axis=1)

        def far_factors(p):
            parts = [[], []]
            for half in range(2):
                d = 2 * p + half
                for i, t in enumerate(members):
                    s = pair_s[i, d]
                    volume = far_vol[d, pl.ds(t, 1), :]
                    near = 1.0 / (s + recv_ref[d, 7:8, :])
                    if kept:
                        square, weight = pair_i[i, d], pair_w[i, d]
                    else:
                        inv = 1.0 / (s + SPAN / UNIT)
                        square, weight = inv * inv, s * inv
                    slope = (square - 4.0 * (weight * near)) * (near * near)
                    parts[half].append(halves(pair_f[i, d] + (scale[i] * volume) * slope))
            columns = [jnp.concatenate([x for pieces_of in half for x in pieces_of], axis=0)
                       for half in parts]
            lines = [jnp.concatenate(parts[0][i] + parts[1][i], axis=1) for i in range(together)]
            return jnp.concatenate(columns, axis=1), jnp.concatenate(lines, axis=0)

        def far_sums(p, factors, own_sum):
            far_acc[p] = far_acc[p] + product(x_sums, factors[0])
            return own_sum + product_turned(far_w[p], factors[1])

        own_sum = over_far(devices // 2, far_factors, far_sums, jnp.concatenate(own_near, axis=1))
        for i, t in enumerate(members):
            total, moment = weighted(own_sum[:, i * LANES : (i + 1) * LANES])
            grad = win_c[window_place(t, SELF, cols), 0:3, :] * total - moment
            for c in range(3):
                grad_ref[c, t // cols, pl.ds(t % cols, 1), :] = grad[c : c + 1]
        return carry

    lax.fori_loop(0, tiles // together, group, 0)

    def send_far(p, carry):
        for half in range(2):
            d = 2 * p + half
            total, moment = weighted(far_acc[p, :, half * LANES : (half + 1) * LANES])
            send_ref[d, 0:3, :] = far_c[d, 0:3, :] * total - moment
        return carry

    lax.fori_loop(0, devices // 2, send_far, 0)

    def partner_grad(az, bs):
        place = (az + 1) * (cols + 2) + bs + 1
        total, moment = weighted(win_acc[place])
        return win_c[place, 0:3, :] * total - moment

    for a in range(rows):
        for b in range(cols):
            grad = partner_grad(a, b)
            for c in range(3):
                grad_ref[c, a, b : b + 1, :] = grad_ref[c, a, b : b + 1, :] + grad[c : c + 1]
    for rz in (-1, 0, 1):
        for rs in (-1, 0, 1):
            if rz == 0 and rs == 0:
                continue
            where = device_at(rz, rs, dom_count, sub_count)

            @pl.when(in_range(rz, dom_count))
            def _(rz=rz, rs=rs, where=where):
                for slot, (pa, pb) in enumerate(side_tiles(-rz, -rs, rows, cols)):
                    az = {0: pa, 1: rows, -1: -1}[rz]
                    bs = {0: pb, 1: cols, -1: -1}[rs]
                    grad = partner_grad(az, bs)
                    for c in range(3):
                        line = 3 + c * slots + slot
                        send_ref[where, line : line + 1, :] = grad[c : c + 1]


def finish_body(dims, recv_ref, grad_ref, members_ref, member_ref, born_ref, rgrad_ref,
                force_ref, born_out, rgrad_out):
    rows, cols, dom_count, sub_count = dims
    slots = max(rows, cols)

    def add(d, total):
        return total + recv_ref[d, 0:3, :]

    centre_grad = lax.fori_loop(
        0, dom_count * sub_count, add, jnp.zeros((3, LANES), jnp.float32))
    per_member = centre_grad / members_ref[0:3, :]
    born_out[...] = born_ref[...]
    rgrad_out[...] = rgrad_ref[...]
    block = pieces(jnp.concatenate([per_member, jnp.zeros((5, LANES), jnp.float32)], axis=0))
    block = jnp.concatenate(block + (jnp.zeros_like(block[0]),), axis=0).astype(jnp.bfloat16)
    back = product(block, member_ref[...])
    back = back[0:8] + back[8:16] + back[16:24]
    for a in range(rows):
        for b in range(cols):
            t = a * cols + b
            spread_out = back[:, t * LANES : (t + 1) * LANES]
            for c in range(3):
                force_ref[c, a, b : b + 1, :] = -(
                    grad_ref[c, a, b : b + 1, :] + spread_out[c : c + 1])
    for rz in (-1, 0, 1):
        for rs in (-1, 0, 1):
            if rz == 0 and rs == 0:
                continue
            where = device_at(rz, rs, dom_count, sub_count)

            @pl.when(in_range(rz, dom_count))
            def _(rz=rz, rs=rs, where=where):
                for slot, (a, b) in enumerate(side_tiles(rz, rs, rows, cols)):
                    for c in range(3):
                        line = 3 + c * slots + slot
                        force_ref[c, a, b : b + 1, :] = (
                            force_ref[c, a, b : b + 1, :] - recv_ref[where, line : line + 1, :])


def f32(*shape):
    return jax.ShapeDtypeStruct(shape, jnp.float32)


def bf16(*shape):
    return jax.ShapeDtypeStruct(shape, jnp.bfloat16)


def local(positions, charge, radius, segment, near_tiles):
    rows, cols, width = charge.shape
    dom_count, sub_count = lax.axis_size("dom"), lax.axis_size("sub")
    dims = (rows, cols, dom_count, sub_count)
    devices = dom_count * sub_count
    tiles = rows * cols
    assert width == LANES and tiles * CT == LANES and sub_count > 2 and devices % 2 == 0
    slots = max(rows, cols)
    places = (rows + 2) * (cols + 2)
    vec = (SUBLANES, LANES)
    together = 2 if devices <= 64 else 1
    kept_shape = (together, devices, LANES, LANES) if devices <= 64 else (1, 1) + vec
    vmem = pltpu.MemorySpace.VMEM

    def call(body, ins, outs, scratch=(), room=8 << 20, space=vmem):
        return pl.pallas_call(
            lambda *refs: body(dims, *refs),
            out_shape=outs,
            in_specs=[pl.BlockSpec(memory_space=pltpu.MemorySpace.SMEM if x is near_tiles else space)
                      for x in ins],
            out_specs=[pl.BlockSpec(memory_space=vmem) for _ in outs],
            scratch_shapes=list(scratch),
            compiler_params=pltpu.CompilerParams(vmem_limit_bytes=room),
            name=body.__name__,
        )(*[pltpu.with_memory_space_constraint(x, space) if space is not vmem else x for x in ins])

    def exchanged(blocks):
        return lax.all_to_all(blocks, AXES, 0, 0, tiled=True)

    send, members, member = call(
        pack_body, (positions, charge, radius, segment),
        [f32(devices, 8 + 4 * slots, LANES), f32(*vec), bf16(LANES, tiles * LANES)],
        [pltpu.VMEM(positions.shape, jnp.float32), pltpu.VMEM(charge.shape, jnp.float32),
         pltpu.VMEM(radius.shape, jnp.float32), pltpu.VMEM(segment.shape, jnp.int32),
         pltpu.SemaphoreType.DMA((4,))],
        space=pltpu.MemorySpace.HBM)
    table = exchanged(send)
    send, born, *tables = call(
        screen_body, (near_tiles, table, positions, charge, radius),
        [f32(devices, 2 * slots, LANES), f32(rows, cols, LANES),
         bf16(tiles, LANES, KROWS), bf16(tiles, WROWS, 2 * LANES),
         bf16(places, KROWS, LANES), bf16(places, WROWS, 2 * LANES),
         f32(places, *vec), f32(places, *vec),
         bf16(devices // 2, KROWS, 2 * LANES), bf16(devices // 2, WROWS, 4 * LANES),
         f32(devices, *vec), f32(devices, tiles, LANES), f32(devices, tiles, LANES)],
        room=(8 << 20) + devices * (1 << 16))
    halo = exchanged(send)
    radius_grad, grad, send = call(
        energy_body, (near_tiles, table, halo, charge, radius, born, *tables),
        [f32(rows, cols, LANES), f32(3, rows, cols, LANES), f32(devices, 4 + 3 * slots, LANES)],
        [pltpu.VMEM((tiles, 3, LANES, LANES), jnp.float32),
         pltpu.VMEM((places,) + vec, jnp.float32),
         pltpu.VMEM((together, devices + NEAR, LANES, LANES), jnp.float32),
         pltpu.VMEM((together, devices + NEAR, LANES, LANES), jnp.float32),
         pltpu.VMEM(kept_shape, jnp.float32),
         pltpu.VMEM(kept_shape, jnp.float32),
         pltpu.VMEM((devices // 2, WROWS, 2 * LANES), jnp.float32),
         pltpu.VMEM((places, WROWS, LANES), jnp.float32)],
        room=(13 << 20) + devices * (3 << 16 if together == 1 else 10 << 16))
    back = exchanged(send)
    shape = f32(rows, cols, LANES)
    forces, born_radii, radius_grad = call(
        finish_body, (back, grad, members, member, born, radius_grad),
        [f32(3, rows, cols, LANES), shape, shape])
    return born_radii, radius_grad, forces


def solution(mesh):
    flat = P(("groups", "dom"), "sub", None)
    stacked = P(None, ("groups", "dom"), "sub", None)
    return jax.shard_map(
        local,
        mesh=mesh,
        in_specs=(stacked, flat, flat, flat, flat),
        out_specs=(flat, flat, stacked),
        check_vma=False,
    )
```

```python
import jax
import jax.numpy as jnp
from jax import lax
from jax.experimental import pallas as pl
from jax.experimental.pallas import tpu as pltpu
from jax.sharding import PartitionSpec as P

CT = 16
LANES = 128
SUBLANES = 8
UNIT = 128.0
TOGETHER = 8
KROWS = 48
WROWS = 16
SPAN = 64.0
CHARGE_UNIT = 0.5 * UNIT ** -1.5
RADIUS_FACTOR = 1.5
LOG2E = 1.4426950408889634
LN2 = 0.6931471805599453
HIGHEST = lax.Precision.HIGHEST
AXES = ("dom", "sub")
STEPS = ((-1, -1), (-1, 0), (-1, 1), (0, -1), (0, 1), (1, -1), (1, 0), (1, 1))
SELF = len(STEPS)
NEAR = len(STEPS) + 1


def side_tiles(rz, rs, rows, cols):
    along = {0: range(rows), 1: [rows - 1], -1: [0]}[rz]
    around = {0: range(cols), 1: [cols - 1], -1: [0]}[rs]
    return [(a, b) for a in along for b in around]


def partner(a, b, k, rows, cols):
    dz, ds = STEPS[k] if k < SELF else (0, 0)
    az, bs = a + dz, b + ds
    rz = -1 if az < 0 else 1 if az >= rows else 0
    rs = -1 if bs < 0 else 1 if bs >= cols else 0
    tile = (az % rows, bs % cols)
    if rz == 0 and rs == 0:
        return (0, 0), None, tile
    return (rz, rs), side_tiles(-rz, -rs, rows, cols).index(tile), tile


def device_at(rz, rs, dom_count, sub_count):
    along = jnp.clip(lax.axis_index("dom") + rz, 0, dom_count - 1)
    around = lax.rem(lax.axis_index("sub") + rs + sub_count, sub_count)
    return along * sub_count + around


def in_range(rz, dom_count):
    at = lax.axis_index("dom") + rz
    return (at >= 0) & (at < dom_count)


def far_unroll(pairs):
    return 8 if pairs % 8 == 0 else 1


def pieces(value):
    first = value.astype(jnp.bfloat16).astype(jnp.float32)
    left = value - first
    second = left.astype(jnp.bfloat16).astype(jnp.float32)
    return first, second, left - second


def line_of(shape=(SUBLANES, LANES)):
    return lax.broadcasted_iota(jnp.int32, shape, 0)


def side_block(points, ones_line, norm_line, factor):
    norm = jnp.sum(points * points, axis=0, keepdims=True) * (1.0 / UNIT)
    line = line_of()
    block = jnp.where(line == norm_line, norm, jnp.where(line == ones_line, 1.0, factor * points))
    return pieces(block)


def weight_rows(first, second, third):
    rows = jnp.concatenate(
        [first, second[0:3], third[0:3], jnp.zeros((2, LANES), jnp.float32)], axis=0)
    return jnp.concatenate([rows, rows], axis=1).astype(jnp.bfloat16)


def other_tables(points):
    c1, c2, c3 = side_block(points, 4, 3, 1.0)
    table = jnp.concatenate([c1, c2, c1, c2, c3, c1], axis=0).astype(jnp.bfloat16)
    return table, weight_rows(c1, c2, c3)


def own_tables(points):
    x1, x2, x3 = side_block(points, 3, 4, -2.0 / UNIT)
    stack = jnp.concatenate(
        [x1, x1, x2, x2, x1, x3, jnp.zeros((LANES - KROWS, LANES), jnp.float32)], axis=0)
    w1, w2, w3 = side_block(points, 4, 3, 1.0)
    return stack.T[:, 0:KROWS].astype(jnp.bfloat16), weight_rows(w1, w2, w3)


def product(a, b):
    return jnp.dot(a, b, preferred_element_type=jnp.float32)


def product_turned(a, b):
    return lax.dot_general(a, b, (((1,), (1,)), ((), ())), preferred_element_type=jnp.float32)


def weighted(block):
    return block[4:5], block[0:3] + block[8:11] + block[11:14]


def member_table(seg_ref, a, b, cols):
    comp = lax.broadcasted_iota(jnp.int32, (LANES, LANES), 0)
    owner = seg_ref[a, b : b + 1, :] + (a * cols + b) * CT
    return (comp == owner).astype(jnp.float32).astype(jnp.bfloat16)


def turned(row):
    return jnp.broadcast_to(row, (LANES, LANES)).T


def lane_sums(block):
    return jnp.sum(block.T, axis=0, keepdims=True)


def pack_body(dims, pos_hbm, q_hbm, r_hbm, seg_hbm, send_ref, members_ref, member_ref,
              pos_ref, q_ref, r_ref, seg_ref, arrived):
    rows, cols, dom_count, sub_count = dims
    copies = [
        pltpu.make_async_copy(source, place, arrived.at[n])
        for n, (source, place) in enumerate(
            [(pos_hbm, pos_ref), (q_hbm, q_ref), (r_hbm, r_ref), (seg_hbm, seg_ref)])]
    for copy in copies:
        copy.start()
    for copy in copies:
        copy.wait()
    slots = max(rows, cols)
    one = jnp.ones((1, LANES), jnp.float32)
    values = []
    for a in range(rows):
        for b in range(cols):
            at, t = slice(b, b + 1), a * cols + b
            rho = r_ref[a, at, :]
            member_ref[:, t * LANES : (t + 1) * LANES] = member_table(seg_ref, a, b, cols)
            block = pieces(jnp.concatenate(
                [pos_ref[0, a, at, :], pos_ref[1, a, at, :], pos_ref[2, a, at, :],
                 q_ref[a, at, :], rho * rho * rho, rho, one, one], axis=0))
            values.append(jnp.concatenate(block + (jnp.zeros_like(block[0]),), axis=0))
    sums = product_turned(jnp.concatenate(values, axis=1).astype(jnp.bfloat16), member_ref[...])
    total = sums[0:8] + sums[8:16] + sums[16:24]
    members = total[6:7]
    comp_radius = RADIUS_FACTOR * total[5:6] / members
    table = jnp.concatenate(
        [total[0:3] / members, CHARGE_UNIT * total[3:4], total[4:5],
         comp_radius * (1.0 / UNIT), (-0.25 * LOG2E * UNIT) / comp_radius,
         comp_radius * comp_radius * (1.0 / UNIT)], axis=0)
    members_ref[...] = jnp.broadcast_to(members, (SUBLANES, LANES))

    def put(d, carry):
        send_ref[d, 0:8, :] = table
        return carry

    lax.fori_loop(0, dom_count * sub_count, put, 0)
    for rz in (-1, 0, 1):
        for rs in (-1, 0, 1):
            where = device_at(rz, rs, dom_count, sub_count)

            @pl.when(in_range(rz, dom_count))
            def _(rz=rz, rs=rs, where=where):
                for slot, (a, b) in enumerate(side_tiles(rz, rs, rows, cols)[:slots]):
                    at = slice(b, b + 1)
                    for c in range(3):
                        line = 8 + c * slots + slot
                        send_ref[where, line : line + 1, :] = pos_ref[c, a, at, :]
                    line = 8 + 3 * slots + slot
                    send_ref[where, line : line + 1, :] = r_ref[a, at, :]


def mask_rows(dims, near_ref, tables):
    rows, cols, dom_count, sub_count = dims
    shape = (rows * cols, LANES)
    row = lax.broadcasted_iota(jnp.int32, shape, 0)
    tile_of = lax.broadcasted_iota(jnp.int32, shape, 1) // CT
    struck = {}
    for a in range(rows):
        for b in range(cols):
            for k in range(NEAR):
                rel, _, (pa, pb) = partner(a, b, k, rows, cols)
                flag = near_ref[a, b, k] if k < SELF else 1
                at = jnp.where(row == a * cols + b, tile_of - (pa * cols + pb), 1)
                hit = jnp.where(at == 0, flag, 0)
                struck[rel] = struck[rel] | hit if rel in struck else hit
    for (rz, rs), hit in struck.items():
        where = device_at(rz, rs, dom_count, sub_count)
        for table in tables:
            table[where] = jnp.where(hit == 1, 0.0, table[where])


def near_source(dims, rz, rs):
    rows, cols, dom_count, sub_count = dims
    return device_at(rz, rs, dom_count, sub_count)


def window_source(dims, place, recv_ref, own, base, c):
    rows, cols, _, _ = dims
    az, bs = place // (cols + 2) - 1, place % (cols + 2) - 1
    rz = -1 if az < 0 else 1 if az >= rows else 0
    rs = -1 if bs < 0 else 1 if bs >= cols else 0
    tile = (az % rows, bs % cols)
    if rz == 0 and rs == 0:
        return own(c, *tile)
    line = base + c * max(rows, cols) + side_tiles(-rz, -rs, rows, cols).index(tile)
    return recv_ref[near_source(dims, rz, rs), line : line + 1, :]


def window_place(t, k, cols):
    dz, ds = STEPS[k] if k < SELF else (0, 0)
    return (t // cols + 1 + dz) * (cols + 2) + t % cols + 1 + ds


def flagged(near_ref, t, k, cols, row):
    if k == SELF:
        return row
    return jnp.where(near_ref[t // cols, t % cols, k] == 1, row, 0.0)


def own_pair():
    shape = (LANES, LANES)
    return lax.broadcasted_iota(jnp.int32, shape, 0) == lax.broadcasted_iota(jnp.int32, shape, 1)


def quarter_of(block, i, half):
    return block[i * LANES : (i + 1) * LANES, half * LANES : (half + 1) * LANES]


def over_far(pairs, begin, end, carry):
    unroll = far_unroll(pairs)

    def chunk(n, carry):
        begun = begin(n * unroll)
        for j in range(unroll):
            ahead = begin(n * unroll + j + 1) if j + 1 < unroll else None
            carry = end(n * unroll + j, begun, carry)
            begun = ahead
        return carry

    if pairs == unroll:
        return chunk(0, carry)
    return lax.fori_loop(0, pairs // unroll, chunk, carry)


def screen_body(dims, near_ref, recv_ref, pos_ref, q_ref, r_ref, send_ref, born_ref,
                own_k, own_w, win_k, win_w, win_c, win_r, far_k, far_w, far_c, far_vol, far_q):
    rows, cols, dom_count, sub_count = dims
    devices = dom_count * sub_count
    slots = max(rows, cols)
    line = line_of()

    middle = jnp.zeros((SUBLANES, LANES), jnp.float32)
    for c in range(3):
        mean = jnp.sum(pos_ref[c]) * (1.0 / (rows * cols * LANES))
        middle = jnp.where(line == c, mean, middle)

    def own(c, a, b):
        if c < 3:
            return pos_ref[c, a, b : b + 1, :]
        return r_ref[a, b : b + 1, :]

    def put(p, carry):
        for half in range(2):
            d = 2 * p + half
            far_q[d] = jnp.broadcast_to(recv_ref[d, 3:4, :], (rows * cols, LANES))
            far_vol[d] = jnp.broadcast_to(recv_ref[d, 4:5, :], (rows * cols, LANES))
            points = jnp.where(line < 3, recv_ref[d, 0:8, :] - middle, 0.0)
            far_c[d] = points
            table, weights = other_tables(points)
            far_k[p, :, half * LANES : (half + 1) * LANES] = table
            far_w[p, :, 2 * half * LANES : 2 * (half + 1) * LANES] = weights
        return carry

    lax.fori_loop(0, devices // 2, put, 0)
    mask_rows(dims, near_ref, (far_vol, far_q))
    none = jnp.zeros((SUBLANES - 3, LANES), jnp.float32)
    for place in range((rows + 2) * (cols + 2)):
        x, y, z, rho = [window_source(dims, place, recv_ref, own, 8, c) for c in range(4)]
        points = jnp.concatenate([x, y, z, none], axis=0) - middle
        win_c[place] = points
        win_k[place], win_w[place] = other_tables(points)
        win_r[place, 0:1, :] = rho * rho * (1.0 / UNIT)
        win_r[place, 1:2, :] = rho * rho * rho
        az, bs = place // (cols + 2) - 1, place % (cols + 2) - 1
        if 0 <= az < rows and 0 <= bs < cols:
            own_k[az * cols + bs], own_w[az * cols + bs] = own_tables(points)

    def tiles(n, carry):
        pair = [n * TOGETHER + i for i in range(TOGETHER)]
        x = [own_k[t] for t in pair]
        sums = []
        for i, t in enumerate(pair):
            total = jnp.zeros((LANES, LANES), jnp.float32)
            for k in range(NEAR):
                place = window_place(t, k, cols)
                volume = flagged(near_ref, t, k, cols, win_r[place, 1:2, :])
                if k == SELF:
                    volume = jnp.where(own_pair(), 0.0, volume)
                near = product(x[i], win_k[place]) + win_r[place, 0:1, :]
                total = total + volume / (near * near)
            sums.append(total)
        x_all = jnp.concatenate(x, axis=0)

        def far_square(p):
            return product(x_all, far_k[p])

        def far(p, s_all, sums):
            out = list(sums)
            for half in range(2):
                d = 2 * p + half
                for i, t in enumerate(pair):
                    s = quarter_of(s_all, i, half)
                    near = s + recv_ref[d, 7:8, :]
                    volume = far_vol[d, pl.ds(t, 1), :]
                    out[i] = out[i] + (volume * s) / ((s + SPAN / UNIT) * (near * near))
            return tuple(out)

        sums = over_far(devices // 2, far_square, far, tuple(sums))
        for i, t in enumerate(pair):
            screening = lane_sums(sums[i]) * (1.0 / (UNIT * UNIT))
            a, b = t // cols, t % cols
            rho = r_ref[a, pl.ds(b, 1), :]
            born_ref[a, pl.ds(b, 1), :] = rho * (1.0 + rho * screening)
        return carry

    lax.fori_loop(0, rows * cols // TOGETHER, tiles, 0)
    for rz in (-1, 0, 1):
        for rs in (-1, 0, 1):
            where = device_at(rz, rs, dom_count, sub_count)

            @pl.when(in_range(rz, dom_count))
            def _(rz=rz, rs=rs, where=where):
                for slot, (a, b) in enumerate(side_tiles(rz, rs, rows, cols)[:slots]):
                    send_ref[where, slot : slot + 1, :] = born_ref[a, b : b + 1, :]
                    line = slots + slot
                    send_ref[where, line : line + 1, :] = q_ref[a, b : b + 1, :]


def energy_body(dims, near_ref, recv_ref, halo_ref, q_ref, r_ref, born_ref,
                own_k, own_w, win_k, win_w, win_c, win_r, far_k, far_w, far_c, far_vol, far_q,
                rgrad_ref, grad_ref, send_ref,
                turned_ref, win_e, *refs):
    rows, cols, dom_count, sub_count = dims
    stores, (far_acc, win_acc) = (refs[0:4], refs[4:8]), refs[8:]
    together = refs[0].shape[0]
    kept = refs[2].shape[1] == dom_count * sub_count
    devices = dom_count * sub_count
    slots = max(rows, cols)
    tiles = rows * cols
    places = (rows + 2) * (cols + 2)

    def own(c, a, b):
        at = slice(b, b + 1)
        return born_ref[a, at, :] if c == 0 else q_ref[a, at, :]

    zero = jnp.zeros((LANES, LANES), jnp.float32)
    no_force = jnp.zeros((WROWS, LANES), jnp.float32)

    def put(p, carry):
        far_acc[p] = jnp.zeros((WROWS, 2 * LANES), jnp.float32)
        return carry

    lax.fori_loop(0, devices // 2, put, 0)
    for place in range(places):
        born, charge = [window_source(dims, place, halo_ref, own, 0, c) for c in range(2)]
        win_e[place, 0:1, :] = born * (1.0 / UNIT)
        win_e[place, 1:2, :] = (-0.25 * LOG2E * UNIT) / born
        win_e[place, 2:3, :] = CHARGE_UNIT * charge
        win_acc[place] = no_force
    for a in range(rows):
        for b in range(cols):
            at = slice(b, b + 1)
            for c, row in enumerate([born_ref[a, at, :], q_ref[a, at, :], r_ref[a, at, :]]):
                turned_ref[a * cols + b, c] = turned(row)

    def energy_steps(n, store):
        pair_f, pair_s, pair_i, pair_w = store
        members = [n * together + i for i in range(together)]
        own_rows = [[turned_ref[t, c] for c in range(3)] for t in members]
        own_inv = [1.0 / rows_of[0] for rows_of in own_rows]

        def pair(i, s, other_born, other_inv, charge):
            own_born, own_q, _ = own_rows[i]
            e = jnp.exp2(s * (own_inv[i] * other_inv))
            r = lax.rsqrt(s + (own_born * other_born) * e)
            return charge * (own_q * r), (r * r) * (1.0 - 0.25 * e)

        def near_energy(k, born_near):
            out = list(born_near)
            for i, t in enumerate(members):
                place = window_place(t, k, cols)
                other_born, other_inv, charge = [win_e[place, c : c + 1, :] for c in range(3)]
                charge = flagged(near_ref, t, k, cols, charge)
                if k == SELF:
                    charge = jnp.where(own_pair(), 0.0, charge)
                s = product(own_k[t], win_k[place])
                qr, slope = pair(i, s, other_born, other_inv, charge)
                f = qr * slope
                pair_f[i, devices + k] = f
                pair_s[i, devices + k] = s
                out[i] = out[i] + (qr - s * f)
            return tuple(out)

        def far_square(p):
            return product(jnp.concatenate([own_k[t] for t in members], axis=0), far_k[p])

        def far_energy(p, s_all, born_far):
            out = list(born_far)
            for half in range(2):
                d = 2 * p + half
                other_born, other_inv = recv_ref[d, 5:6, :], recv_ref[d, 6:7, :]
                for i, t in enumerate(members):
                    charge = far_q[d, pl.ds(t, 1), :]
                    s = quarter_of(s_all, i, half)
                    qr, slope = pair(i, s, other_born, other_inv, charge)
                    inv = 1.0 / (s + SPAN / UNIT)
                    weight = s * inv
                    falling = weight * slope
                    square = inv * inv
                    pair_f[i, d] = qr * (falling - square)
                    pair_s[i, d] = s
                    if kept:
                        pair_i[i, d] = square
                        pair_w[i, d] = weight
                    out[i] = out[i] + qr * (weight - s * falling)
            return tuple(out)

        def finish(born_near, born_far):
            scale = []
            for i, t in enumerate(members):
                _, own_q, own_rho = own_rows[i]
                part = own_inv[i] * (UNIT * (0.5 * born_far[i] + born_near[i]))
                own_part = own_q * own_inv[i]
                rg = jnp.sum(part, axis=1, keepdims=True) + 0.5 * (own_part * own_part)
                scale.append(rg * (own_rho * own_rho) * (1.0 / UNIT ** 3))
                rgrad_ref[t // cols, pl.ds(t % cols, 1), :] = rg.T[0:1]
            return scale

        return near_energy, far_square, far_energy, finish

    def halves(f):
        high = f.astype(jnp.bfloat16)
        return high, (f - high.astype(jnp.float32)).astype(jnp.bfloat16)

    def chain_steps(n, store, scale):
        pair_f, pair_s, pair_i, pair_w = store
        members = [n * together + i for i in range(together)]

        def near_chain(k, own_near):
            out = list(own_near)
            for i, t in enumerate(members):
                place = window_place(t, k, cols)
                volume = flagged(near_ref, t, k, cols, 4.0 * win_r[place, 1:2, :])
                inv = 1.0 / (pair_s[i, devices + k] + win_r[place, 0:1, :])
                f = pair_f[i, devices + k] - (scale[i] * volume) * (inv * inv * inv)
                if k == SELF:
                    f = jnp.where(own_pair(), 0.0, f)
                high, low = halves(f)
                out[i] = out[i] + product_turned(
                    win_w[place], jnp.concatenate([high, low], axis=1))
                win_acc[place] = win_acc[place] + product(
                    own_w[t], jnp.concatenate([high, low], axis=0))
            return tuple(out)

        x_sums = jnp.concatenate([own_w[t] for t in members], axis=1)

        def far_factors(p):
            parts = [[], []]
            for half in range(2):
                d = 2 * p + half
                for i, t in enumerate(members):
                    s = pair_s[i, d]
                    volume = far_vol[d, pl.ds(t, 1), :]
                    near = 1.0 / (s + recv_ref[d, 7:8, :])
                    if kept:
                        square, weight = pair_i[i, d], pair_w[i, d]
                    else:
                        inv = 1.0 / (s + SPAN / UNIT)
                        square, weight = inv * inv, s * inv
                    slope = (square - 4.0 * (weight * near)) * (near * near)
                    parts[half].append(halves(pair_f[i, d] + (scale[i] * volume) * slope))
            columns = [jnp.concatenate([x for pieces_of in half for x in pieces_of], axis=0)
                       for half in parts]
            lines = [jnp.concatenate(parts[0][i] + parts[1][i], axis=1) for i in range(together)]
            return jnp.concatenate(columns, axis=1), jnp.concatenate(lines, axis=0)

        def far_sums(p, factors, own_sum):
            far_acc[p] = far_acc[p] + product(x_sums, factors[0])
            return own_sum + product_turned(far_w[p], factors[1])

        def finish(own_sum):
            for i, t in enumerate(members):
                total, moment = weighted(own_sum[:, i * LANES : (i + 1) * LANES])
                grad = win_c[window_place(t, SELF, cols), 0:3, :] * total - moment
                for c in range(3):
                    grad_ref[c, t // cols, pl.ds(t % cols, 1), :] = grad[c : c + 1]

        return near_chain, far_factors, far_sums, finish

    pairs = devices // 2

    def energy_of(n, store):
        near_energy, far_square, far_energy, finish = energy_steps(n, store)
        born_near = tuple([zero] * together)
        for k in range(NEAR):
            born_near = near_energy(k, born_near)
        return finish(born_near, over_far(pairs, far_square, far_energy, tuple([zero] * together)))

    def chain_of(n, store, scale):
        near_chain, far_factors, far_sums, finish = chain_steps(n, store, scale)
        own_near = tuple([no_force] * together)
        for k in range(NEAR):
            own_near = near_chain(k, own_near)
        finish(over_far(pairs, far_factors, far_sums, jnp.concatenate(own_near, axis=1)))

    def both_of(n, store, last_store, scale):
        near_energy, far_square, far_energy, finish = energy_steps(n, store)
        near_chain, far_factors, far_sums, finish_chain = chain_steps(n - 1, last_store, scale)
        born_near, own_near = tuple([zero] * together), tuple([no_force] * together)
        for k in range(NEAR):
            born_near = near_energy(k, born_near)
            own_near = near_chain(k, own_near)

        def begin(p):
            return far_square(p), far_factors(p)

        def end(p, begun, carry):
            return far_energy(p, begun[0], carry[0]), far_sums(p, begun[1], carry[1])

        born_far, own_sum = over_far(
            pairs, begin, end, (tuple([zero] * together), jnp.concatenate(own_near, axis=1)))
        finish_chain(own_sum)
        return finish(born_near, born_far)

    groups = tiles // together
    if kept:
        scale = energy_of(0, stores[0])
        for n in range(1, groups):
            scale = both_of(n, stores[n % 2], stores[(n - 1) % 2], scale)
        chain_of(groups - 1, stores[(groups - 1) % 2], scale)
    else:

        def group(n, carry):
            chain_of(n, stores[0], energy_of(n, stores[0]))
            return carry

        lax.fori_loop(0, groups, group, 0)

    def send_far(p, carry):
        for half in range(2):
            d = 2 * p + half
            total, moment = weighted(far_acc[p, :, half * LANES : (half + 1) * LANES])
            send_ref[d, 0:3, :] = far_c[d, 0:3, :] * total - moment
        return carry

    lax.fori_loop(0, devices // 2, send_far, 0)

    def partner_grad(az, bs):
        place = (az + 1) * (cols + 2) + bs + 1
        total, moment = weighted(win_acc[place])
        return win_c[place, 0:3, :] * total - moment

    for a in range(rows):
        for b in range(cols):
            grad = partner_grad(a, b)
            for c in range(3):
                grad_ref[c, a, b : b + 1, :] = grad_ref[c, a, b : b + 1, :] + grad[c : c + 1]
    for rz in (-1, 0, 1):
        for rs in (-1, 0, 1):
            if rz == 0 and rs == 0:
                continue
            where = device_at(rz, rs, dom_count, sub_count)

            @pl.when(in_range(rz, dom_count))
            def _(rz=rz, rs=rs, where=where):
                for slot, (pa, pb) in enumerate(side_tiles(-rz, -rs, rows, cols)):
                    az = {0: pa, 1: rows, -1: -1}[rz]
                    bs = {0: pb, 1: cols, -1: -1}[rs]
                    grad = partner_grad(az, bs)
                    for c in range(3):
                        line = 3 + c * slots + slot
                        send_ref[where, line : line + 1, :] = grad[c : c + 1]


def finish_body(dims, recv_ref, grad_ref, members_ref, member_ref, born_ref, rgrad_ref,
                force_ref, born_out, rgrad_out):
    rows, cols, dom_count, sub_count = dims
    slots = max(rows, cols)

    def add(d, total):
        return total + recv_ref[d, 0:3, :]

    centre_grad = lax.fori_loop(
        0, dom_count * sub_count, add, jnp.zeros((3, LANES), jnp.float32))
    per_member = centre_grad / members_ref[0:3, :]
    born_out[...] = born_ref[...]
    rgrad_out[...] = rgrad_ref[...]
    block = pieces(jnp.concatenate([per_member, jnp.zeros((5, LANES), jnp.float32)], axis=0))
    block = jnp.concatenate(block + (jnp.zeros_like(block[0]),), axis=0).astype(jnp.bfloat16)
    back = product(block, member_ref[...])
    back = back[0:8] + back[8:16] + back[16:24]
    for a in range(rows):
        for b in range(cols):
            t = a * cols + b
            spread_out = back[:, t * LANES : (t + 1) * LANES]
            for c in range(3):
                force_ref[c, a, b : b + 1, :] = -(
                    grad_ref[c, a, b : b + 1, :] + spread_out[c : c + 1])
    for rz in (-1, 0, 1):
        for rs in (-1, 0, 1):
            if rz == 0 and rs == 0:
                continue
            where = device_at(rz, rs, dom_count, sub_count)

            @pl.when(in_range(rz, dom_count))
            def _(rz=rz, rs=rs, where=where):
                for slot, (a, b) in enumerate(side_tiles(rz, rs, rows, cols)):
                    for c in range(3):
                        line = 3 + c * slots + slot
                        force_ref[c, a, b : b + 1, :] = (
                            force_ref[c, a, b : b + 1, :] - recv_ref[where, line : line + 1, :])


def f32(*shape):
    return jax.ShapeDtypeStruct(shape, jnp.float32)


def bf16(*shape):
    return jax.ShapeDtypeStruct(shape, jnp.bfloat16)


def local(positions, charge, radius, segment, near_tiles):
    rows, cols, width = charge.shape
    dom_count, sub_count = lax.axis_size("dom"), lax.axis_size("sub")
    dims = (rows, cols, dom_count, sub_count)
    devices = dom_count * sub_count
    tiles = rows * cols
    assert width == LANES and tiles * CT == LANES and sub_count > 2 and devices % 2 == 0
    slots = max(rows, cols)
    places = (rows + 2) * (cols + 2)
    vec = (SUBLANES, LANES)
    together = 2 if devices <= 64 else 1
    kept_shape = (together, devices, LANES, LANES) if devices <= 64 else (1, 1) + vec
    second_shape = (together, devices + NEAR, LANES, LANES) if devices <= 64 else (1, 1) + vec
    vmem = pltpu.MemorySpace.VMEM

    def call(body, ins, outs, scratch=(), room=8 << 20, space=vmem):
        return pl.pallas_call(
            lambda *refs: body(dims, *refs),
            out_shape=outs,
            in_specs=[pl.BlockSpec(memory_space=pltpu.MemorySpace.SMEM if x is near_tiles else space)
                      for x in ins],
            out_specs=[pl.BlockSpec(memory_space=vmem) for _ in outs],
            scratch_shapes=list(scratch),
            compiler_params=pltpu.CompilerParams(vmem_limit_bytes=room),
            name=body.__name__,
        )(*[pltpu.with_memory_space_constraint(x, space) if space is not vmem else x for x in ins])

    def exchanged(blocks):
        return lax.all_to_all(blocks, AXES, 0, 0, tiled=True)

    send, members, member = call(
        pack_body, (positions, charge, radius, segment),
        [f32(devices, 8 + 4 * slots, LANES), f32(*vec), bf16(LANES, tiles * LANES)],
        [pltpu.VMEM(positions.shape, jnp.float32), pltpu.VMEM(charge.shape, jnp.float32),
         pltpu.VMEM(radius.shape, jnp.float32), pltpu.VMEM(segment.shape, jnp.int32),
         pltpu.SemaphoreType.DMA((4,))],
        space=pltpu.MemorySpace.HBM)
    table = exchanged(send)
    send, born, *tables = call(
        screen_body, (near_tiles, table, positions, charge, radius),
        [f32(devices, 2 * slots, LANES), f32(rows, cols, LANES),
         bf16(tiles, LANES, KROWS), bf16(tiles, WROWS, 2 * LANES),
         bf16(places, KROWS, LANES), bf16(places, WROWS, 2 * LANES),
         f32(places, *vec), f32(places, *vec),
         bf16(devices // 2, KROWS, 2 * LANES), bf16(devices // 2, WROWS, 4 * LANES),
         f32(devices, *vec), f32(devices, tiles, LANES), f32(devices, tiles, LANES)],
        room=(8 << 20) + devices * (1 << 16))
    halo = exchanged(send)
    radius_grad, grad, send = call(
        energy_body, (near_tiles, table, halo, charge, radius, born, *tables),
        [f32(rows, cols, LANES), f32(3, rows, cols, LANES), f32(devices, 4 + 3 * slots, LANES)],
        [pltpu.VMEM((tiles, 3, LANES, LANES), jnp.float32),
         pltpu.VMEM((places,) + vec, jnp.float32),
         pltpu.VMEM((together, devices + NEAR, LANES, LANES), jnp.float32),
         pltpu.VMEM((together, devices + NEAR, LANES, LANES), jnp.float32),
         pltpu.VMEM(kept_shape, jnp.float32),
         pltpu.VMEM(kept_shape, jnp.float32),
         pltpu.VMEM(second_shape, jnp.float32),
         pltpu.VMEM(second_shape, jnp.float32),
         pltpu.VMEM(kept_shape, jnp.float32),
         pltpu.VMEM(kept_shape, jnp.float32),
         pltpu.VMEM((devices // 2, WROWS, 2 * LANES), jnp.float32),
         pltpu.VMEM((places, WROWS, LANES), jnp.float32)],
        room=(13 << 20) + devices * (3 << 16 if together == 1 else 20 << 16))
    back = exchanged(send)
    shape = f32(rows, cols, LANES)
    forces, born_radii, radius_grad = call(
        finish_body, (back, grad, members, member, born, radius_grad),
        [f32(3, rows, cols, LANES), shape, shape])
    return born_radii, radius_grad, forces


def solution(mesh):
    flat = P(("groups", "dom"), "sub", None)
    stacked = P(None, ("groups", "dom"), "sub", None)
    return jax.shard_map(
        local,
        mesh=mesh,
        in_specs=(stacked, flat, flat, flat, flat),
        out_specs=(flat, flat, stacked),
        check_vma=False,
    )
```

```python
import jax
import jax.numpy as jnp
from jax import lax
from jax.experimental import pallas as pl
from jax.experimental.pallas import tpu as pltpu
from jax.sharding import PartitionSpec as P

CT = 16
LANES = 128
SUBLANES = 8
UNIT = 128.0
TOGETHER = 8
KROWS = 48
WROWS = 16
SPAN = 64.0
CHARGE_UNIT = 0.5 * UNIT ** -1.5
RADIUS_FACTOR = 1.5
LOG2E = 1.4426950408889634
LN2 = 0.6931471805599453
HIGHEST = lax.Precision.HIGHEST
AXES = ("dom", "sub")
STEPS = ((-1, -1), (-1, 0), (-1, 1), (0, -1), (0, 1), (1, -1), (1, 0), (1, 1))
SELF = len(STEPS)
NEAR = len(STEPS) + 1


def side_tiles(rz, rs, rows, cols):
    along = {0: range(rows), 1: [rows - 1], -1: [0]}[rz]
    around = {0: range(cols), 1: [cols - 1], -1: [0]}[rs]
    return [(a, b) for a in along for b in around]


def partner(a, b, k, rows, cols):
    dz, ds = STEPS[k] if k < SELF else (0, 0)
    az, bs = a + dz, b + ds
    rz = -1 if az < 0 else 1 if az >= rows else 0
    rs = -1 if bs < 0 else 1 if bs >= cols else 0
    tile = (az % rows, bs % cols)
    if rz == 0 and rs == 0:
        return (0, 0), None, tile
    return (rz, rs), side_tiles(-rz, -rs, rows, cols).index(tile), tile


def device_at(rz, rs, dom_count, sub_count):
    along = jnp.clip(lax.axis_index("dom") + rz, 0, dom_count - 1)
    around = lax.rem(lax.axis_index("sub") + rs + sub_count, sub_count)
    return along * sub_count + around


def in_range(rz, dom_count):
    at = lax.axis_index("dom") + rz
    return (at >= 0) & (at < dom_count)


def far_unroll(pairs):
    return 8 if pairs % 8 == 0 else 1


def short_loop(trips, step, carry):
    return lax.fori_loop(0, trips, step, carry, unroll=trips <= 16)


def pieces(value):
    first = value.astype(jnp.bfloat16).astype(jnp.float32)
    left = value - first
    second = left.astype(jnp.bfloat16).astype(jnp.float32)
    return first, second, left - second


def line_of(shape=(SUBLANES, LANES)):
    return lax.broadcasted_iota(jnp.int32, shape, 0)


def side_block(points, ones_line, norm_line, factor):
    norm = jnp.sum(points * points, axis=0, keepdims=True) * (1.0 / UNIT)
    line = line_of()
    block = jnp.where(line == norm_line, norm, jnp.where(line == ones_line, 1.0, factor * points))
    return pieces(block)


def weight_rows(first, second, third):
    rows = jnp.concatenate(
        [first, second[0:3], third[0:3], jnp.zeros((2, LANES), jnp.float32)], axis=0)
    return jnp.concatenate([rows, rows], axis=1).astype(jnp.bfloat16)


def other_tables(points):
    c1, c2, c3 = side_block(points, 4, 3, 1.0)
    table = jnp.concatenate([c1, c2, c1, c2, c3, c1], axis=0).astype(jnp.bfloat16)
    return table, weight_rows(c1, c2, c3)


def own_tables(points):
    x1, x2, x3 = side_block(points, 3, 4, -2.0 / UNIT)
    stack = jnp.concatenate(
        [x1, x1, x2, x2, x1, x3, jnp.zeros((LANES - KROWS, LANES), jnp.float32)], axis=0)
    w1, w2, w3 = side_block(points, 4, 3, 1.0)
    return stack.T[:, 0:KROWS].astype(jnp.bfloat16), weight_rows(w1, w2, w3)


def product(a, b):
    return jnp.dot(a, b, preferred_element_type=jnp.float32)


def product_turned(a, b):
    return lax.dot_general(a, b, (((1,), (1,)), ((), ())), preferred_element_type=jnp.float32)


def weighted(block):
    return block[4:5], block[0:3] + block[8:11] + block[11:14]


def member_table(seg_ref, a, b, cols):
    comp = lax.broadcasted_iota(jnp.int32, (LANES, LANES), 0)
    owner = seg_ref[a, b : b + 1, :] + (a * cols + b) * CT
    return (comp == owner).astype(jnp.float32).astype(jnp.bfloat16)


def turned(row):
    return jnp.broadcast_to(row, (LANES, LANES)).T


def lane_sums(block):
    return jnp.sum(block.T, axis=0, keepdims=True)


def pack_body(dims, pos_hbm, q_hbm, r_hbm, seg_hbm, send_ref, members_ref, member_ref,
              pos_ref, q_ref, r_ref, seg_ref, arrived):
    rows, cols, dom_count, sub_count = dims
    copies = [
        pltpu.make_async_copy(source, place, arrived.at[n])
        for n, (source, place) in enumerate(
            [(pos_hbm, pos_ref), (q_hbm, q_ref), (r_hbm, r_ref), (seg_hbm, seg_ref)])]
    for copy in copies:
        copy.start()
    for copy in copies:
        copy.wait()
    slots = max(rows, cols)
    one = jnp.ones((1, LANES), jnp.float32)
    values = []
    for a in range(rows):
        for b in range(cols):
            at, t = slice(b, b + 1), a * cols + b
            rho = r_ref[a, at, :]
            member_ref[:, t * LANES : (t + 1) * LANES] = member_table(seg_ref, a, b, cols)
            block = pieces(jnp.concatenate(
                [pos_ref[0, a, at, :], pos_ref[1, a, at, :], pos_ref[2, a, at, :],
                 q_ref[a, at, :], rho * rho * rho, rho, one, one], axis=0))
            values.append(jnp.concatenate(block + (jnp.zeros_like(block[0]),), axis=0))
    sums = product_turned(jnp.concatenate(values, axis=1).astype(jnp.bfloat16), member_ref[...])
    total = sums[0:8] + sums[8:16] + sums[16:24]
    members = total[6:7]
    comp_radius = RADIUS_FACTOR * total[5:6] / members
    table = jnp.concatenate(
        [total[0:3] / members, CHARGE_UNIT * total[3:4], total[4:5],
         comp_radius * (1.0 / UNIT), (-0.25 * LOG2E * UNIT) / comp_radius,
         comp_radius * comp_radius * (1.0 / UNIT)], axis=0)
    members_ref[...] = jnp.broadcast_to(members, (SUBLANES, LANES))

    def put(d, carry):
        send_ref[d, 0:8, :] = table
        return carry

    short_loop(dom_count * sub_count, put, 0)
    for rz in (-1, 0, 1):
        for rs in (-1, 0, 1):
            where = device_at(rz, rs, dom_count, sub_count)

            @pl.when(in_range(rz, dom_count))
            def _(rz=rz, rs=rs, where=where):
                for slot, (a, b) in enumerate(side_tiles(rz, rs, rows, cols)[:slots]):
                    at = slice(b, b + 1)
                    for c in range(3):
                        line = 8 + c * slots + slot
                        send_ref[where, line : line + 1, :] = pos_ref[c, a, at, :]
                    line = 8 + 3 * slots + slot
                    send_ref[where, line : line + 1, :] = r_ref[a, at, :]


def mask_rows(dims, near_ref, tables):
    rows, cols, dom_count, sub_count = dims
    shape = (rows * cols, LANES)
    row = lax.broadcasted_iota(jnp.int32, shape, 0)
    tile_of = lax.broadcasted_iota(jnp.int32, shape, 1) // CT
    struck = {}
    for a in range(rows):
        for b in range(cols):
            for k in range(NEAR):
                rel, _, (pa, pb) = partner(a, b, k, rows, cols)
                flag = near_ref[a, b, k] if k < SELF else 1
                at = jnp.where(row == a * cols + b, tile_of - (pa * cols + pb), 1)
                hit = jnp.where(at == 0, flag, 0)
                struck[rel] = struck[rel] | hit if rel in struck else hit
    for (rz, rs), hit in struck.items():
        where = device_at(rz, rs, dom_count, sub_count)
        for table in tables:
            table[where] = jnp.where(hit == 1, 0.0, table[where])


def near_source(dims, rz, rs):
    rows, cols, dom_count, sub_count = dims
    return device_at(rz, rs, dom_count, sub_count)


def window_source(dims, place, recv_ref, own, base, c):
    rows, cols, _, _ = dims
    az, bs = place // (cols + 2) - 1, place % (cols + 2) - 1
    rz = -1 if az < 0 else 1 if az >= rows else 0
    rs = -1 if bs < 0 else 1 if bs >= cols else 0
    tile = (az % rows, bs % cols)
    if rz == 0 and rs == 0:
        return own(c, *tile)
    line = base + c * max(rows, cols) + side_tiles(-rz, -rs, rows, cols).index(tile)
    return recv_ref[near_source(dims, rz, rs), line : line + 1, :]


def window_place(t, k, cols):
    dz, ds = STEPS[k] if k < SELF else (0, 0)
    return (t // cols + 1 + dz) * (cols + 2) + t % cols + 1 + ds


def flagged(near_ref, t, k, cols, row):
    if k == SELF:
        return row
    return jnp.where(near_ref[t // cols, t % cols, k] == 1, row, 0.0)


def own_pair():
    shape = (LANES, LANES)
    return lax.broadcasted_iota(jnp.int32, shape, 0) == lax.broadcasted_iota(jnp.int32, shape, 1)


def quarter_of(block, i, half):
    return block[i * LANES : (i + 1) * LANES, half * LANES : (half + 1) * LANES]


def over_far(pairs, begin, end, carry):
    unroll = far_unroll(pairs)

    def chunk(n, carry):
        begun = begin(n * unroll)
        for j in range(unroll):
            ahead = begin(n * unroll + j + 1) if j + 1 < unroll else None
            carry = end(n * unroll + j, begun, carry)
            begun = ahead
        return carry

    if pairs == unroll:
        return chunk(0, carry)
    return lax.fori_loop(0, pairs // unroll, chunk, carry)


def screen_body(dims, near_ref, recv_ref, pos_ref, q_ref, r_ref, send_ref, born_ref,
                own_k, own_w, win_k, win_w, win_c, win_r, far_k, far_w, far_c, far_vol, far_q):
    rows, cols, dom_count, sub_count = dims
    devices = dom_count * sub_count
    slots = max(rows, cols)
    line = line_of()

    middle = jnp.zeros((SUBLANES, LANES), jnp.float32)
    for c in range(3):
        mean = jnp.sum(pos_ref[c]) * (1.0 / (rows * cols * LANES))
        middle = jnp.where(line == c, mean, middle)

    def own(c, a, b):
        if c < 3:
            return pos_ref[c, a, b : b + 1, :]
        return r_ref[a, b : b + 1, :]

    def put(p, carry):
        for half in range(2):
            d = 2 * p + half
            far_q[d] = jnp.broadcast_to(recv_ref[d, 3:4, :], (rows * cols, LANES))
            far_vol[d] = jnp.broadcast_to(recv_ref[d, 4:5, :], (rows * cols, LANES))
            points = jnp.where(line < 3, recv_ref[d, 0:8, :] - middle, 0.0)
            far_c[d] = points
            table, weights = other_tables(points)
            far_k[p, :, half * LANES : (half + 1) * LANES] = table
            far_w[p, :, 2 * half * LANES : 2 * (half + 1) * LANES] = weights
        return carry

    short_loop(devices // 2, put, 0)
    mask_rows(dims, near_ref, (far_vol, far_q))
    none = jnp.zeros((SUBLANES - 3, LANES), jnp.float32)
    for place in range((rows + 2) * (cols + 2)):
        x, y, z, rho = [window_source(dims, place, recv_ref, own, 8, c) for c in range(4)]
        points = jnp.concatenate([x, y, z, none], axis=0) - middle
        win_c[place] = points
        win_k[place], win_w[place] = other_tables(points)
        win_r[place, 0:1, :] = rho * rho * (1.0 / UNIT)
        win_r[place, 1:2, :] = rho * rho * rho
        az, bs = place // (cols + 2) - 1, place % (cols + 2) - 1
        if 0 <= az < rows and 0 <= bs < cols:
            own_k[az * cols + bs], own_w[az * cols + bs] = own_tables(points)

    def tiles(n, carry):
        pair = [n * TOGETHER + i for i in range(TOGETHER)]
        x = [own_k[t] for t in pair]
        sums = []
        for i, t in enumerate(pair):
            total = jnp.zeros((LANES, LANES), jnp.float32)
            for k in range(NEAR):
                place = window_place(t, k, cols)
                volume = flagged(near_ref, t, k, cols, win_r[place, 1:2, :])
                if k == SELF:
                    volume = jnp.where(own_pair(), 0.0, volume)
                near = product(x[i], win_k[place]) + win_r[place, 0:1, :]
                total = total + volume / (near * near)
            sums.append(total)
        x_all = jnp.concatenate(x, axis=0)

        def far_square(p):
            return product(x_all, far_k[p])

        def far(p, s_all, sums):
            out = list(sums)
            for half in range(2):
                d = 2 * p + half
                for i, t in enumerate(pair):
                    s = quarter_of(s_all, i, half)
                    near = s + recv_ref[d, 7:8, :]
                    volume = far_vol[d, pl.ds(t, 1), :]
                    out[i] = out[i] + (volume * s) / ((s + SPAN / UNIT) * (near * near))
            return tuple(out)

        sums = over_far(devices // 2, far_square, far, tuple(sums))
        for i, t in enumerate(pair):
            screening = lane_sums(sums[i]) * (1.0 / (UNIT * UNIT))
            a, b = t // cols, t % cols
            rho = r_ref[a, pl.ds(b, 1), :]
            born_ref[a, pl.ds(b, 1), :] = rho * (1.0 + rho * screening)
        return carry

    lax.fori_loop(0, rows * cols // TOGETHER, tiles, 0)
    for rz in (-1, 0, 1):
        for rs in (-1, 0, 1):
            where = device_at(rz, rs, dom_count, sub_count)

            @pl.when(in_range(rz, dom_count))
            def _(rz=rz, rs=rs, where=where):
                for slot, (a, b) in enumerate(side_tiles(rz, rs, rows, cols)[:slots]):
                    send_ref[where, slot : slot + 1, :] = born_ref[a, b : b + 1, :]
                    line = slots + slot
                    send_ref[where, line : line + 1, :] = q_ref[a, b : b + 1, :]


def energy_body(dims, near_ref, recv_ref, halo_ref, q_ref, r_ref, born_ref,
                own_k, own_w, win_k, win_w, win_c, win_r, far_k, far_w, far_c, far_vol, far_q,
                rgrad_ref, grad_ref, send_ref,
                turned_ref, win_e, *refs):
    rows, cols, dom_count, sub_count = dims
    stores, (far_acc, win_acc) = (refs[0:4], refs[4:8]), refs[8:]
    together = refs[0].shape[0]
    kept = refs[2].shape[1] == dom_count * sub_count
    devices = dom_count * sub_count
    slots = max(rows, cols)
    tiles = rows * cols
    places = (rows + 2) * (cols + 2)

    def own(c, a, b):
        at = slice(b, b + 1)
        return born_ref[a, at, :] if c == 0 else q_ref[a, at, :]

    zero = jnp.zeros((LANES, LANES), jnp.float32)
    no_force = jnp.zeros((WROWS, LANES), jnp.float32)

    def put(p, carry):
        far_acc[p] = jnp.zeros((WROWS, 2 * LANES), jnp.float32)
        return carry

    short_loop(devices // 2, put, 0)
    for place in range(places):
        born, charge = [window_source(dims, place, halo_ref, own, 0, c) for c in range(2)]
        win_e[place, 0:1, :] = born * (1.0 / UNIT)
        win_e[place, 1:2, :] = (-0.25 * LOG2E * UNIT) / born
        win_e[place, 2:3, :] = CHARGE_UNIT * charge
        win_acc[place] = no_force
    for a in range(rows):
        for b in range(cols):
            at = slice(b, b + 1)
            for c, row in enumerate([born_ref[a, at, :], q_ref[a, at, :], r_ref[a, at, :]]):
                turned_ref[a * cols + b, c] = turned(row)

    def energy_steps(n, store):
        pair_f, pair_s, pair_i, pair_w = store
        members = [n * together + i for i in range(together)]
        own_rows = [[turned_ref[t, c] for c in range(3)] for t in members]
        own_inv = [1.0 / rows_of[0] for rows_of in own_rows]

        def pair(i, s, other_born, other_inv, charge):
            own_born, own_q, _ = own_rows[i]
            e = jnp.exp2(s * (own_inv[i] * other_inv))
            r = lax.rsqrt(s + (own_born * other_born) * e)
            return charge * (own_q * r), (r * r) * (1.0 - 0.25 * e)

        def near_energy(k, born_near):
            out = list(born_near)
            for i, t in enumerate(members):
                place = window_place(t, k, cols)
                other_born, other_inv, charge = [win_e[place, c : c + 1, :] for c in range(3)]
                charge = flagged(near_ref, t, k, cols, charge)
                if k == SELF:
                    charge = jnp.where(own_pair(), 0.0, charge)
                s = product(own_k[t], win_k[place])
                qr, slope = pair(i, s, other_born, other_inv, charge)
                f = qr * slope
                pair_f[i, devices + k] = f
                pair_s[i, devices + k] = s
                out[i] = out[i] + (qr - s * f)
            return tuple(out)

        def far_square(p):
            return product(jnp.concatenate([own_k[t] for t in members], axis=0), far_k[p])

        def far_energy(p, s_all, born_far):
            out = list(born_far)
            for half in range(2):
                d = 2 * p + half
                other_born, other_inv = recv_ref[d, 5:6, :], recv_ref[d, 6:7, :]
                for i, t in enumerate(members):
                    charge = far_q[d, pl.ds(t, 1), :]
                    s = quarter_of(s_all, i, half)
                    qr, slope = pair(i, s, other_born, other_inv, charge)
                    inv = 1.0 / (s + SPAN / UNIT)
                    weight = s * inv
                    falling = weight * slope
                    square = inv * inv
                    pair_f[i, d] = qr * (falling - square)
                    pair_s[i, d] = s
                    if kept:
                        pair_i[i, d] = square
                        pair_w[i, d] = weight
                    out[i] = out[i] + qr * (weight - s * falling)
            return tuple(out)

        def finish(born_near, born_far):
            scale = []
            for i, t in enumerate(members):
                _, own_q, own_rho = own_rows[i]
                part = own_inv[i] * (UNIT * (0.5 * born_far[i] + born_near[i]))
                own_part = own_q * own_inv[i]
                rg = jnp.sum(part, axis=1, keepdims=True) + 0.5 * (own_part * own_part)
                scale.append(rg * (own_rho * own_rho) * (1.0 / UNIT ** 3))
                rgrad_ref[t // cols, pl.ds(t % cols, 1), :] = rg.T[0:1]
            return scale

        return near_energy, far_square, far_energy, finish

    def halves(f):
        high = f.astype(jnp.bfloat16)
        return high, (f - high.astype(jnp.float32)).astype(jnp.bfloat16)

    def chain_steps(n, store, scale):
        pair_f, pair_s, pair_i, pair_w = store
        members = [n * together + i for i in range(together)]

        def near_chain(k, own_near):
            out = list(own_near)
            for i, t in enumerate(members):
                place = window_place(t, k, cols)
                volume = flagged(near_ref, t, k, cols, 4.0 * win_r[place, 1:2, :])
                inv = 1.0 / (pair_s[i, devices + k] + win_r[place, 0:1, :])
                f = pair_f[i, devices + k] - (scale[i] * volume) * (inv * inv * inv)
                if k == SELF:
                    f = jnp.where(own_pair(), 0.0, f)
                high, low = halves(f)
                out[i] = out[i] + product_turned(
                    win_w[place], jnp.concatenate([high, low], axis=1))
                win_acc[place] = win_acc[place] + product(
                    own_w[t], jnp.concatenate([high, low], axis=0))
            return tuple(out)

        x_sums = jnp.concatenate([own_w[t] for t in members], axis=1)

        def far_factors(p):
            parts = [[], []]
            for half in range(2):
                d = 2 * p + half
                for i, t in enumerate(members):
                    s = pair_s[i, d]
                    volume = far_vol[d, pl.ds(t, 1), :]
                    near = 1.0 / (s + recv_ref[d, 7:8, :])
                    if kept:
                        square, weight = pair_i[i, d], pair_w[i, d]
                    else:
                        inv = 1.0 / (s + SPAN / UNIT)
                        square, weight = inv * inv, s * inv
                    slope = (square - 4.0 * (weight * near)) * (near * near)
                    parts[half].append(halves(pair_f[i, d] + (scale[i] * volume) * slope))
            columns = [jnp.concatenate([x for pieces_of in half for x in pieces_of], axis=0)
                       for half in parts]
            lines = [jnp.concatenate(parts[0][i] + parts[1][i], axis=1) for i in range(together)]
            return jnp.concatenate(columns, axis=1), jnp.concatenate(lines, axis=0)

        def far_sums(p, factors, own_sum):
            far_acc[p] = far_acc[p] + product(x_sums, factors[0])
            return own_sum + product_turned(far_w[p], factors[1])

        def finish(own_sum):
            for i, t in enumerate(members):
                total, moment = weighted(own_sum[:, i * LANES : (i + 1) * LANES])
                grad = win_c[window_place(t, SELF, cols), 0:3, :] * total - moment
                for c in range(3):
                    grad_ref[c, t // cols, pl.ds(t % cols, 1), :] = grad[c : c + 1]

        return near_chain, far_factors, far_sums, finish

    pairs = devices // 2

    def energy_of(n, store):
        near_energy, far_square, far_energy, finish = energy_steps(n, store)
        born_near = tuple([zero] * together)
        for k in range(NEAR):
            born_near = near_energy(k, born_near)
        return finish(born_near, over_far(pairs, far_square, far_energy, tuple([zero] * together)))

    def chain_of(n, store, scale):
        near_chain, far_factors, far_sums, finish = chain_steps(n, store, scale)
        own_near = tuple([no_force] * together)
        for k in range(NEAR):
            own_near = near_chain(k, own_near)
        finish(over_far(pairs, far_factors, far_sums, jnp.concatenate(own_near, axis=1)))

    def both_of(n, store, last_store, scale):
        near_energy, far_square, far_energy, finish = energy_steps(n, store)
        near_chain, far_factors, far_sums, finish_chain = chain_steps(n - 1, last_store, scale)
        born_near, own_near = tuple([zero] * together), tuple([no_force] * together)
        for k in range(NEAR):
            born_near = near_energy(k, born_near)
            own_near = near_chain(k, own_near)

        def begin(p):
            return far_square(p), far_factors(p)

        def end(p, begun, carry):
            return far_energy(p, begun[0], carry[0]), far_sums(p, begun[1], carry[1])

        born_far, own_sum = over_far(
            pairs, begin, end, (tuple([zero] * together), jnp.concatenate(own_near, axis=1)))
        finish_chain(own_sum)
        return finish(born_near, born_far)

    groups = tiles // together
    if kept:
        scale = energy_of(0, stores[0])
        for n in range(1, groups):
            scale = both_of(n, stores[n % 2], stores[(n - 1) % 2], scale)
        chain_of(groups - 1, stores[(groups - 1) % 2], scale)
    else:

        def group(n, carry):
            chain_of(n, stores[0], energy_of(n, stores[0]))
            return carry

        lax.fori_loop(0, groups, group, 0)

    def send_far(p, carry):
        for half in range(2):
            d = 2 * p + half
            total, moment = weighted(far_acc[p, :, half * LANES : (half + 1) * LANES])
            send_ref[d, 0:3, :] = far_c[d, 0:3, :] * total - moment
        return carry

    short_loop(devices // 2, send_far, 0)

    def partner_grad(az, bs):
        place = (az + 1) * (cols + 2) + bs + 1
        total, moment = weighted(win_acc[place])
        return win_c[place, 0:3, :] * total - moment

    for a in range(rows):
        for b in range(cols):
            grad = partner_grad(a, b)
            for c in range(3):
                grad_ref[c, a, b : b + 1, :] = grad_ref[c, a, b : b + 1, :] + grad[c : c + 1]
    for rz in (-1, 0, 1):
        for rs in (-1, 0, 1):
            if rz == 0 and rs == 0:
                continue
            where = device_at(rz, rs, dom_count, sub_count)

            @pl.when(in_range(rz, dom_count))
            def _(rz=rz, rs=rs, where=where):
                for slot, (pa, pb) in enumerate(side_tiles(-rz, -rs, rows, cols)):
                    az = {0: pa, 1: rows, -1: -1}[rz]
                    bs = {0: pb, 1: cols, -1: -1}[rs]
                    grad = partner_grad(az, bs)
                    for c in range(3):
                        line = 3 + c * slots + slot
                        send_ref[where, line : line + 1, :] = grad[c : c + 1]


def finish_body(dims, recv_ref, grad_ref, members_ref, member_ref, born_ref, rgrad_ref,
                force_ref, born_out, rgrad_out):
    rows, cols, dom_count, sub_count = dims
    slots = max(rows, cols)

    def add(d, total):
        return total + recv_ref[d, 0:3, :]

    centre_grad = short_loop(
        dom_count * sub_count, add, jnp.zeros((3, LANES), jnp.float32))
    per_member = centre_grad / members_ref[0:3, :]
    born_out[...] = born_ref[...]
    rgrad_out[...] = rgrad_ref[...]
    block = pieces(jnp.concatenate([per_member, jnp.zeros((5, LANES), jnp.float32)], axis=0))
    block = jnp.concatenate(block + (jnp.zeros_like(block[0]),), axis=0).astype(jnp.bfloat16)
    back = product(block, member_ref[...])
    back = back[0:8] + back[8:16] + back[16:24]
    for a in range(rows):
        for b in range(cols):
            t = a * cols + b
            spread_out = back[:, t * LANES : (t + 1) * LANES]
            for c in range(3):
                force_ref[c, a, b : b + 1, :] = -(
                    grad_ref[c, a, b : b + 1, :] + spread_out[c : c + 1])
    for rz in (-1, 0, 1):
        for rs in (-1, 0, 1):
            if rz == 0 and rs == 0:
                continue
            where = device_at(rz, rs, dom_count, sub_count)

            @pl.when(in_range(rz, dom_count))
            def _(rz=rz, rs=rs, where=where):
                for slot, (a, b) in enumerate(side_tiles(rz, rs, rows, cols)):
                    for c in range(3):
                        line = 3 + c * slots + slot
                        force_ref[c, a, b : b + 1, :] = (
                            force_ref[c, a, b : b + 1, :] - recv_ref[where, line : line + 1, :])


def f32(*shape):
    return jax.ShapeDtypeStruct(shape, jnp.float32)


def bf16(*shape):
    return jax.ShapeDtypeStruct(shape, jnp.bfloat16)


def local(positions, charge, radius, segment, near_tiles):
    rows, cols, width = charge.shape
    dom_count, sub_count = lax.axis_size("dom"), lax.axis_size("sub")
    dims = (rows, cols, dom_count, sub_count)
    devices = dom_count * sub_count
    tiles = rows * cols
    assert width == LANES and tiles * CT == LANES and sub_count > 2 and devices % 2 == 0
    slots = max(rows, cols)
    places = (rows + 2) * (cols + 2)
    vec = (SUBLANES, LANES)
    together = 2 if devices <= 64 else 1
    kept_shape = (together, devices, LANES, LANES) if devices <= 64 else (1, 1) + vec
    second_shape = (together, devices + NEAR, LANES, LANES) if devices <= 64 else (1, 1) + vec
    vmem = pltpu.MemorySpace.VMEM

    def call(body, ins, outs, scratch=(), room=8 << 20, space=vmem):
        return pl.pallas_call(
            lambda *refs: body(dims, *refs),
            out_shape=outs,
            in_specs=[pl.BlockSpec(memory_space=pltpu.MemorySpace.SMEM if x is near_tiles else space)
                      for x in ins],
            out_specs=[pl.BlockSpec(memory_space=vmem) for _ in outs],
            scratch_shapes=list(scratch),
            compiler_params=pltpu.CompilerParams(vmem_limit_bytes=room),
            name=body.__name__,
        )(*[pltpu.with_memory_space_constraint(x, space) if space is not vmem else x for x in ins])

    def exchanged(blocks):
        return lax.all_to_all(blocks, AXES, 0, 0, tiled=True)

    send, members, member = call(
        pack_body, (positions, charge, radius, segment),
        [f32(devices, 8 + 4 * slots, LANES), f32(*vec), bf16(LANES, tiles * LANES)],
        [pltpu.VMEM(positions.shape, jnp.float32), pltpu.VMEM(charge.shape, jnp.float32),
         pltpu.VMEM(radius.shape, jnp.float32), pltpu.VMEM(segment.shape, jnp.int32),
         pltpu.SemaphoreType.DMA((4,))],
        space=pltpu.MemorySpace.HBM)
    table = exchanged(send)
    send, born, *tables = call(
        screen_body, (near_tiles, table, positions, charge, radius),
        [f32(devices, 2 * slots, LANES), f32(rows, cols, LANES),
         bf16(tiles, LANES, KROWS), bf16(tiles, WROWS, 2 * LANES),
         bf16(places, KROWS, LANES), bf16(places, WROWS, 2 * LANES),
         f32(places, *vec), f32(places, *vec),
         bf16(devices // 2, KROWS, 2 * LANES), bf16(devices // 2, WROWS, 4 * LANES),
         f32(devices, *vec), f32(devices, tiles, LANES), f32(devices, tiles, LANES)],
        room=(8 << 20) + devices * (1 << 16))
    halo = exchanged(send)
    radius_grad, grad, send = call(
        energy_body, (near_tiles, table, halo, charge, radius, born, *tables),
        [f32(rows, cols, LANES), f32(3, rows, cols, LANES), f32(devices, 4 + 3 * slots, LANES)],
        [pltpu.VMEM((tiles, 3, LANES, LANES), jnp.float32),
         pltpu.VMEM((places,) + vec, jnp.float32),
         pltpu.VMEM((together, devices + NEAR, LANES, LANES), jnp.float32),
         pltpu.VMEM((together, devices + NEAR, LANES, LANES), jnp.float32),
         pltpu.VMEM(kept_shape, jnp.float32),
         pltpu.VMEM(kept_shape, jnp.float32),
         pltpu.VMEM(second_shape, jnp.float32),
         pltpu.VMEM(second_shape, jnp.float32),
         pltpu.VMEM(kept_shape, jnp.float32),
         pltpu.VMEM(kept_shape, jnp.float32),
         pltpu.VMEM((devices // 2, WROWS, 2 * LANES), jnp.float32),
         pltpu.VMEM((places, WROWS, LANES), jnp.float32)],
        room=(13 << 20) + devices * (3 << 16 if together == 1 else 20 << 16))
    back = exchanged(send)
    shape = f32(rows, cols, LANES)
    forces, born_radii, radius_grad = call(
        finish_body, (back, grad, members, member, born, radius_grad),
        [f32(3, rows, cols, LANES), shape, shape])
    return born_radii, radius_grad, forces


def solution(mesh):
    flat = P(("groups", "dom"), "sub", None)
    stacked = P(None, ("groups", "dom"), "sub", None)
    return jax.shard_map(
        local,
        mesh=mesh,
        in_specs=(stacked, flat, flat, flat, flat),
        out_specs=(flat, flat, stacked),
        check_vma=False,
    )
```
